512 devices in a mesh: py: 32 (over y, x), pz: 16 (over z, core).
Axes of the slice: x: 4, y: 8, z: 8, core: 2. Of those that a mesh axis runs over, the one named last changes fastest.
Arguments:
- velocity: float32 [3, 32, 1024, 1024], P(None, 'py', 'pz'), may hold values from -14 to 14
Outputs:
- nu_t: float32 [32, 1024, 1024], P('py', 'pz')
- filtered_velocity: bfloat16 [3, 32, 1024, 1024], P(None, 'py', None, 'pz')
The draws below stay inside these ranges and needn't reach their ends.
All inputs are finite; a program needn't handle non-finite values.
Results may differ from the reference program's by a relative error of at most 0.012.
The reference program's roundings to bfloat16 on the way count: a program that leaves them out, or rounds other values in their place, can miss the bound.
Values may be sent and summed in bfloat16 or wider, within the bound.
No kernel may reach another device: no remote copies, remote signals or barrier semaphores. Data moves between devices by JAX's collectives and lax.ppermute only.
A program may use at most 64 MiB of HBM per device.

```python
import math
import jax
import jax.numpy as jnp
import numpy as np
from jax import lax

NX = 1024
NZ = 1024
NY = 32


def draw_velocity(key, part):
    base = jax.random.fold_in(key, 17)
    noise_key, span_key, stream_key = jax.random.split(base, 3)
    heights = (jnp.arange(NY, dtype=jnp.float32) + 0.5) * (2.0 / NY) - 1.0
    profile = 1.5 * (1.0 - heights * heights)
    offset = jnp.stack([profile, jnp.zeros_like(profile), jnp.zeros_like(profile)])[:, :, None, None]
    span_frac = jnp.arange(NZ, dtype=jnp.float32) / NZ
    span_scale = jnp.exp(jnp.log(3.0) * span_frac + jax.random.uniform(span_key, (NZ,), jnp.float32, 0.0, jnp.log(1.8)))
    stream_scale = jnp.exp(jax.random.uniform(stream_key, (NX,), jnp.float32, 0.0, jnp.log(1.8)))
    amplitude = 0.25 * span_scale[:, None] * stream_scale[None, :]
    values = jnp.clip(jax.random.normal(noise_key, (3, NY, NZ, NX), jnp.float32), -5.0, 5.0) * amplitude
    return values + offset


def setup_inputs(seed: int = 0) -> dict:
    splits = jax.random.split(jax.random.key(seed), 2)
    return {
        "velocity": draw_velocity(jax.random.fold_in(splits[1], 71), 0),
    }


index_pairs = ((0, 0), (1, 1), (2, 2), (0, 1), (0, 2), (1, 2))
pair_weights = (1.0, 1.0, 1.0, 2.0, 2.0, 2.0)
epsilon = 1e-06

def filter_table(length):
    offsets = np.arange(length, dtype=np.int64)
    wavenumbers = np.arange(1, length // 4, dtype=np.int64)
    phase = offsets[:, None] * wavenumbers[None, :] % length
    kernel = (1.0 + 2.0 * np.cos(phase * (2.0 * math.pi / length)).sum(axis=1)) / length
    kernel = kernel.astype(np.float32)
    lagged = (offsets[:, None] - offsets[None, :]) % length
    return jnp.asarray(kernel[lagged], dtype=jnp.float32).astype(jnp.bfloat16)

def smooth_fields(fields, table_x, table_z):
    fields = lax.optimization_barrier(fields)
    along_x = jnp.einsum('fzx,xv->fzv', fields.astype(jnp.float32), table_x.astype(jnp.float32), precision=lax.Precision.HIGHEST).astype(jnp.bfloat16)
    along_x = lax.optimization_barrier(along_x)
    return jnp.einsum('wz,fzx->fwx', table_z.astype(jnp.float32), along_x.astype(jnp.float32), precision=lax.Precision.HIGHEST).astype(jnp.bfloat16)

def row_slopes(rows):
    rows = rows.astype(jnp.float32)
    center = rows[:, 1]
    slope_x = (jnp.roll(center, -1, 2) - jnp.roll(center, 1, 2)) * 0.5
    slope_z = (jnp.roll(center, -1, 1) - jnp.roll(center, 1, 1)) * 0.5
    slope_y = (rows[:, 2] - rows[:, 0]) * 0.5
    return (slope_x, slope_y, slope_z)

def strain(gradients):
    strain_parts = [0.5 * (gradients[b][a] + gradients[a][b]) for a, b in index_pairs]
    squares_sum = pair_weights[0] * strain_parts[0] * strain_parts[0]
    for weight, part_value in zip(pair_weights[1:], strain_parts[1:]):
        squares_sum = squares_sum + weight * part_value * part_value
    return (strain_parts, jnp.sqrt(2.0 * squares_sum))

def reference(velocity):
    table_x = filter_table(NX)
    table_z = filter_table(NZ)
    wall_rows = jnp.zeros((3, 1, NZ, NX), velocity.dtype)
    velocity_padded = jnp.concatenate([wall_rows, velocity, wall_rows], axis=1)

    def first_pass(row):
        center = lax.dynamic_slice_in_dim(velocity, row, 1, 1)[:, 0]
        return smooth_fields(center.astype(jnp.bfloat16), table_x, table_z)
    filtered_rows = lax.map(first_pass, jnp.arange(NY, dtype=jnp.int32))
    filtered_velocity = jnp.transpose(filtered_rows, (1, 0, 2, 3))
    wall_filtered = jnp.zeros((3, 1, NZ, NX), filtered_velocity.dtype)
    filtered_padded = jnp.concatenate([wall_filtered, filtered_velocity, wall_filtered], axis=1)

    def second_pass(row):
        rows_velocity = lax.dynamic_slice_in_dim(velocity_padded, row, 3, 1)
        rows_filtered = lax.dynamic_slice_in_dim(filtered_padded, row, 3, 1).astype(jnp.float32)
        strain_parts, magnitude = strain(row_slopes(rows_velocity))
        center = rows_velocity[:, 1]
        pieces = [(center[a] * center[b]).astype(jnp.bfloat16) for a, b in index_pairs]
        pieces = pieces + [(magnitude * part_value).astype(jnp.bfloat16) for part_value in strain_parts]
        smoothed = smooth_fields(jnp.stack(pieces), table_x, table_z).astype(jnp.float32)
        hat_parts, magnitude_hat = strain(row_slopes(rows_filtered))
        smooth_velocity = rows_filtered[:, 1]
        numerator = jnp.zeros_like(magnitude)
        denominator = jnp.zeros_like(magnitude)
        for pair_index, (a, b) in enumerate(index_pairs):
            leonard = smoothed[pair_index] - smooth_velocity[a] * smooth_velocity[b]
            model_term = smoothed[6 + pair_index] - 4.0 * magnitude_hat * hat_parts[pair_index]
            numerator = numerator + pair_weights[pair_index] * leonard * model_term
            denominator = denominator + pair_weights[pair_index] * model_term * model_term
        return (jnp.sum(numerator), jnp.sum(denominator), magnitude)
    numerator, denominator, magnitude = lax.map(second_pass, jnp.arange(NY, dtype=jnp.int32))
    plane_cells = NX * NZ
    coefficient = numerator / plane_cells / (2.0 * (denominator / plane_cells + epsilon))
    nu_t = coefficient[:, None, None] * magnitude
    return (nu_t, filtered_velocity)
```

```python
import math

import jax
import jax.numpy as jnp
import numpy as np
from jax import lax
from jax.experimental import pallas as pl
from jax.experimental.pallas import tpu as pltpu
from jax.sharding import PartitionSpec as P

index_pairs = ((0, 0), (1, 1), (2, 2), (0, 1), (0, 2), (1, 2))
pair_weights = (1.0, 1.0, 1.0, 2.0, 2.0, 2.0)
epsilon = 1e-06
LANES = 128


def filter_table(length):
    offsets = np.arange(length, dtype=np.int64)
    wavenumbers = np.arange(1, length // 4, dtype=np.int64)
    phase = offsets[:, None] * wavenumbers[None, :] % length
    kernel = (1.0 + 2.0 * np.cos(phase * (2.0 * math.pi / length)).sum(axis=1)) / length
    kernel = kernel.astype(np.float32)
    lagged = (offsets[:, None] - offsets[None, :]) % length
    return kernel[lagged].astype(jnp.bfloat16)


def call(kernel, out_shape, flops, moved, scratch=(), name=None, smem=()):
    def run(*args):
        specs = [
            pl.BlockSpec(memory_space=pltpu.SMEM if i in smem else pltpu.VMEM)
            for i in range(len(args))
        ]
        return pl.pallas_call(
            kernel,
            out_shape=out_shape,
            in_specs=specs,
            out_specs=jax.tree.map(lambda _: pl.BlockSpec(memory_space=pltpu.VMEM), out_shape),
            scratch_shapes=list(scratch),
            cost_estimate=pl.CostEstimate(flops=flops, bytes_accessed=moved, transcendentals=0),
            compiler_params=pltpu.CompilerParams(vmem_limit_bytes=12 * 1024 * 1024),
            name=name,
        )(*args)

    return run


def nt(a, b):
    return lax.dot_general(a, b, (((1,), (1,)), ((), ())), preferred_element_type=jnp.float32)


def send_blocks(table_ref, fields_ref, out_ref, count, depth):
    receivers, _, _ = out_ref.shape
    width = table_ref.shape[0] // receivers
    per = LANES // depth
    group = 2 * per
    full = count // per
    for first in range(0, full * per, group):
        here = min(group, full * per - first)
        got = nt(table_ref[...], fields_ref[first * depth : (first + here) * depth, :])
        got = got.astype(jnp.bfloat16)
        for j in range(here // per):
            slot = first // per + j
            block = got[:, j * LANES : (j + 1) * LANES].reshape(receivers, width, LANES)
            out_ref[:, slot * width : (slot + 1) * width, :] = block
    if count % per:
        last = fields_ref[full * per * depth : count * depth, :]
        got = nt(table_ref[...], jnp.concatenate([last, last], axis=0))
        got = got.reshape(receivers, width, LANES)
        half = width // 2
        lane = lax.broadcasted_iota(jnp.int32, (receivers, half, LANES), 2)
        block = jnp.where(lane < depth, got[:, :half, :], got[:, half:, :])
        out_ref[:, full * width :, :] = block.astype(jnp.bfloat16)


def swapped(x):
    return pltpu.roll(x.astype(jnp.float32), LANES // 2, 1).astype(x.dtype)


def gather_pair(recv_ref, slot, lines_ref, at, width):
    senders = recv_ref.shape[0]
    lane = lax.broadcasted_iota(jnp.int32, (width, LANES), 1)
    low = lane < LANES // 2
    rows = slice(slot * width, (slot + 1) * width)
    for t in range(senders // 2):
        even = recv_ref[2 * t, rows, :].astype(jnp.float32)
        odd = recv_ref[2 * t + 1, rows, :].astype(jnp.float32)
        one = jnp.where(low, even, pltpu.roll(odd, LANES // 2, 1))
        two = jnp.where(low, pltpu.roll(even, LANES // 2, 1), odd)
        cols = slice(t * LANES, (t + 1) * LANES)
        lines_ref[at * width : (at + 1) * width, cols] = one.astype(jnp.bfloat16)
        if (at + 2) * width <= lines_ref.shape[0]:
            lines_ref[(at + 1) * width : (at + 2) * width, cols] = two.astype(jnp.bfloat16)


def gather_second(recv_ref, slot, lines_ref, at, width):
    senders = recv_ref.shape[0]
    low = lax.broadcasted_iota(jnp.int32, (width, LANES), 1) < LANES // 2
    rows = slice(slot * width, (slot + 1) * width)
    for t in range(senders // 2):
        even = recv_ref[2 * t, rows, :].astype(jnp.float32)
        odd = recv_ref[2 * t + 1, rows, :].astype(jnp.float32)
        two = jnp.where(low, pltpu.roll(even, LANES // 2, 1), odd)
        cols = slice(t * LANES, (t + 1) * LANES)
        lines_ref[at * width : (at + 1) * width, cols] = two.astype(jnp.bfloat16)


def gather_single(recv_ref, slot, lines_ref, at, width):
    senders = recv_ref.shape[0]
    half = width // 2
    low = lax.broadcasted_iota(jnp.int32, (half, LANES), 1) < LANES // 2
    rows = slice(slot * width, slot * width + half)
    for t in range(senders // 2):
        even = recv_ref[2 * t, rows, :].astype(jnp.float32)
        odd = recv_ref[2 * t + 1, rows, :].astype(jnp.float32)
        top = jnp.where(low, even, pltpu.roll(odd, LANES // 2, 1))
        bottom = jnp.where(low, pltpu.roll(even, LANES // 2, 1), odd)
        cols = slice(t * LANES, (t + 1) * LANES)
        lines_ref[at * width : at * width + half, cols] = top.astype(jnp.bfloat16)
        lines_ref[at * width + half : (at + 1) * width, cols] = bottom.astype(jnp.bfloat16)


def products_kernel(table_ref, velocity_ref, out_ref, fields_ref):
    depth = velocity_ref.shape[1]
    parts = [velocity_ref[a] for a in range(3)]
    for a in range(3):
        fields_ref[a * depth : (a + 1) * depth, :] = parts[a].astype(jnp.bfloat16)
    for p, (a, b) in enumerate(index_pairs):
        at = (3 + p) * depth
        fields_ref[at : at + depth, :] = (parts[a] * parts[b]).astype(jnp.bfloat16)
    send_blocks(table_ref, fields_ref, out_ref, 9, depth)


def strain(gradients):
    strain_parts = [0.5 * (gradients[b][a] + gradients[a][b]) for a, b in index_pairs]
    squares_sum = pair_weights[0] * strain_parts[0] * strain_parts[0]
    for weight, part_value in zip(pair_weights[1:], strain_parts[1:]):
        squares_sum = squares_sum + weight * part_value * part_value
    return (strain_parts, jnp.sqrt(2.0 * squares_sum))


def slopes(center, below, above, first, last):
    rows, length = center.shape
    row = lax.broadcasted_iota(jnp.int32, center.shape, 0)
    along = (pltpu.roll(center, length - 1, 1) - pltpu.roll(center, 1, 1)) * 0.5
    following = jnp.where(row == rows - 1, last, pltpu.roll(center, rows - 1, 0))
    previous = jnp.where(row == 0, first, pltpu.roll(center, 1, 0))
    return (along, (above - below) * 0.5, (following - previous) * 0.5)


def strain_kernel(
    table_ref, velocity_ref, below_ref, above_ref, first_ref, last_ref, out_ref, magnitude_ref, fields_ref
):
    depth = velocity_ref.shape[1]
    gradients = [
        slopes(velocity_ref[a], below_ref[a], above_ref[a], first_ref[a], last_ref[a])
        for a in range(3)
    ]
    strain_parts, magnitude = strain(gradients)
    magnitude_ref[...] = magnitude
    for p, part_value in enumerate(strain_parts):
        fields_ref[p * depth : (p + 1) * depth, :] = (magnitude * part_value).astype(jnp.bfloat16)
    send_blocks(table_ref, fields_ref, out_ref, 6, depth)


def smooth_kernel(table_ref, recv_ref, smooth_ref, first_ref, last_ref, lines_ref):
    width = smooth_ref.shape[1]
    gather_pair(recv_ref, 0, lines_ref, 0, width)
    gather_pair(recv_ref, 1, lines_ref, 2, width)
    got = nt(lines_ref[...], table_ref[...]).astype(jnp.bfloat16)
    for a in range(3):
        smooth_ref[a] = got[a * width : (a + 1) * width, :]
        first_ref[a] = got[a * width : a * width + 1, :]
        last_ref[a] = got[(a + 1) * width - 1 : (a + 1) * width, :]


def leonard_kernel(table_ref, recv_ref, smooth_ref, leonard_ref, lines_ref):
    width = smooth_ref.shape[1]
    gather_second(recv_ref, 1, lines_ref, 0, width)
    gather_pair(recv_ref, 2, lines_ref, 1, width)
    gather_pair(recv_ref, 3, lines_ref, 3, width)
    gather_single(recv_ref, 4, lines_ref, 5, width)
    got = nt(lines_ref[...], table_ref[...]).astype(jnp.bfloat16)
    for p, (a, b) in enumerate(index_pairs):
        product = smooth_ref[a].astype(jnp.float32) * smooth_ref[b].astype(jnp.float32)
        leonard_ref[p] = got[p * width : (p + 1) * width, :].astype(jnp.float32) - product


def model_kernel(smooth_ref, below_ref, above_ref, first_ref, last_ref, model_ref):
    gradients = []
    for a in range(3):
        arrays = [
            ref[a].astype(jnp.float32)
            for ref in (smooth_ref, below_ref, above_ref, first_ref, last_ref)
        ]
        along, across, between = slopes(*arrays)
        gradients.append((between, across, along))
    strain_parts, magnitude = strain(gradients)
    for p, part_value in enumerate(strain_parts):
        model_ref[p] = 4.0 * magnitude * part_value


def sums_kernel(table_ref, recv_ref, leonard_ref, model_ref, out_ref, lines_ref):
    width = leonard_ref.shape[1]
    for j in range(3):
        gather_pair(recv_ref, j, lines_ref, 2 * j, width)
    got = nt(lines_ref[...], table_ref[...]).astype(jnp.bfloat16)
    numerator = jnp.zeros(leonard_ref.shape[1:], jnp.float32)
    denominator = jnp.zeros(leonard_ref.shape[1:], jnp.float32)
    for p, weight in enumerate(pair_weights):
        model_term = got[p * width : (p + 1) * width, :].astype(jnp.float32) - model_ref[p]
        numerator = numerator + weight * leonard_ref[p] * model_term
        denominator = denominator + weight * model_term * model_term

    def lanes(x):
        x = x.reshape(width // 8, 8, x.shape[1]).sum(axis=0)
        total = x[:, :LANES]
        for at in range(LANES, x.shape[1], LANES):
            total = total + x[:, at : at + LANES]
        return total

    pair = jnp.concatenate([lanes(numerator), lanes(denominator)], axis=0)
    out_ref[...] = jnp.broadcast_to(pair, out_ref.shape)


def viscosity_kernel(cells, sums_ref, magnitude_ref, out_ref):
    total = sums_ref[...].sum(axis=0)
    numerator = jnp.sum(total[:8, :])
    denominator = jnp.sum(total[8:, :])
    down = jnp.full((8, LANES), 2.0 * (denominator / cells + epsilon), jnp.float32)
    coefficient = (jnp.full((8, LANES), numerator / cells, jnp.float32) / down)[:1, :1]
    out_ref[...] = magnitude_ref[...] * coefficient


def body(velocity):
    _, _, depth, nx = velocity.shape
    parts = lax.axis_size("pz")
    rows = lax.axis_size("py")
    nz = depth * parts
    width = nx // parts
    f32, bf16 = jnp.float32, jnp.bfloat16
    table_x = filter_table(nx)
    table_z = filter_table(nz)
    lanes_x = jnp.asarray(np.ascontiguousarray(table_x.T))
    lanes_z = lanes_x if np.array_equal(table_x.T, table_z) else jnp.asarray(table_z)
    up = [(i, i + 1) for i in range(rows - 1)]
    down = [(b, a) for a, b in up]
    around = [(i, (i + 1) % parts) for i in range(parts)]
    back = [(b, a) for a, b in around]
    velocity = velocity.reshape(3, depth, nx)

    send = call(
        products_kernel,
        jax.ShapeDtypeStruct((parts, 9 * width // 2, LANES), bf16),
        2 * 9 * depth * nx * nx,
        12 * depth * nx + 2 * nx * nx,
        [pltpu.VMEM((9 * depth, nx), bf16)],
        "products",
    )(lanes_x, velocity)
    received = lax.all_to_all(send, "pz", 0, 0, tiled=True)

    below = lax.ppermute(velocity, "py", up)
    above = lax.ppermute(velocity, "py", down)
    first = lax.ppermute(velocity[:, -1:], "pz", around)
    last = lax.ppermute(velocity[:, :1], "pz", back)
    send_strain, magnitude = call(
        strain_kernel,
        (
            jax.ShapeDtypeStruct((parts, 3 * width, LANES), bf16),
            jax.ShapeDtypeStruct((depth, nx), f32),
        ),
        2 * 6 * depth * nx * nx,
        36 * depth * nx + 2 * nx * nx,
        [pltpu.VMEM((6 * depth, nx), bf16)],
        "strain",
    )(lanes_x, velocity, below, above, first, last)
    received_strain = lax.all_to_all(send_strain, "pz", 0, 0, tiled=True)

    edge = jax.ShapeDtypeStruct((3, 1, nz), bf16)
    smooth, smooth_first, smooth_last = call(
        smooth_kernel,
        (jax.ShapeDtypeStruct((3, width, nz), bf16), edge, edge),
        2 * 4 * width * nz * nz,
        2 * nz * nz,
        [pltpu.VMEM((4 * width, nz), bf16)],
        "smooth",
    )(lanes_z, received)
    smooth_below = lax.ppermute(smooth, "py", up)
    smooth_above = lax.ppermute(smooth, "py", down)
    first_hat = lax.ppermute(smooth_last, "pz", around)
    last_hat = lax.ppermute(smooth_first, "pz", back)
    leonard = call(
        leonard_kernel,
        jax.ShapeDtypeStruct((6, width, nz), f32),
        2 * 6 * width * nz * nz,
        24 * width * nz + 2 * nz * nz,
        [pltpu.VMEM((6 * width, nz), bf16)],
        "leonard",
    )(lanes_z, received, smooth)
    model = call(
        model_kernel,
        jax.ShapeDtypeStruct((6, width, nz), f32),
        100 * width * nz,
        24 * width * nz,
        (),
        "model",
    )(smooth, smooth_below, smooth_above, first_hat, last_hat)
    sums = call(
        sums_kernel,
        jax.ShapeDtypeStruct((parts, 16, LANES), f32),
        2 * 6 * width * nz * nz,
        48 * width * nz + 2 * nz * nz,
        [pltpu.VMEM((6 * width, nz), bf16)],
        "sums",
    )(lanes_z, received_strain, leonard, model)
    totals = lax.all_to_all(sums, "pz", 0, 0, tiled=True)
    cells = nx * nz
    nu_t = call(
        lambda *refs: viscosity_kernel(cells, *refs),
        jax.ShapeDtypeStruct((depth, nx), f32),
        2 * depth * nx,
        8 * depth * nx,
        (),
        "viscosity",
    )(totals, magnitude)
    filtered_velocity = jnp.transpose(smooth, (0, 2, 1))
    return (nu_t[None], filtered_velocity[:, None])


def solution(mesh):
    in_specs = (P(None, "py", "pz", None),)
    out_specs = (P("py", "pz", None), P(None, "py", None, "pz"))
    return jax.shard_map(body, mesh=mesh, in_specs=in_specs, out_specs=out_specs, check_vma=False)
```

```python
import math

import jax
import jax.numpy as jnp
import numpy as np
from jax import lax
from jax.experimental import pallas as pl
from jax.experimental.pallas import tpu as pltpu
from jax.sharding import PartitionSpec as P

index_pairs = ((0, 0), (1, 1), (2, 2), (0, 1), (0, 2), (1, 2))
pair_weights = (1.0, 1.0, 1.0, 2.0, 2.0, 2.0)
epsilon = 1e-06
LANES = 128


def filter_table(length):
    offsets = np.arange(length, dtype=np.int64)
    wavenumbers = np.arange(1, length // 4, dtype=np.int64)
    phase = offsets[:, None] * wavenumbers[None, :] % length
    kernel = (1.0 + 2.0 * np.cos(phase * (2.0 * math.pi / length)).sum(axis=1)) / length
    kernel = kernel.astype(np.float32)
    lagged = (offsets[:, None] - offsets[None, :]) % length
    return kernel[lagged].astype(jnp.bfloat16)


def call(kernel, out_shape, flops, moved, scratch=(), name=None, far=(), room=24):
    outs = jax.tree.leaves(out_shape)

    def space(i):
        return pl.BlockSpec(memory_space=pltpu.HBM if i in far else pltpu.VMEM)

    def run(*args):
        out_specs = [space(len(args) + i) for i in range(len(outs))]
        return pl.pallas_call(
            kernel,
            out_shape=out_shape,
            in_specs=[space(i) for i in range(len(args))],
            out_specs=out_specs if isinstance(out_shape, tuple) else out_specs[0],
            scratch_shapes=list(scratch),
            cost_estimate=pl.CostEstimate(flops=flops, bytes_accessed=moved, transcendentals=0),
            compiler_params=pltpu.CompilerParams(vmem_limit_bytes=room * 1024 * 1024),
            name=name,
        )(*args)

    return run


def nt(a, b):
    return lax.dot_general(a, b, (((1,), (1,)), ((), ())), preferred_element_type=jnp.float32)


def send_blocks(table_ref, fields_ref, block_ref, out_ref, sem, count, depth, edges, tables=()):
    receivers = block_ref.shape[0]
    width = fields_ref.shape[1] // receivers
    per = LANES // depth
    full = count // per
    if edges:
        tables[0].wait()
        beside = table_ref[receivers * width :, :]
        got = nt(beside, fields_ref[: 2 * per * depth, :])
        row = lax.broadcasted_iota(jnp.int32, (receivers * 8, LANES), 0) % 8
        got = jnp.where(row < 2, got[:, :LANES], got[:, LANES:]).reshape(receivers, 8, LANES)
        block_ref[:, count * width // per :, :] = got.astype(jnp.bfloat16)
    chunks = 2
    some = receivers // chunks
    copies = []
    for c in range(chunks):
        mine = slice(c * some, (c + 1) * some)
        if tables:
            tables[1 + c].wait()
        table = table_ref[c * some * width : (c + 1) * some * width, :]
        for first in range(0, full, 2):
            here = min(2, full - first)
            got = nt(table, fields_ref[first * LANES : (first + here) * LANES, :])
            got = got.astype(jnp.bfloat16)
            for j in range(here):
                block = got[:, j * LANES : (j + 1) * LANES].reshape(some, width, LANES)
                block_ref[mine, (first + j) * width : (first + j + 1) * width, :] = block
        if count % per:
            last = fields_ref[full * LANES : count * depth, :]
            got = nt(table, jnp.concatenate([last, last], axis=0))
            got = got.reshape(some, width, LANES)
            half = width // 2
            lane = lax.broadcasted_iota(jnp.int32, (some, half, LANES), 2)
            block = jnp.where(lane < depth, got[:, :half, :], got[:, half:, :])
            at = full * width
            block_ref[mine, at : at + half, :] = block.astype(jnp.bfloat16)
        copies.append(pltpu.make_async_copy(block_ref.at[mine], out_ref.at[mine], sem.at[c]))
        copies[-1].start()
    for copy in copies:
        copy.wait()


def sorted_lines(recv_ref, t, start, count):
    low = lax.broadcasted_iota(jnp.int32, (count, LANES), 1) < LANES // 2
    even = recv_ref[2 * t, start : start + count, :].astype(jnp.float32)
    odd = recv_ref[2 * t + 1, start : start + count, :].astype(jnp.float32)
    one = jnp.where(low, even, pltpu.roll(odd, LANES // 2, 1))
    two = jnp.where(low, pltpu.roll(even, LANES // 2, 1), odd)
    return one, two


def place(lines_ref, at, t, rows):
    lines_ref[at : at + rows.shape[0], t * LANES : (t + 1) * LANES] = rows.astype(jnp.bfloat16)


def products_kernel(
    table_far, velocity_far, out_ref, table_ref, velocity_ref, fields_ref, block_ref, sem, table_sem, velocity_sem
):
    depth = velocity_ref.shape[1]
    length = velocity_ref.shape[2]
    components, tables = [], []
    for a in range(3):
        components.append(
            pltpu.make_async_copy(velocity_far.at[a], velocity_ref.at[a], velocity_sem.at[a])
        )
        components[-1].start()
    bounds = ((length, table_far.shape[0]), (0, length // 2), (length // 2, length))
    for i, (low, high) in enumerate(bounds):
        tables.append(
            pltpu.make_async_copy(
                table_far.at[low:high], table_ref.at[low:high], table_sem.at[i]
            )
        )
        tables[-1].start()
    parts = []
    for a in range(3):
        components[a].wait()
        parts.append(velocity_ref[a])
        fields_ref[a * depth : (a + 1) * depth, :] = parts[a].astype(jnp.bfloat16)
    for p, (a, b) in enumerate(index_pairs):
        at = (3 + p) * depth
        fields_ref[at : at + depth, :] = (parts[a] * parts[b]).astype(jnp.bfloat16)
    send_blocks(table_ref, fields_ref, block_ref, out_ref, sem, 9, depth, True, tables)


def strain(gradients):
    strain_parts = [0.5 * (gradients[b][a] + gradients[a][b]) for a, b in index_pairs]
    squares_sum = pair_weights[0] * strain_parts[0] * strain_parts[0]
    for weight, part_value in zip(pair_weights[1:], strain_parts[1:]):
        squares_sum = squares_sum + weight * part_value * part_value
    return (strain_parts, jnp.sqrt(2.0 * squares_sum))


def slopes(center, below, above, first, last):
    rows, length = center.shape
    row = lax.broadcasted_iota(jnp.int32, center.shape, 0)
    along = (pltpu.roll(center, length - 1, 1) - pltpu.roll(center, 1, 1)) * 0.5
    following = jnp.where(row == rows - 1, last, pltpu.roll(center, rows - 1, 0))
    previous = jnp.where(row == 0, first, pltpu.roll(center, 1, 0))
    return (along, (above - below) * 0.5, (following - previous) * 0.5)


def strain_kernel(
    table_ref, velocity_ref, below_ref, above_ref, first_ref, last_ref, out_ref, magnitude_ref,
    fields_ref, block_ref, sem,
):
    depth = velocity_ref.shape[1]
    gradients = [
        slopes(velocity_ref[a], below_ref[a], above_ref[a], first_ref[a], last_ref[a])
        for a in range(3)
    ]
    strain_parts, magnitude = strain(gradients)
    magnitude_ref[...] = magnitude
    for p, part_value in enumerate(strain_parts):
        fields_ref[p * depth : (p + 1) * depth, :] = (magnitude * part_value).astype(jnp.bfloat16)
    send_blocks(table_ref, fields_ref, block_ref, out_ref, sem, 6, depth, False)


def smooth_kernel(table_ref, recv_ref, smooth_ref, edges_ref, lines_ref):
    senders = recv_ref.shape[0]
    _, width, length = smooth_ref.shape
    for t in range(senders // 2):
        one, two = sorted_lines(recv_ref, t, 0, width)
        place(lines_ref, 0, t, one)
        place(lines_ref, width, t, two)
        one, two = sorted_lines(recv_ref, t, width, width)
        place(lines_ref, 2 * width, t, one)
        one, two = sorted_lines(recv_ref, t, 9 * width // 2, 8)
        place(lines_ref, 3 * width, t, jnp.concatenate([one, two], axis=0))
    got = nt(lines_ref[...], table_ref[:length, :]).astype(jnp.bfloat16)
    for a in range(3):
        smooth_ref[a] = got[a * width : (a + 1) * width, :]
    edges_ref[...] = got[3 * width :, :].astype(jnp.float32)


def leonard_kernel(table_ref, recv_ref, smooth_ref, out_ref, lines_ref, leonard_ref, sem):
    senders = recv_ref.shape[0]
    _, width, length = smooth_ref.shape
    half = width // 2
    for t in range(senders // 2):
        place(lines_ref, 0, t, sorted_lines(recv_ref, t, width, width)[1])
        for j in range(2):
            one, two = sorted_lines(recv_ref, t, (2 + j) * width, width)
            place(lines_ref, (1 + 2 * j) * width, t, one)
            place(lines_ref, (2 + 2 * j) * width, t, two)
        one, two = sorted_lines(recv_ref, t, 4 * width, half)
        place(lines_ref, 5 * width, t, one)
        place(lines_ref, 5 * width + half, t, two)
    got = nt(lines_ref[...], table_ref[:length, :]).astype(jnp.bfloat16)
    for p, (a, b) in enumerate(index_pairs):
        product = smooth_ref[a].astype(jnp.float32) * smooth_ref[b].astype(jnp.float32)
        leonard_ref[p] = got[p * width : (p + 1) * width, :].astype(jnp.float32) - product
    copy = pltpu.make_async_copy(leonard_ref, out_ref, sem)
    copy.start()
    copy.wait()


def model_kernel(smooth_ref, below_ref, above_ref, edges_ref, out_ref, model_ref, sem):
    gradients = []
    for a, at in zip(range(3), (0, 8, 2)):
        center, below, above = (
            ref[a].astype(jnp.float32) for ref in (smooth_ref, below_ref, above_ref)
        )
        first, last = edges_ref[at : at + 1, :], edges_ref[at + 1 : at + 2, :]
        along, across, between = slopes(center, below, above, first, last)
        gradients.append((between, across, along))
    strain_parts, magnitude = strain(gradients)
    for p, part_value in enumerate(strain_parts):
        model_ref[p] = 4.0 * magnitude * part_value
    copy = pltpu.make_async_copy(model_ref, out_ref, sem)
    copy.start()
    copy.wait()


def sums_kernel(
    table_far, recv_far, leonard_far, model_far, out_ref,
    table_ref, recv_ref, leonard_ref, model_ref, lines_ref, table_sem, recv_sem, leonard_sem, model_sem,
):
    senders = recv_ref.shape[0]
    _, width, length = leonard_ref.shape
    groups = recv_sem.shape[0]
    some = senders // groups
    arrivals = []
    for g in range(groups):
        mine = slice(g * some, (g + 1) * some)
        arrivals.append(pltpu.make_async_copy(recv_far.at[mine], recv_ref.at[mine], recv_sem.at[g]))
        arrivals[-1].start()
    table = pltpu.make_async_copy(table_far.at[:length], table_ref, table_sem)
    table.start()
    terms = []
    for p in range(6):
        terms.append(
            (
                pltpu.make_async_copy(model_far.at[p], model_ref.at[p], model_sem.at[p]),
                pltpu.make_async_copy(leonard_far.at[p], leonard_ref.at[p], leonard_sem.at[p]),
            )
        )
        for copy in terms[-1]:
            copy.start()
    for g in range(groups):
        arrivals[g].wait()
        for t in range(g * some // 2, (g + 1) * some // 2):
            for j in range(3):
                one, two = sorted_lines(recv_ref, t, j * width, width)
                place(lines_ref, 2 * j * width, t, one)
                place(lines_ref, (2 * j + 1) * width, t, two)
    table.wait()
    got = nt(lines_ref[...], table_ref[...]).astype(jnp.bfloat16)
    numerator = jnp.zeros((8, length), jnp.float32)
    denominator = jnp.zeros((8, length), jnp.float32)
    for p, weight in enumerate(pair_weights):
        for copy in terms[p]:
            copy.wait()
        model_term = got[p * width : (p + 1) * width, :].astype(jnp.float32) - model_ref[p]
        top = leonard_ref[p] * model_term
        bottom = model_term * model_term
        numerator = numerator + weight * top.reshape(width // 8, 8, length).sum(axis=0)
        denominator = denominator + weight * bottom.reshape(width // 8, 8, length).sum(axis=0)

    def lanes(x):
        total = x[:, :LANES]
        for at in range(LANES, length, LANES):
            total = total + x[:, at : at + LANES]
        total = total.sum(axis=0, keepdims=True)
        return total + pltpu.roll(total, LANES // 2, 1)

    low = lax.broadcasted_iota(jnp.int32, (1, LANES), 1) < LANES // 2
    pair = jnp.where(low, lanes(numerator), lanes(denominator))
    out_ref[...] = jnp.broadcast_to(pair, out_ref.shape)


def viscosity_kernel(cells, sums_ref, magnitude_ref, out_ref):
    total = sums_ref[...].sum(axis=0)
    low = lax.broadcasted_iota(jnp.int32, total.shape, 1) < LANES // 2
    numerator = jnp.sum(jnp.where(low, total, 0.0), axis=1, keepdims=True)
    denominator = jnp.sum(jnp.where(low, 0.0, total), axis=1, keepdims=True)
    coefficient = numerator / cells / (2.0 * (denominator / cells + epsilon))
    out_ref[...] = magnitude_ref[...] * coefficient


def body(velocity):
    _, _, depth, nx = velocity.shape
    parts = lax.axis_size("pz")
    rows = lax.axis_size("py")
    nz = depth * parts
    width = nx // parts
    f32, bf16 = jnp.float32, jnp.bfloat16
    table_x = filter_table(nx).T
    table_z = filter_table(nz)
    beside = np.zeros((parts, 8, nx), bf16)
    for r in range(parts):
        beside[r, :4] = table_x[[r * width - 1, (r + 1) * width % nx] * 2]
    lanes_x = jnp.asarray(np.concatenate([table_x, beside.reshape(parts * 8, nx)]))
    lanes_z = lanes_x if np.array_equal(table_x, table_z) else jnp.asarray(table_z)
    up = [(i, i + 1) for i in range(rows - 1)]
    down = [(b, a) for a, b in up]
    around = [(i, (i + 1) % parts) for i in range(parts)]
    back = [(b, a) for a, b in around]
    velocity = velocity.reshape(3, depth, nx)
    vmem, dma = pltpu.VMEM, pltpu.SemaphoreType.DMA

    first = lax.ppermute(velocity[:, -1:], "pz", around)
    last = lax.ppermute(velocity[:, :1], "pz", back)
    send_shape = (parts, 9 * width // 2 + 8, LANES)
    send = call(
        products_kernel,
        jax.ShapeDtypeStruct(send_shape, bf16),
        2 * 9 * depth * nx * nx,
        12 * depth * nx + 2 * nx * nx,
        [
            vmem(lanes_x.shape, bf16), vmem(velocity.shape, f32),
            vmem((9 * depth, nx), bf16), vmem(send_shape, bf16), dma((2,)), dma((3,)), dma((3,)),
        ],
        "products",
        (0, 1, 2),
        58,
    )(lanes_x, velocity)
    send, first, last = lax.optimization_barrier((send, first, last))
    received = lax.all_to_all(send, "pz", 0, 0, tiled=True)

    below = lax.ppermute(velocity, "py", up)
    above = lax.ppermute(velocity, "py", down)
    strain_shape = (parts, 3 * width, LANES)
    send_strain, magnitude = call(
        strain_kernel,
        (jax.ShapeDtypeStruct(strain_shape, bf16), jax.ShapeDtypeStruct((depth, nx), f32)),
        2 * 6 * depth * nx * nx,
        36 * depth * nx + 2 * nx * nx,
        [vmem((6 * depth, nx), bf16), vmem(strain_shape, bf16), dma((2,))],
        "strain",
        (6,),
    )(lanes_x, velocity, below, above, first, last)
    received_strain = lax.all_to_all(send_strain, "pz", 0, 0, tiled=True)

    smooth, edges = call(
        smooth_kernel,
        (jax.ShapeDtypeStruct((3, width, nz), bf16), jax.ShapeDtypeStruct((16, nz), f32)),
        2 * 4 * width * nz * nz,
        2 * nz * nz,
        [vmem((3 * width + 16, nz), bf16)],
        "smooth",
    )(lanes_z, received)
    smooth_below = lax.ppermute(smooth, "py", up)
    smooth_above = lax.ppermute(smooth, "py", down)
    six = jax.ShapeDtypeStruct((6, width, nz), f32)
    leonard = call(
        leonard_kernel,
        six,
        2 * 6 * width * nz * nz,
        24 * width * nz + 2 * nz * nz,
        [vmem((6 * width, nz), bf16), vmem(six.shape, f32), dma],
        "leonard",
        (3,),
        58,
    )(lanes_z, received, smooth)
    model = call(
        model_kernel,
        six,
        100 * width * nz,
        24 * width * nz,
        [vmem(six.shape, f32), dma],
        "model",
        (4,),
        58,
    )(smooth, smooth_below, smooth_above, edges)
    sums = call(
        sums_kernel,
        jax.ShapeDtypeStruct((parts, 1, LANES), f32),
        2 * 6 * width * nz * nz,
        48 * width * nz + 2 * nz * nz,
        [
            vmem((nz, nz), bf16), vmem(strain_shape, bf16), vmem(six.shape, f32),
            vmem(six.shape, f32), vmem((6 * width, nz), bf16), dma, dma((4,)), dma((6,)), dma((6,)),
        ],
        "sums",
        (0, 1, 2, 3),
        58,
    )(lanes_z, received_strain, leonard, model)
    totals = lax.all_to_all(sums, "pz", 0, 0, tiled=True)
    cells = nx * nz
    nu_t = call(
        lambda *refs: viscosity_kernel(cells, *refs),
        jax.ShapeDtypeStruct((depth, nx), f32),
        2 * depth * nx,
        8 * depth * nx,
        (),
        "viscosity",
    )(totals, magnitude)
    filtered_velocity = jnp.transpose(smooth, (0, 2, 1))
    return (nu_t[None], filtered_velocity[:, None])


def solution(mesh):
    in_specs = (P(None, "py", "pz", None),)
    out_specs = (P("py", "pz", None), P(None, "py", None, "pz"))
    return jax.shard_map(body, mesh=mesh, in_specs=in_specs, out_specs=out_specs, check_vma=False)
```

```python
import math

import jax
import jax.numpy as jnp
import numpy as np
from jax import lax
from jax.experimental import pallas as pl
from jax.experimental.pallas import tpu as pltpu
from jax.sharding import PartitionSpec as P

index_pairs = ((0, 0), (1, 1), (2, 2), (0, 1), (0, 2), (1, 2))
pair_weights = (1.0, 1.0, 1.0, 2.0, 2.0, 2.0)
epsilon = 1e-06
LANES = 128


def filter_table(length):
    offsets = np.arange(length, dtype=np.int64)
    wavenumbers = np.arange(1, length // 4, dtype=np.int64)
    phase = offsets[:, None] * wavenumbers[None, :] % length
    kernel = (1.0 + 2.0 * np.cos(phase * (2.0 * math.pi / length)).sum(axis=1)) / length
    kernel = kernel.astype(np.float32)
    lagged = (offsets[:, None] - offsets[None, :]) % length
    return kernel[lagged].astype(jnp.bfloat16)


def call(kernel, out_shape, flops, moved, scratch=(), name=None, far=(), room=24):
    outs = jax.tree.leaves(out_shape)

    def space(i):
        return pl.BlockSpec(memory_space=pltpu.HBM if i in far else pltpu.VMEM)

    def run(*args):
        out_specs = [space(len(args) + i) for i in range(len(outs))]
        return pl.pallas_call(
            kernel,
            out_shape=out_shape,
            in_specs=[space(i) for i in range(len(args))],
            out_specs=out_specs if isinstance(out_shape, tuple) else out_specs[0],
            scratch_shapes=list(scratch),
            cost_estimate=pl.CostEstimate(flops=flops, bytes_accessed=moved, transcendentals=0),
            compiler_params=pltpu.CompilerParams(vmem_limit_bytes=room * 1024 * 1024),
            name=name,
        )(*args)

    return run


def nt(a, b):
    return lax.dot_general(a, b, (((1,), (1,)), ((), ())), preferred_element_type=jnp.float32)


def turned(rows, blocks):
    at = rows.shape[1] - blocks * LANES
    return rows if blocks == 0 else jnp.concatenate([rows[:, at:], rows[:, :at]], axis=1)


def table_rows(band_ref, first, last):
    band = band_ref[:LANES, :]
    return jnp.concatenate([turned(band, a) for a in range(first, last)], axis=0)


def send_blocks(table_ref, fields_ref, block_ref, out_ref, sem, count, depth, edges):
    receivers = block_ref.shape[0]
    width = fields_ref.shape[1] // receivers
    per = LANES // depth
    full = count // per
    if edges:
        seed = table_ref[LANES:, :]
        beside = [turned(seed, q) for q in range(receivers * width // LANES)]
        beside = jnp.concatenate(beside, axis=0)
        got = nt(beside, fields_ref[: 2 * per * depth, :])
        row = lax.broadcasted_iota(jnp.int32, (receivers * 8, LANES), 0) % 8
        got = jnp.where(row < 2, got[:, :LANES], got[:, LANES:]).reshape(receivers, 8, LANES)
        block_ref[:, count * width // per :, :] = got.astype(jnp.bfloat16)
    chunks = 2
    some = receivers // chunks
    copies = []
    for c in range(chunks):
        mine = slice(c * some, (c + 1) * some)
        blocks = some * width // LANES
        table = table_rows(table_ref, c * blocks, (c + 1) * blocks)
        for first in range(0, full, 2):
            here = min(2, full - first)
            got = nt(table, fields_ref[first * LANES : (first + here) * LANES, :])
            got = got.astype(jnp.bfloat16)
            for j in range(here):
                block = got[:, j * LANES : (j + 1) * LANES].reshape(some, width, LANES)
                block_ref[mine, (first + j) * width : (first + j + 1) * width, :] = block
        if count % per:
            last = fields_ref[full * LANES : count * depth, :]
            got = nt(table, jnp.concatenate([last, last], axis=0))
            got = got.reshape(some, width, LANES)
            half = width // 2
            lane = lax.broadcasted_iota(jnp.int32, (some, half, LANES), 2)
            block = jnp.where(lane < depth, got[:, :half, :], got[:, half:, :])
            at = full * width
            block_ref[mine, at : at + half, :] = block.astype(jnp.bfloat16)
        copies.append(pltpu.make_async_copy(block_ref.at[mine], out_ref.at[mine], sem.at[c]))
        copies[-1].start()
    for copy in copies:
        copy.wait()


def sorted_lines(recv_ref, t, start, count):
    low = lax.broadcasted_iota(jnp.int32, (count, LANES), 1) < LANES // 2
    even = recv_ref[2 * t, start : start + count, :].astype(jnp.float32)
    odd = recv_ref[2 * t + 1, start : start + count, :].astype(jnp.float32)
    one = jnp.where(low, even, pltpu.roll(odd, LANES // 2, 1))
    two = jnp.where(low, pltpu.roll(even, LANES // 2, 1), odd)
    return one, two


def place(lines_ref, at, t, rows):
    lines_ref[at : at + rows.shape[0], t * LANES : (t + 1) * LANES] = rows.astype(jnp.bfloat16)


def products_kernel(table_ref, velocity_ref, out_ref, fields_ref, block_ref, sem):
    depth = velocity_ref.shape[1]
    parts = [velocity_ref[a] for a in range(3)]
    for a in range(3):
        fields_ref[a * depth : (a + 1) * depth, :] = parts[a].astype(jnp.bfloat16)
    for p, (a, b) in enumerate(index_pairs):
        at = (3 + p) * depth
        fields_ref[at : at + depth, :] = (parts[a] * parts[b]).astype(jnp.bfloat16)
    send_blocks(table_ref, fields_ref, block_ref, out_ref, sem, 9, depth, True)


def strain(gradients):
    strain_parts = [0.5 * (gradients[b][a] + gradients[a][b]) for a, b in index_pairs]
    squares_sum = pair_weights[0] * strain_parts[0] * strain_parts[0]
    for weight, part_value in zip(pair_weights[1:], strain_parts[1:]):
        squares_sum = squares_sum + weight * part_value * part_value
    return (strain_parts, jnp.sqrt(2.0 * squares_sum))


def slopes(center, below, above, first, last):
    rows, length = center.shape
    row = lax.broadcasted_iota(jnp.int32, center.shape, 0)
    along = (pltpu.roll(center, length - 1, 1) - pltpu.roll(center, 1, 1)) * 0.5
    following = jnp.where(row == rows - 1, last, pltpu.roll(center, rows - 1, 0))
    previous = jnp.where(row == 0, first, pltpu.roll(center, 1, 0))
    return (along, (above - below) * 0.5, (following - previous) * 0.5)


def strain_kernel(
    table_ref, velocity_ref, below_ref, above_ref, first_ref, last_ref, out_ref, magnitude_ref,
    fields_ref, block_ref, sem,
):
    depth = velocity_ref.shape[1]
    gradients = [
        slopes(velocity_ref[a], below_ref[a], above_ref[a], first_ref[a], last_ref[a])
        for a in range(3)
    ]
    strain_parts, magnitude = strain(gradients)
    magnitude_ref[...] = magnitude
    for p, part_value in enumerate(strain_parts):
        fields_ref[p * depth : (p + 1) * depth, :] = (magnitude * part_value).astype(jnp.bfloat16)
    send_blocks(table_ref, fields_ref, block_ref, out_ref, sem, 6, depth, False)


def smooth_kernel(table_ref, recv_ref, smooth_ref, edges_ref, lines_ref):
    senders = recv_ref.shape[0]
    _, width, length = smooth_ref.shape
    for t in range(senders // 2):
        one, two = sorted_lines(recv_ref, t, 0, width)
        place(lines_ref, 0, t, one)
        place(lines_ref, width, t, two)
        one, two = sorted_lines(recv_ref, t, width, width)
        place(lines_ref, 2 * width, t, one)
        one, two = sorted_lines(recv_ref, t, 9 * width // 2, 8)
        place(lines_ref, 3 * width, t, jnp.concatenate([one, two], axis=0))
    got = nt(lines_ref[...], table_rows(table_ref, 0, length // LANES)).astype(jnp.bfloat16)
    for a in range(3):
        smooth_ref[a] = got[a * width : (a + 1) * width, :]
    edges_ref[...] = got[3 * width :, :].astype(jnp.float32)


def leonard_kernel(table_ref, recv_ref, smooth_ref, leonard_ref, lines_ref):
    senders = recv_ref.shape[0]
    _, width, length = smooth_ref.shape
    half = width // 2
    for t in range(senders // 2):
        place(lines_ref, 0, t, sorted_lines(recv_ref, t, width, width)[1])
        for j in range(2):
            one, two = sorted_lines(recv_ref, t, (2 + j) * width, width)
            place(lines_ref, (1 + 2 * j) * width, t, one)
            place(lines_ref, (2 + 2 * j) * width, t, two)
        one, two = sorted_lines(recv_ref, t, 4 * width, half)
        place(lines_ref, 5 * width, t, one)
        place(lines_ref, 5 * width + half, t, two)
    got = nt(lines_ref[...], table_rows(table_ref, 0, length // LANES)).astype(jnp.bfloat16)
    for p, (a, b) in enumerate(index_pairs):
        product = smooth_ref[a].astype(jnp.float32) * smooth_ref[b].astype(jnp.float32)
        leonard_ref[p] = got[p * width : (p + 1) * width, :].astype(jnp.float32) - product


def model_kernel(smooth_ref, below_ref, above_ref, edges_ref, model_ref):
    gradients = []
    for a, at in zip(range(3), (0, 8, 2)):
        center, below, above = (
            ref[a].astype(jnp.float32) for ref in (smooth_ref, below_ref, above_ref)
        )
        first, last = edges_ref[at : at + 1, :], edges_ref[at + 1 : at + 2, :]
        along, across, between = slopes(center, below, above, first, last)
        gradients.append((between, across, along))
    strain_parts, magnitude = strain(gradients)
    for p, part_value in enumerate(strain_parts):
        model_ref[p] = 4.0 * magnitude * part_value


def sums_kernel(table_ref, recv_ref, leonard_ref, model_ref, out_ref, lines_ref):
    senders = recv_ref.shape[0]
    _, width, length = leonard_ref.shape
    for t in range(senders // 2):
        for j in range(3):
            one, two = sorted_lines(recv_ref, t, j * width, width)
            place(lines_ref, 2 * j * width, t, one)
            place(lines_ref, (2 * j + 1) * width, t, two)
    got = nt(lines_ref[...], table_rows(table_ref, 0, length // LANES)).astype(jnp.bfloat16)
    numerator = jnp.zeros((8, length), jnp.float32)
    denominator = jnp.zeros((8, length), jnp.float32)
    for p, weight in enumerate(pair_weights):
        model_term = got[p * width : (p + 1) * width, :].astype(jnp.float32) - model_ref[p]
        top = leonard_ref[p] * model_term
        bottom = model_term * model_term
        numerator = numerator + weight * top.reshape(width // 8, 8, length).sum(axis=0)
        denominator = denominator + weight * bottom.reshape(width // 8, 8, length).sum(axis=0)

    def lanes(x):
        total = x[:, :LANES]
        for at in range(LANES, length, LANES):
            total = total + x[:, at : at + LANES]
        total = total.sum(axis=0, keepdims=True)
        return total + pltpu.roll(total, LANES // 2, 1)

    low = lax.broadcasted_iota(jnp.int32, (1, LANES), 1) < LANES // 2
    pair = jnp.where(low, lanes(numerator), lanes(denominator))
    out_ref[...] = jnp.broadcast_to(pair, out_ref.shape)


def viscosity_kernel(cells, sums_ref, magnitude_ref, out_ref):
    total = sums_ref[...].sum(axis=0)
    low = lax.broadcasted_iota(jnp.int32, total.shape, 1) < LANES // 2
    numerator = jnp.sum(jnp.where(low, total, 0.0), axis=1, keepdims=True)
    denominator = jnp.sum(jnp.where(low, 0.0, total), axis=1, keepdims=True)
    coefficient = numerator / cells / (2.0 * (denominator / cells + epsilon))
    out_ref[...] = magnitude_ref[...] * coefficient


def body(velocity):
    _, _, depth, nx = velocity.shape
    parts = lax.axis_size("pz")
    rows = lax.axis_size("py")
    nz = depth * parts
    width = nx // parts
    f32, bf16 = jnp.float32, jnp.bfloat16
    table_x = filter_table(nx).T
    table_z = filter_table(nz)
    beside = np.zeros((2, 8, nx), bf16)
    for r in range(2):
        beside[r, :4] = table_x[[r * width - 1, (r + 1) * width] * 2]
    lanes_x = jnp.asarray(np.concatenate([table_x[:LANES], beside.reshape(16, nx)]))
    same = np.array_equal(table_x[:LANES], table_z[:LANES])
    lanes_z = lanes_x if same else jnp.asarray(table_z[:LANES])
    up = [(i, i + 1) for i in range(rows - 1)]
    down = [(b, a) for a, b in up]
    around = [(i, (i + 1) % parts) for i in range(parts)]
    back = [(b, a) for a, b in around]
    velocity = velocity.reshape(3, depth, nx)
    vmem, dma = pltpu.VMEM, pltpu.SemaphoreType.DMA

    first = lax.ppermute(velocity[:, -1:], "pz", around)
    last = lax.ppermute(velocity[:, :1], "pz", back)
    send_shape = (parts, 9 * width // 2 + 8, LANES)
    send = call(
        products_kernel,
        jax.ShapeDtypeStruct(send_shape, bf16),
        2 * 9 * depth * nx * nx,
        12 * depth * nx + 2 * nx * nx,
        [vmem((9 * depth, nx), bf16), vmem(send_shape, bf16), dma((2,))],
        "products",
        (2,),
        58,
    )(lanes_x, velocity)
    send, first, last = lax.optimization_barrier((send, first, last))
    received = lax.all_to_all(send, "pz", 0, 0, tiled=True)

    below = lax.ppermute(velocity, "py", up)
    above = lax.ppermute(velocity, "py", down)
    strain_shape = (parts, 3 * width, LANES)
    send_strain, magnitude = call(
        strain_kernel,
        (jax.ShapeDtypeStruct(strain_shape, bf16), jax.ShapeDtypeStruct((depth, nx), f32)),
        2 * 6 * depth * nx * nx,
        36 * depth * nx + 2 * nx * nx,
        [vmem((6 * depth, nx), bf16), vmem(strain_shape, bf16), dma((2,))],
        "strain",
        (6,),
    )(lanes_x, velocity, below, above, first, last)
    received_strain = lax.all_to_all(send_strain, "pz", 0, 0, tiled=True)

    smooth, edges = call(
        smooth_kernel,
        (jax.ShapeDtypeStruct((3, width, nz), bf16), jax.ShapeDtypeStruct((16, nz), f32)),
        2 * 4 * width * nz * nz,
        2 * nz * nz,
        [vmem((3 * width + 16, nz), bf16)],
        "smooth",
    )(lanes_z, received)
    smooth_below = lax.ppermute(smooth, "py", up)
    smooth_above = lax.ppermute(smooth, "py", down)
    six = jax.ShapeDtypeStruct((6, width, nz), f32)
    leonard = call(
        leonard_kernel,
        six,
        2 * 6 * width * nz * nz,
        24 * width * nz + 2 * nz * nz,
        [vmem((6 * width, nz), bf16)],
        "leonard",
    )(lanes_z, received, smooth)
    model = call(
        model_kernel,
        six,
        100 * width * nz,
        24 * width * nz,
        (),
        "model",
    )(smooth, smooth_below, smooth_above, edges)
    sums = call(
        sums_kernel,
        jax.ShapeDtypeStruct((parts, 1, LANES), f32),
        2 * 6 * width * nz * nz,
        48 * width * nz + 2 * nz * nz,
        [vmem((6 * width, nz), bf16)],
        "sums",
    )(lanes_z, received_strain, leonard, model)
    totals = lax.all_to_all(sums, "pz", 0, 0, tiled=True)
    cells = nx * nz
    nu_t = call(
        lambda *refs: viscosity_kernel(cells, *refs),
        jax.ShapeDtypeStruct((depth, nx), f32),
        2 * depth * nx,
        8 * depth * nx,
        (),
        "viscosity",
    )(totals, magnitude)
    filtered_velocity = jnp.transpose(smooth, (0, 2, 1))
    return (nu_t[None], filtered_velocity[:, None])


def solution(mesh):
    in_specs = (P(None, "py", "pz", None),)
    out_specs = (P("py", "pz", None), P(None, "py", None, "pz"))
    return jax.shard_map(body, mesh=mesh, in_specs=in_specs, out_specs=out_specs, check_vma=False)
```

```python
import math

import jax
import jax.numpy as jnp
import numpy as np
from jax import lax
from jax.experimental import pallas as pl
from jax.experimental.pallas import tpu as pltpu
from jax.sharding import PartitionSpec as P

index_pairs = ((0, 0), (1, 1), (2, 2), (0, 1), (0, 2), (1, 2))
pair_weights = (1.0, 1.0, 1.0, 2.0, 2.0, 2.0)
epsilon = 1e-06
LANES = 128


def filter_table(length):
    offsets = np.arange(length, dtype=np.int64)
    wavenumbers = np.arange(1, length // 4, dtype=np.int64)
    phase = offsets[:, None] * wavenumbers[None, :] % length
    kernel = (1.0 + 2.0 * np.cos(phase * (2.0 * math.pi / length)).sum(axis=1)) / length
    kernel = kernel.astype(np.float32)
    lagged = (offsets[:, None] - offsets[None, :]) % length
    return kernel[lagged].astype(jnp.bfloat16)


def call(kernel, out_shape, flops, moved, scratch=(), name=None, far=(), room=24):
    outs = jax.tree.leaves(out_shape)

    def space(i):
        return pl.BlockSpec(memory_space=pltpu.HBM if i in far else pltpu.VMEM)

    def run(*args):
        out_specs = [space(len(args) + i) for i in range(len(outs))]
        return pl.pallas_call(
            kernel,
            out_shape=out_shape,
            in_specs=[space(i) for i in range(len(args))],
            out_specs=out_specs if isinstance(out_shape, tuple) else out_specs[0],
            scratch_shapes=list(scratch),
            cost_estimate=pl.CostEstimate(flops=flops, bytes_accessed=moved, transcendentals=0),
            compiler_params=pltpu.CompilerParams(vmem_limit_bytes=room * 1024 * 1024),
            name=name,
        )(*args)

    return run


def nt(a, b):
    return lax.dot_general(a, b, (((1,), (1,)), ((), ())), preferred_element_type=jnp.float32)


def turned(rows, blocks):
    at = rows.shape[1] - blocks * LANES
    return rows if blocks == 0 else jnp.concatenate([rows[:, at:], rows[:, :at]], axis=1)


def table_rows(band_ref, first, last):
    band = band_ref[:LANES, :]
    return jnp.concatenate([turned(band, a) for a in range(first, last)], axis=0)


def send_blocks(table_ref, fields_ref, block_ref, out_ref, sem, count, depth, edges):
    receivers = block_ref.shape[0]
    width = fields_ref.shape[1] // receivers
    per = LANES // depth
    full = count // per
    if edges:
        seed = table_ref[LANES:, :]
        beside = [turned(seed, q) for q in range(receivers * width // LANES)]
        beside = jnp.concatenate(beside, axis=0)
        got = nt(beside, fields_ref[: 2 * per * depth, :])
        row = lax.broadcasted_iota(jnp.int32, (receivers * 8, LANES), 0) % 8
        got = jnp.where(row < 2, got[:, :LANES], got[:, LANES:]).reshape(receivers, 8, LANES)
        block_ref[:, count * width // per :, :] = got.astype(jnp.bfloat16)
    chunks = 2
    some = receivers // chunks
    copies = []
    for c in range(chunks):
        mine = slice(c * some, (c + 1) * some)
        blocks = some * width // LANES
        table = table_rows(table_ref, c * blocks, (c + 1) * blocks)
        for first in range(0, full, 2):
            here = min(2, full - first)
            got = nt(table, fields_ref[first * LANES : (first + here) * LANES, :])
            got = got.astype(jnp.bfloat16)
            for j in range(here):
                block = got[:, j * LANES : (j + 1) * LANES].reshape(some, width, LANES)
                block_ref[mine, (first + j) * width : (first + j + 1) * width, :] = block
        if count % per:
            last = fields_ref[full * LANES : count * depth, :]
            got = nt(table, jnp.concatenate([last, last], axis=0))
            got = got.reshape(some, width, LANES)
            half = width // 2
            lane = lax.broadcasted_iota(jnp.int32, (some, half, LANES), 2)
            block = jnp.where(lane < depth, got[:, :half, :], got[:, half:, :])
            at = full * width
            block_ref[mine, at : at + half, :] = block.astype(jnp.bfloat16)
        copies.append(pltpu.make_async_copy(block_ref.at[mine], out_ref.at[mine], sem.at[c]))
        copies[-1].start()
    for copy in copies:
        copy.wait()


def sorted_lines(recv_ref, t, start, count):
    low = lax.broadcasted_iota(jnp.int32, (count, LANES), 1) < LANES // 2
    even = recv_ref[2 * t, start : start + count, :].astype(jnp.float32)
    odd = recv_ref[2 * t + 1, start : start + count, :].astype(jnp.float32)
    one = jnp.where(low, even, pltpu.roll(odd, LANES // 2, 1))
    two = jnp.where(low, pltpu.roll(even, LANES // 2, 1), odd)
    return one, two


def place(lines_ref, at, t, rows):
    lines_ref[at : at + rows.shape[0], t * LANES : (t + 1) * LANES] = rows.astype(jnp.bfloat16)


def products_kernel(table_ref, velocity_ref, out_ref, fields_ref, block_ref, sem):
    depth = velocity_ref.shape[1]
    parts = [velocity_ref[a] for a in range(3)]
    for a in range(3):
        fields_ref[a * depth : (a + 1) * depth, :] = parts[a].astype(jnp.bfloat16)
    for p, (a, b) in enumerate(index_pairs):
        at = (3 + p) * depth
        fields_ref[at : at + depth, :] = (parts[a] * parts[b]).astype(jnp.bfloat16)
    send_blocks(table_ref, fields_ref, block_ref, out_ref, sem, 9, depth, True)


def strain(gradients):
    strain_parts = [0.5 * (gradients[b][a] + gradients[a][b]) for a, b in index_pairs]
    squares_sum = pair_weights[0] * strain_parts[0] * strain_parts[0]
    for weight, part_value in zip(pair_weights[1:], strain_parts[1:]):
        squares_sum = squares_sum + weight * part_value * part_value
    return (strain_parts, jnp.sqrt(2.0 * squares_sum))


def slopes(center, one, two, sense, first, last):
    rows, length = center.shape
    row = lax.broadcasted_iota(jnp.int32, center.shape, 0)
    along = (pltpu.roll(center, length - 1, 1) - pltpu.roll(center, 1, 1)) * 0.5
    following = jnp.where(row == rows - 1, last, pltpu.roll(center, rows - 1, 0))
    previous = jnp.where(row == 0, first, pltpu.roll(center, 1, 0))
    return (along, (two - one) * sense, (following - previous) * 0.5)


def strain_kernel(
    table_ref, velocity_ref, one_ref, two_ref, sense_ref, first_ref, last_ref, out_ref, magnitude_ref,
    fields_ref, block_ref, sem,
):
    depth = velocity_ref.shape[1]
    gradients = [
        slopes(velocity_ref[a], one_ref[a], two_ref[a], sense_ref[...], first_ref[a], last_ref[a])
        for a in range(3)
    ]
    strain_parts, magnitude = strain(gradients)
    magnitude_ref[...] = magnitude
    for p, part_value in enumerate(strain_parts):
        fields_ref[p * depth : (p + 1) * depth, :] = (magnitude * part_value).astype(jnp.bfloat16)
    send_blocks(table_ref, fields_ref, block_ref, out_ref, sem, 6, depth, False)


def smooth_kernel(table_ref, recv_ref, smooth_ref, edges_ref, lines_ref):
    senders = recv_ref.shape[0]
    _, width, length = smooth_ref.shape
    for t in range(senders // 2):
        one, two = sorted_lines(recv_ref, t, 0, width)
        place(lines_ref, 0, t, one)
        place(lines_ref, width, t, two)
        one, two = sorted_lines(recv_ref, t, width, width)
        place(lines_ref, 2 * width, t, one)
        one, two = sorted_lines(recv_ref, t, 9 * width // 2, 8)
        place(lines_ref, 3 * width, t, jnp.concatenate([one, two], axis=0))
    got = nt(lines_ref[...], table_rows(table_ref, 0, length // LANES)).astype(jnp.bfloat16)
    for a in range(3):
        smooth_ref[a] = got[a * width : (a + 1) * width, :]
    edges_ref[...] = got[3 * width :, :].astype(jnp.float32)


def squares_kernel(table_ref, recv_ref, squares_ref, lines_ref):
    senders = recv_ref.shape[0]
    _, width, length = squares_ref.shape
    half = width // 2
    for t in range(senders // 2):
        place(lines_ref, 0, t, sorted_lines(recv_ref, t, width, width)[1])
        for j in range(2):
            one, two = sorted_lines(recv_ref, t, (2 + j) * width, width)
            place(lines_ref, (1 + 2 * j) * width, t, one)
            place(lines_ref, (2 + 2 * j) * width, t, two)
        one, two = sorted_lines(recv_ref, t, 4 * width, half)
        place(lines_ref, 5 * width, t, one)
        place(lines_ref, 5 * width + half, t, two)
    got = nt(lines_ref[...], table_rows(table_ref, 0, length // LANES)).astype(jnp.bfloat16)
    for p in range(6):
        squares_ref[p] = got[p * width : (p + 1) * width, :]


def model_kernel(smooth_ref, one_ref, two_ref, sense_ref, edges_ref, model_ref):
    gradients = []
    for a, at in zip(range(3), (0, 8, 2)):
        center, one, two = (ref[a].astype(jnp.float32) for ref in (smooth_ref, one_ref, two_ref))
        first, last = edges_ref[at : at + 1, :], edges_ref[at + 1 : at + 2, :]
        along, across, between = slopes(center, one, two, sense_ref[...], first, last)
        gradients.append((between, across, along))
    strain_parts, magnitude = strain(gradients)
    for p, part_value in enumerate(strain_parts):
        model_ref[p] = 4.0 * magnitude * part_value


def sums_kernel(
    table_ref, recv_far, smooth_ref, squares_ref, model_ref, out_ref, recv_ref, lines_ref, sem
):
    senders = recv_ref.shape[0]
    _, width, length = model_ref.shape
    groups = sem.shape[0]
    some = senders // groups
    arrivals = []
    for g in range(groups):
        mine = slice(g * some, (g + 1) * some)
        arrivals.append(pltpu.make_async_copy(recv_far.at[mine], recv_ref.at[mine], sem.at[g]))
        arrivals[-1].start()
    for g in range(groups):
        arrivals[g].wait()
        for t in range(g * some // 2, (g + 1) * some // 2):
            for j in range(3):
                one, two = sorted_lines(recv_ref, t, j * width, width)
                place(lines_ref, 2 * j * width, t, one)
                place(lines_ref, (2 * j + 1) * width, t, two)
    got = nt(lines_ref[...], table_rows(table_ref, 0, length // LANES)).astype(jnp.bfloat16)
    smooth = [smooth_ref[a].astype(jnp.float32) for a in range(3)]
    numerator = jnp.zeros((8, length), jnp.float32)
    denominator = jnp.zeros((8, length), jnp.float32)
    for p, (weight, (a, b)) in enumerate(zip(pair_weights, index_pairs)):
        leonard = squares_ref[p].astype(jnp.float32) - smooth[a] * smooth[b]
        model_term = got[p * width : (p + 1) * width, :].astype(jnp.float32) - model_ref[p]
        top = leonard * model_term
        bottom = model_term * model_term
        numerator = numerator + weight * top.reshape(width // 8, 8, length).sum(axis=0)
        denominator = denominator + weight * bottom.reshape(width // 8, 8, length).sum(axis=0)

    def lanes(x):
        total = x[:, :LANES]
        for at in range(LANES, length, LANES):
            total = total + x[:, at : at + LANES]
        total = total.sum(axis=0, keepdims=True)
        return total + pltpu.roll(total, LANES // 2, 1)

    low = lax.broadcasted_iota(jnp.int32, (1, LANES), 1) < LANES // 2
    pair = jnp.where(low, lanes(numerator), lanes(denominator))
    out_ref[...] = jnp.broadcast_to(pair, out_ref.shape)


def viscosity_kernel(cells, sums_ref, magnitude_ref, out_ref):
    total = sums_ref[...].sum(axis=0)
    low = lax.broadcasted_iota(jnp.int32, total.shape, 1) < LANES // 2
    numerator = jnp.sum(jnp.where(low, total, 0.0), axis=1, keepdims=True)
    denominator = jnp.sum(jnp.where(low, 0.0, total), axis=1, keepdims=True)
    coefficient = numerator / cells / (2.0 * (denominator / cells + epsilon))
    out_ref[...] = magnitude_ref[...] * coefficient


def body(velocity):
    _, _, depth, nx = velocity.shape
    parts = lax.axis_size("pz")
    rows = lax.axis_size("py")
    nz = depth * parts
    width = nx // parts
    f32, bf16 = jnp.float32, jnp.bfloat16
    table_x = filter_table(nx).T
    table_z = filter_table(nz)
    beside = np.zeros((2, 8, nx), bf16)
    for r in range(2):
        beside[r, :4] = table_x[[r * width - 1, (r + 1) * width] * 2]
    lanes_x = jnp.asarray(np.concatenate([table_x[:LANES], beside.reshape(16, nx)]))
    same = np.array_equal(table_x[:LANES], table_z[:LANES])
    lanes_z = lanes_x if same else jnp.asarray(table_z[:LANES])
    outward, inward = [], []
    for i in range(rows - 1):
        for j in range(parts):
            pair = (i * parts + j, (i + 1) * parts + j)
            (inward if j % 2 else outward).append(pair)
            (outward if j % 2 else inward).append(pair[::-1])
    sense = (0.5 - (lax.axis_index("pz") % 2).astype(f32)).reshape(1, 1)
    around = [(i, (i + 1) % parts) for i in range(parts)]
    back = [(b, a) for a, b in around]
    velocity = velocity.reshape(3, depth, nx)
    vmem, dma = pltpu.VMEM, pltpu.SemaphoreType.DMA

    first = lax.ppermute(velocity[:, -1:], "pz", around)
    last = lax.ppermute(velocity[:, :1], "pz", back)
    send_shape = (parts, 9 * width // 2 + 8, LANES)
    send = call(
        products_kernel,
        jax.ShapeDtypeStruct(send_shape, bf16),
        2 * 9 * depth * nx * nx,
        12 * depth * nx + 2 * nx * nx,
        [vmem((9 * depth, nx), bf16), vmem(send_shape, bf16), dma((2,))],
        "products",
        (2,),
        58,
    )(lanes_x, velocity)
    send, first, last = lax.optimization_barrier((send, first, last))
    received = lax.all_to_all(send, "pz", 0, 0, tiled=True)

    one = lax.ppermute(velocity, ("py", "pz"), outward)
    two = lax.ppermute(velocity, ("py", "pz"), inward)
    strain_shape = (parts, 3 * width, LANES)
    send_strain, magnitude = call(
        strain_kernel,
        (jax.ShapeDtypeStruct(strain_shape, bf16), jax.ShapeDtypeStruct((depth, nx), f32)),
        2 * 6 * depth * nx * nx,
        36 * depth * nx + 2 * nx * nx,
        [vmem((6 * depth, nx), bf16), vmem(strain_shape, bf16), dma((2,))],
        "strain",
        (7,),
    )(lanes_x, velocity, one, two, sense, first, last)
    received_strain = lax.all_to_all(send_strain, "pz", 0, 0, tiled=True)

    smooth, edges = call(
        smooth_kernel,
        (jax.ShapeDtypeStruct((3, width, nz), bf16), jax.ShapeDtypeStruct((16, nz), f32)),
        2 * 4 * width * nz * nz,
        2 * nz * nz,
        [vmem((3 * width + 16, nz), bf16)],
        "smooth",
    )(lanes_z, received)
    smooth_one = lax.ppermute(smooth, ("py", "pz"), outward)
    smooth_two = lax.ppermute(smooth, ("py", "pz"), inward)
    squares = call(
        squares_kernel,
        jax.ShapeDtypeStruct((6, width, nz), bf16),
        2 * 6 * width * nz * nz,
        24 * width * nz,
        [vmem((6 * width, nz), bf16)],
        "squares",
    )(lanes_z, received)
    model = call(
        model_kernel,
        jax.ShapeDtypeStruct((6, width, nz), f32),
        100 * width * nz,
        24 * width * nz,
        (),
        "model",
    )(smooth, smooth_one, smooth_two, sense, edges)
    sums = call(
        sums_kernel,
        jax.ShapeDtypeStruct((parts, 1, LANES), f32),
        2 * 6 * width * nz * nz,
        48 * width * nz,
        [vmem(strain_shape, bf16), vmem((6 * width, nz), bf16), dma((4,))],
        "sums",
        (1,),
    )(lanes_z, received_strain, smooth, squares, model)
    totals = lax.all_to_all(sums, "pz", 0, 0, tiled=True)
    cells = nx * nz
    nu_t = call(
        lambda *refs: viscosity_kernel(cells, *refs),
        jax.ShapeDtypeStruct((depth, nx), f32),
        2 * depth * nx,
        8 * depth * nx,
        (),
        "viscosity",
    )(totals, magnitude)
    filtered_velocity = jnp.transpose(smooth, (0, 2, 1))
    return (nu_t[None], filtered_velocity[:, None])


def solution(mesh):
    in_specs = (P(None, "py", "pz", None),)
    out_specs = (P("py", "pz", None), P(None, "py", None, "pz"))
    return jax.shard_map(body, mesh=mesh, in_specs=in_specs, out_specs=out_specs, check_vma=False)
```

```python
import math

import jax
import jax.numpy as jnp
import numpy as np
from jax import lax
from jax.experimental import pallas as pl
from jax.experimental.pallas import tpu as pltpu
from jax.sharding import PartitionSpec as P

index_pairs = ((0, 0), (1, 1), (2, 2), (0, 1), (0, 2), (1, 2))
pair_weights = (1.0, 1.0, 1.0, 2.0, 2.0, 2.0)
epsilon = 1e-06
LANES = 128
BAND = 32


def filter_table(length):
    offsets = np.arange(length, dtype=np.int64)
    wavenumbers = np.arange(1, length // 4, dtype=np.int64)
    phase = offsets[:, None] * wavenumbers[None, :] % length
    kernel = (1.0 + 2.0 * np.cos(phase * (2.0 * math.pi / length)).sum(axis=1)) / length
    kernel = kernel.astype(np.float32)
    lagged = (offsets[:, None] - offsets[None, :]) % length
    return kernel[lagged].astype(jnp.bfloat16)


def call(kernel, out_shape, flops, moved, scratch=(), name=None, far=(), room=24, aliases=None):
    outs = jax.tree.leaves(out_shape)

    def space(i):
        return pl.BlockSpec(memory_space=pltpu.HBM if i in far else pltpu.VMEM)

    def run(*args):
        out_specs = [space(len(args) + i) for i in range(len(outs))]
        return pl.pallas_call(
            kernel,
            out_shape=out_shape,
            in_specs=[space(i) for i in range(len(args))],
            out_specs=out_specs if isinstance(out_shape, tuple) else out_specs[0],
            scratch_shapes=list(scratch),
            cost_estimate=pl.CostEstimate(flops=flops, bytes_accessed=moved, transcendentals=0),
            compiler_params=pltpu.CompilerParams(vmem_limit_bytes=room * 1024 * 1024),
            input_output_aliases=aliases or {},
            name=name,
        )(*args)

    return run


def nt(a, b):
    return lax.dot_general(a, b, (((1,), (1,)), ((), ())), preferred_element_type=jnp.float32)


def turned(rows, blocks):
    at = rows.shape[1] - blocks * LANES
    return rows if blocks == 0 else jnp.concatenate([rows[:, at:], rows[:, :at]], axis=1)


def table_rows(band_ref):
    rows = band_ref[:BAND, :].astype(jnp.float32)
    rows = [rows] + [pltpu.roll(rows, at, 1) for at in range(BAND, LANES, BAND)]
    tile = jnp.concatenate(rows, axis=0).astype(jnp.bfloat16)
    blocks = band_ref.shape[1] // LANES
    return jnp.concatenate([turned(tile, a) for a in range(blocks)], axis=0)


def send_blocks(band_ref, fields_ref, block_ref, out_ref, sem, count, depth, edges):
    receivers = block_ref.shape[0]
    width = fields_ref.shape[1] // receivers
    per = LANES // depth
    full = count // per
    table = table_rows(band_ref)
    copies = []

    def send(first, last):
        rows = slice(first, last)
        copies.append(
            pltpu.make_async_copy(
                block_ref.at[:, rows, :], out_ref.at[:, rows, :], sem.at[len(copies)]
            )
        )
        copies[-1].start()

    for first in range(0, full, 2):
        here = min(2, full - first)
        got = nt(table, fields_ref[first * LANES : (first + here) * LANES, :])
        got = got.astype(jnp.bfloat16)
        for j in range(here):
            block = got[:, j * LANES : (j + 1) * LANES].reshape(receivers, width, LANES)
            block_ref[:, (first + j) * width : (first + j + 1) * width, :] = block
        send(first * width, (first + here) * width)
    tail = full * width
    if count % per:
        last = fields_ref[full * LANES : count * depth, :]
        got = nt(table, jnp.concatenate([last, last], axis=0))
        got = got.reshape(receivers, width, LANES)
        half = width // 2
        lane = lax.broadcasted_iota(jnp.int32, (receivers, half, LANES), 2)
        block = jnp.where(lane < depth, got[:, :half, :], got[:, half:, :])
        block_ref[:, tail : tail + half, :] = block.astype(jnp.bfloat16)
    if edges:
        seed = band_ref[BAND:, :]
        beside = [turned(seed, q) for q in range(receivers * width // LANES)]
        got = nt(jnp.concatenate(beside, axis=0), fields_ref[: 2 * LANES, :])
        row = lax.broadcasted_iota(jnp.int32, (receivers * 8, LANES), 0) % 8
        got = jnp.where(row < 2, got[:, :LANES], got[:, LANES:]).reshape(receivers, 8, LANES)
        block_ref[:, count * width // per :, :] = got.astype(jnp.bfloat16)
    if tail < block_ref.shape[1]:
        send(tail, block_ref.shape[1])
    for copy in copies:
        copy.wait()


def sorted_lines(recv_ref, t, start, count):
    low = lax.broadcasted_iota(jnp.int32, (count, LANES), 1) < LANES // 2
    even = recv_ref[2 * t, start : start + count, :].astype(jnp.float32)
    odd = recv_ref[2 * t + 1, start : start + count, :].astype(jnp.float32)
    one = jnp.where(low, even, pltpu.roll(odd, LANES // 2, 1))
    two = jnp.where(low, pltpu.roll(even, LANES // 2, 1), odd)
    return one, two


def place(lines_ref, at, t, rows):
    lines_ref[at : at + rows.shape[0], t * LANES : (t + 1) * LANES] = rows.astype(jnp.bfloat16)


def products_kernel(
    table_ref, velocity_far, out_ref, velocity_ref, fields_ref, block_ref, velocity_sem, sem
):
    depth = velocity_ref.shape[1]
    arrivals = []
    for a in range(3):
        arrivals.append(
            pltpu.make_async_copy(velocity_far.at[a], velocity_ref.at[a], velocity_sem.at[a])
        )
        arrivals[-1].start()
    for a in range(3):
        arrivals[a].wait()
        fields_ref[a * depth : (a + 1) * depth, :] = velocity_ref[a].astype(jnp.bfloat16)
        for p, pair in enumerate(index_pairs):
            if max(pair) == a:
                at = (3 + p) * depth
                product = velocity_ref[pair[0]] * velocity_ref[pair[1]]
                fields_ref[at : at + depth, :] = product.astype(jnp.bfloat16)
    send_blocks(table_ref, fields_ref, block_ref, out_ref, sem, 9, depth, True)


def strain(gradients):
    strain_parts = [0.5 * (gradients[b][a] + gradients[a][b]) for a, b in index_pairs]
    squares_sum = pair_weights[0] * strain_parts[0] * strain_parts[0]
    for weight, part_value in zip(pair_weights[1:], strain_parts[1:]):
        squares_sum = squares_sum + weight * part_value * part_value
    return (strain_parts, jnp.sqrt(2.0 * squares_sum))


def slopes(center, one, two, sense, first, last):
    rows, length = center.shape
    row = lax.broadcasted_iota(jnp.int32, center.shape, 0)
    along = (pltpu.roll(center, length - 1, 1) - pltpu.roll(center, 1, 1)) * 0.5
    following = jnp.where(row == rows - 1, last, pltpu.roll(center, rows - 1, 0))
    previous = jnp.where(row == 0, first, pltpu.roll(center, 1, 0))
    return (along, (two - one) * sense, (following - previous) * 0.5)


def strain_kernel(
    table_ref, velocity_ref, one_ref, two_ref, sense_ref, within_ref, across_ref, out_ref, magnitude_ref,
    fields_ref, block_ref, sem,
):
    depth = velocity_ref.shape[1]
    sense = sense_ref[...]
    gradients = []
    for a in range(3):
        first = jnp.where(sense > 0.0, across_ref[a], within_ref[a])
        last = jnp.where(sense > 0.0, within_ref[a], across_ref[a])
        gradients.append(slopes(velocity_ref[a], one_ref[a], two_ref[a], sense, first, last))
    strain_parts, magnitude = strain(gradients)
    magnitude_ref[...] = magnitude
    for p, part_value in enumerate(strain_parts):
        fields_ref[p * depth : (p + 1) * depth, :] = (magnitude * part_value).astype(jnp.bfloat16)
    send_blocks(table_ref, fields_ref, block_ref, out_ref, sem, 6, depth, False)


def smooth_kernel(table_ref, recv_ref, smooth_ref, edges_ref, lines_ref):
    senders = recv_ref.shape[0]
    _, width, length = smooth_ref.shape
    for t in range(senders // 2):
        one, two = sorted_lines(recv_ref, t, 0, width)
        place(lines_ref, 0, t, one)
        place(lines_ref, width, t, two)
        one, two = sorted_lines(recv_ref, t, width, width)
        place(lines_ref, 2 * width, t, one)
        one, two = sorted_lines(recv_ref, t, 9 * width // 2, 8)
        place(lines_ref, 3 * width, t, jnp.concatenate([one, two], axis=0))
    got = nt(lines_ref[...], table_rows(table_ref)).astype(jnp.bfloat16)
    for a in range(3):
        smooth_ref[a] = got[a * width : (a + 1) * width, :]
    edges_ref[...] = got[3 * width :, :].astype(jnp.float32)


def squares_kernel(table_ref, recv_ref, squares_ref, lines_ref):
    senders = recv_ref.shape[0]
    _, width, length = squares_ref.shape
    half = width // 2
    for t in range(senders // 2):
        place(lines_ref, 0, t, sorted_lines(recv_ref, t, width, width)[1])
        for j in range(2):
            one, two = sorted_lines(recv_ref, t, (2 + j) * width, width)
            place(lines_ref, (1 + 2 * j) * width, t, one)
            place(lines_ref, (2 + 2 * j) * width, t, two)
        one, two = sorted_lines(recv_ref, t, 4 * width, half)
        place(lines_ref, 5 * width, t, one)
        place(lines_ref, 5 * width + half, t, two)
    got = nt(lines_ref[...], table_rows(table_ref)).astype(jnp.bfloat16)
    for p in range(6):
        squares_ref[p] = got[p * width : (p + 1) * width, :]


def model_kernel(smooth_ref, one_ref, two_ref, sense_ref, edges_ref, model_ref):
    gradients = []
    for a, at in zip(range(3), (0, 8, 2)):
        center, one, two = (ref[a].astype(jnp.float32) for ref in (smooth_ref, one_ref, two_ref))
        first, last = edges_ref[at : at + 1, :], edges_ref[at + 1 : at + 2, :]
        along, across, between = slopes(center, one, two, sense_ref[...], first, last)
        gradients.append((between, across, along))
    strain_parts, magnitude = strain(gradients)
    for p, part_value in enumerate(strain_parts):
        model_ref[p] = 4.0 * magnitude * part_value


def sums_kernel(table_ref, recv_ref, smooth_ref, squares_ref, model_ref, out_ref, lines_ref):
    senders = recv_ref.shape[0]
    _, width, length = model_ref.shape
    for t in range(senders // 2):
        for j in range(3):
            one, two = sorted_lines(recv_ref, t, j * width, width)
            place(lines_ref, 2 * j * width, t, one)
            place(lines_ref, (2 * j + 1) * width, t, two)
    got = nt(lines_ref[...], table_rows(table_ref)).astype(jnp.bfloat16)
    smooth = [smooth_ref[a].astype(jnp.float32) for a in range(3)]
    numerator = jnp.zeros((8, length), jnp.float32)
    denominator = jnp.zeros((8, length), jnp.float32)
    for p, (weight, (a, b)) in enumerate(zip(pair_weights, index_pairs)):
        leonard = squares_ref[p].astype(jnp.float32) - smooth[a] * smooth[b]
        model_term = got[p * width : (p + 1) * width, :].astype(jnp.float32) - model_ref[p]
        top = leonard * model_term
        bottom = model_term * model_term
        numerator = numerator + weight * top.reshape(width // 8, 8, length).sum(axis=0)
        denominator = denominator + weight * bottom.reshape(width // 8, 8, length).sum(axis=0)

    def lanes(x):
        total = x[:, :LANES]
        for at in range(LANES, length, LANES):
            total = total + x[:, at : at + LANES]
        total = total.sum(axis=0, keepdims=True)
        return total + pltpu.roll(total, LANES // 2, 1)

    low = lax.broadcasted_iota(jnp.int32, (1, LANES), 1) < LANES // 2
    pair = jnp.where(low, lanes(numerator), lanes(denominator))
    out_ref[...] = jnp.broadcast_to(pair, out_ref.shape)


def viscosity_kernel(cells, sums_ref, magnitude_ref, out_ref):
    total = sums_ref[...].sum(axis=0)
    low = lax.broadcasted_iota(jnp.int32, total.shape, 1) < LANES // 2
    numerator = jnp.sum(jnp.where(low, total, 0.0), axis=1, keepdims=True)
    denominator = jnp.sum(jnp.where(low, 0.0, total), axis=1, keepdims=True)
    coefficient = numerator / cells / (2.0 * (denominator / cells + epsilon))
    out_ref[...] = magnitude_ref[...] * coefficient


def body(velocity):
    _, _, depth, nx = velocity.shape
    parts = lax.axis_size("pz")
    rows = lax.axis_size("py")
    nz = depth * parts
    width = nx // parts
    f32, bf16 = jnp.float32, jnp.bfloat16
    table_x = filter_table(nx).T
    table_z = filter_table(nz)
    beside = np.zeros((2, 8, nx), bf16)
    for r in range(2):
        beside[r, :4] = table_x[[r * width - 1, (r + 1) * width] * 2]
    lanes_x = jnp.asarray(np.concatenate([table_x[:BAND], beside.reshape(16, nx)]))
    lanes_z = jnp.asarray(table_z[:BAND])
    outward, inward = [], []
    for i in range(rows - 1):
        for j in range(parts):
            pair = (i * parts + j, (i + 1) * parts + j)
            (inward if j % 2 else outward).append(pair)
            (outward if j % 2 else inward).append(pair[::-1])
    sense = (0.5 - (lax.axis_index("pz") % 2).astype(f32)).reshape(1, 1)
    inside = [(j, j ^ 1) for j in range(parts)]
    outside = [(j, (j + 1 if j % 2 else j - 1) % parts) for j in range(parts)]
    velocity = velocity.reshape(3, depth, nx)
    vmem, dma = pltpu.VMEM, pltpu.SemaphoreType.DMA

    low, high = velocity[:, :1], velocity[:, -1:]
    even = lax.axis_index("pz") % 2 == 0
    within = lax.ppermute(jnp.where(even, high, low), "pz", inside)
    across = lax.ppermute(jnp.where(even, low, high), "pz", outside)
    send_shape = (parts, 9 * width // 2 + 8, LANES)
    send = call(
        products_kernel,
        jax.ShapeDtypeStruct(send_shape, bf16),
        2 * 9 * depth * nx * nx,
        12 * depth * nx + 2 * nx * nx,
        [
            vmem(velocity.shape, f32), vmem((9 * depth, nx), bf16), vmem(send_shape, bf16),
            dma((3,)), dma((3,)),
        ],
        "products",
        (1, 2),
        58,
    )(lanes_x, velocity)
    send, within, across = lax.optimization_barrier((send, within, across))
    received = lax.all_to_all(send, "pz", 0, 0, tiled=True)

    one = lax.ppermute(velocity, ("py", "pz"), outward)
    two = lax.ppermute(velocity, ("py", "pz"), inward)
    strain_shape = (parts, 3 * width, LANES)
    send_strain, magnitude = call(
        strain_kernel,
        (jax.ShapeDtypeStruct(strain_shape, bf16), jax.ShapeDtypeStruct((depth, nx), f32)),
        2 * 6 * depth * nx * nx,
        36 * depth * nx + 2 * nx * nx,
        [vmem((6 * depth, nx), bf16), vmem(strain_shape, bf16), dma((2,))],
        "strain",
        (7,),
    )(lanes_x, velocity, one, two, sense, within, across)
    received_strain = lax.all_to_all(send_strain, "pz", 0, 0, tiled=True)

    smooth, edges = call(
        smooth_kernel,
        (jax.ShapeDtypeStruct((3, width, nz), bf16), jax.ShapeDtypeStruct((16, nz), f32)),
        2 * 4 * width * nz * nz,
        2 * nz * nz,
        [vmem((3 * width + 16, nz), bf16)],
        "smooth",
    )(lanes_z, received)
    smooth_one = lax.ppermute(smooth, ("py", "pz"), outward)
    smooth_two = lax.ppermute(smooth, ("py", "pz"), inward)
    squares = call(
        squares_kernel,
        jax.ShapeDtypeStruct((6, width, nz), bf16),
        2 * 6 * width * nz * nz,
        24 * width * nz,
        [vmem((6 * width, nz), bf16)],
        "squares",
    )(lanes_z, received)
    model = call(
        model_kernel,
        jax.ShapeDtypeStruct((6, width, nz), f32),
        100 * width * nz,
        24 * width * nz,
        (),
        "model",
    )(smooth, smooth_one, smooth_two, sense, edges)
    sums = call(
        sums_kernel,
        jax.ShapeDtypeStruct((parts, 1, LANES), f32),
        2 * 6 * width * nz * nz,
        48 * width * nz,
        [vmem((6 * width, nz), bf16)],
        "sums",
    )(lanes_z, received_strain, smooth, squares, model)
    totals = lax.all_to_all(sums, "pz", 0, 0, tiled=True)
    cells = nx * nz
    nu_t = call(
        lambda *refs: viscosity_kernel(cells, *refs),
        jax.ShapeDtypeStruct((depth, nx), f32),
        2 * depth * nx,
        8 * depth * nx,
        (),
        "viscosity",
        aliases={1: 0},
    )(totals, magnitude)
    filtered_velocity = jnp.transpose(smooth, (0, 2, 1))
    return (nu_t[None], filtered_velocity[:, None])


def solution(mesh):
    in_specs = (P(None, "py", "pz", None),)
    out_specs = (P("py", "pz", None), P(None, "py", None, "pz"))
    return jax.shard_map(body, mesh=mesh, in_specs=in_specs, out_specs=out_specs, check_vma=False)
```

```python
import math

import jax
import jax.numpy as jnp
import numpy as np
from jax import lax
from jax.experimental import pallas as pl
from jax.experimental.pallas import tpu as pltpu
from jax.sharding import PartitionSpec as P

index_pairs = ((0, 0), (1, 1), (2, 2), (0, 1), (0, 2), (1, 2))
pair_weights = (1.0, 1.0, 1.0, 2.0, 2.0, 2.0)
epsilon = 1e-06
LANES = 128
BAND = 32


def filter_table(length):
    offsets = np.arange(length, dtype=np.int64)
    wavenumbers = np.arange(1, length // 4, dtype=np.int64)
    phase = offsets[:, None] * wavenumbers[None, :] % length
    kernel = (1.0 + 2.0 * np.cos(phase * (2.0 * math.pi / length)).sum(axis=1)) / length
    kernel = kernel.astype(np.float32)
    lagged = (offsets[:, None] - offsets[None, :]) % length
    return kernel[lagged].astype(jnp.bfloat16)


def call(kernel, out_shape, flops, moved, scratch=(), name=None, far=(), room=24):
    outs = jax.tree.leaves(out_shape)

    def space(i):
        return pl.BlockSpec(memory_space=pltpu.HBM if i in far else pltpu.VMEM)

    def run(*args):
        out_specs = [space(len(args) + i) for i in range(len(outs))]
        return pl.pallas_call(
            kernel,
            out_shape=out_shape,
            in_specs=[space(i) for i in range(len(args))],
            out_specs=out_specs if isinstance(out_shape, tuple) else out_specs[0],
            scratch_shapes=list(scratch),
            cost_estimate=pl.CostEstimate(flops=flops, bytes_accessed=moved, transcendentals=0),
            compiler_params=pltpu.CompilerParams(vmem_limit_bytes=room * 1024 * 1024),
            name=name,
        )(*args)

    return run


def nt(a, b):
    return lax.dot_general(a, b, (((1,), (1,)), ((), ())), preferred_element_type=jnp.float32)


def turned(rows, blocks):
    at = rows.shape[1] - blocks * LANES
    return rows if blocks == 0 else jnp.concatenate([rows[:, at:], rows[:, :at]], axis=1)


def table_rows(band_ref, first, last):
    band = band_ref[:LANES, :]
    return jnp.concatenate([turned(band, a) for a in range(first, last)], axis=0)


def table_of(band):
    band = band.astype(jnp.float32)
    rows = [band] + [pltpu.roll(band, at, 1) for at in range(BAND, LANES, BAND)]
    tile = jnp.concatenate(rows, axis=0).astype(jnp.bfloat16)
    return jnp.concatenate([turned(tile, a) for a in range(band.shape[1] // LANES)], axis=0)


def send_blocks(table_ref, fields_ref, block_ref, out_ref, sem, count, depth, edges):
    receivers = block_ref.shape[0]
    width = fields_ref.shape[1] // receivers
    per = LANES // depth
    full = count // per
    if edges:
        seed = table_ref[LANES:, :]
        beside = [turned(seed, q) for q in range(receivers * width // LANES)]
        beside = jnp.concatenate(beside, axis=0)
        got = nt(beside, fields_ref[: 2 * per * depth, :])
        row = lax.broadcasted_iota(jnp.int32, (receivers * 8, LANES), 0) % 8
        got = jnp.where(row < 2, got[:, :LANES], got[:, LANES:]).reshape(receivers, 8, LANES)
        block_ref[:, count * width // per :, :] = got.astype(jnp.bfloat16)
    chunks = 2
    some = receivers // chunks
    copies = []
    for c in range(chunks):
        mine = slice(c * some, (c + 1) * some)
        blocks = some * width // LANES
        table = table_rows(table_ref, c * blocks, (c + 1) * blocks)
        for first in range(0, full, 2):
            here = min(2, full - first)
            got = nt(table, fields_ref[first * LANES : (first + here) * LANES, :])
            got = got.astype(jnp.bfloat16)
            for j in range(here):
                block = got[:, j * LANES : (j + 1) * LANES].reshape(some, width, LANES)
                block_ref[mine, (first + j) * width : (first + j + 1) * width, :] = block
        if count % per:
            last = fields_ref[full * LANES : count * depth, :]
            got = nt(table, jnp.concatenate([last, last], axis=0))
            got = got.reshape(some, width, LANES)
            half = width // 2
            lane = lax.broadcasted_iota(jnp.int32, (some, half, LANES), 2)
            block = jnp.where(lane < depth, got[:, :half, :], got[:, half:, :])
            at = full * width
            block_ref[mine, at : at + half, :] = block.astype(jnp.bfloat16)
        copies.append(pltpu.make_async_copy(block_ref.at[mine], out_ref.at[mine], sem.at[c]))
        copies[-1].start()
    for copy in copies:
        copy.wait()


def sorted_lines(recv_ref, t, start, count):
    low = lax.broadcasted_iota(jnp.int32, (count, LANES), 1) < LANES // 2
    even = recv_ref[2 * t, start : start + count, :].astype(jnp.float32)
    odd = recv_ref[2 * t + 1, start : start + count, :].astype(jnp.float32)
    one = jnp.where(low, even, pltpu.roll(odd, LANES // 2, 1))
    two = jnp.where(low, pltpu.roll(even, LANES // 2, 1), odd)
    return one, two


def place(lines_ref, at, t, rows):
    lines_ref[at : at + rows.shape[0], t * LANES : (t + 1) * LANES] = rows.astype(jnp.bfloat16)


def products_kernel(table_ref, velocity_ref, out_ref, fields_ref, block_ref, sem):
    depth = velocity_ref.shape[1]
    parts = [velocity_ref[a] for a in range(3)]
    for a in range(3):
        fields_ref[a * depth : (a + 1) * depth, :] = parts[a].astype(jnp.bfloat16)
    for p, (a, b) in enumerate(index_pairs):
        at = (3 + p) * depth
        fields_ref[at : at + depth, :] = (parts[a] * parts[b]).astype(jnp.bfloat16)
    send_blocks(table_ref, fields_ref, block_ref, out_ref, sem, 9, depth, True)


def strain(gradients):
    strain_parts = [0.5 * (gradients[b][a] + gradients[a][b]) for a, b in index_pairs]
    squares_sum = pair_weights[0] * strain_parts[0] * strain_parts[0]
    for weight, part_value in zip(pair_weights[1:], strain_parts[1:]):
        squares_sum = squares_sum + weight * part_value * part_value
    return (strain_parts, jnp.sqrt(2.0 * squares_sum))


def slopes(center, one, two, sense, first, last):
    rows, length = center.shape
    row = lax.broadcasted_iota(jnp.int32, center.shape, 0)
    along = (pltpu.roll(center, length - 1, 1) - pltpu.roll(center, 1, 1)) * 0.5
    following = jnp.where(row == rows - 1, last, pltpu.roll(center, rows - 1, 0))
    previous = jnp.where(row == 0, first, pltpu.roll(center, 1, 0))
    return (along, (two - one) * sense, (following - previous) * 0.5)


def strain_kernel(
    table_ref, velocity_ref, one_ref, two_ref, sense_ref, first_ref, last_ref, out_ref, magnitude_ref,
    fields_ref, block_ref, sem,
):
    depth = velocity_ref.shape[1]
    gradients = [
        slopes(velocity_ref[a], one_ref[a], two_ref[a], sense_ref[...], first_ref[a], last_ref[a])
        for a in range(3)
    ]
    strain_parts, magnitude = strain(gradients)
    magnitude_ref[...] = magnitude
    for p, part_value in enumerate(strain_parts):
        fields_ref[p * depth : (p + 1) * depth, :] = (magnitude * part_value).astype(jnp.bfloat16)
    send_blocks(table_ref, fields_ref, block_ref, out_ref, sem, 6, depth, False)


def smooth_kernel(table_ref, recv_ref, smooth_ref, edges_ref, lines_ref):
    senders = recv_ref.shape[0]
    _, width, length = smooth_ref.shape
    for t in range(senders // 2):
        one, two = sorted_lines(recv_ref, t, 0, width)
        place(lines_ref, 0, t, one)
        place(lines_ref, width, t, two)
        one, two = sorted_lines(recv_ref, t, width, width)
        place(lines_ref, 2 * width, t, one)
        one, two = sorted_lines(recv_ref, t, 9 * width // 2, 8)
        place(lines_ref, 3 * width, t, jnp.concatenate([one, two], axis=0))
    got = nt(lines_ref[...], table_of(table_ref[...])).astype(jnp.bfloat16)
    for a in range(3):
        smooth_ref[a] = got[a * width : (a + 1) * width, :]
    edges_ref[...] = got[3 * width :, :].astype(jnp.float32)


def squares_kernel(table_ref, recv_ref, squares_ref, lines_ref):
    senders = recv_ref.shape[0]
    _, width, length = squares_ref.shape
    half = width // 2
    for t in range(senders // 2):
        place(lines_ref, 0, t, sorted_lines(recv_ref, t, width, width)[1])
        for j in range(2):
            one, two = sorted_lines(recv_ref, t, (2 + j) * width, width)
            place(lines_ref, (1 + 2 * j) * width, t, one)
            place(lines_ref, (2 + 2 * j) * width, t, two)
        one, two = sorted_lines(recv_ref, t, 4 * width, half)
        place(lines_ref, 5 * width, t, one)
        place(lines_ref, 5 * width + half, t, two)
    got = nt(lines_ref[...], table_of(table_ref[...])).astype(jnp.bfloat16)
    for p in range(6):
        squares_ref[p] = got[p * width : (p + 1) * width, :]


def model_kernel(smooth_ref, one_ref, two_ref, sense_ref, edges_ref, model_ref):
    gradients = []
    for a, at in zip(range(3), (0, 8, 2)):
        center, one, two = (ref[a].astype(jnp.float32) for ref in (smooth_ref, one_ref, two_ref))
        first, last = edges_ref[at : at + 1, :], edges_ref[at + 1 : at + 2, :]
        along, across, between = slopes(center, one, two, sense_ref[...], first, last)
        gradients.append((between, across, along))
    strain_parts, magnitude = strain(gradients)
    for p, part_value in enumerate(strain_parts):
        model_ref[p] = 4.0 * magnitude * part_value


def sums_kernel(table_ref, recv_ref, smooth_ref, squares_ref, model_ref, out_ref, lines_ref):
    senders = recv_ref.shape[0]
    _, width, length = model_ref.shape
    for t in range(senders // 2):
        for j in range(3):
            one, two = sorted_lines(recv_ref, t, j * width, width)
            place(lines_ref, 2 * j * width, t, one)
            place(lines_ref, (2 * j + 1) * width, t, two)
    got = nt(lines_ref[...], table_of(table_ref[...])).astype(jnp.bfloat16)
    smooth = [smooth_ref[a].astype(jnp.float32) for a in range(3)]
    numerator = jnp.zeros((8, length), jnp.float32)
    denominator = jnp.zeros((8, length), jnp.float32)
    for p, (weight, (a, b)) in enumerate(zip(pair_weights, index_pairs)):
        leonard = squares_ref[p].astype(jnp.float32) - smooth[a] * smooth[b]
        model_term = got[p * width : (p + 1) * width, :].astype(jnp.float32) - model_ref[p]
        top = leonard * model_term
        bottom = model_term * model_term
        numerator = numerator + weight * top.reshape(width // 8, 8, length).sum(axis=0)
        denominator = denominator + weight * bottom.reshape(width // 8, 8, length).sum(axis=0)

    def lanes(x):
        total = x[:, :LANES]
        for at in range(LANES, length, LANES):
            total = total + x[:, at : at + LANES]
        total = total.sum(axis=0, keepdims=True)
        return total + pltpu.roll(total, LANES // 2, 1)

    low = lax.broadcasted_iota(jnp.int32, (1, LANES), 1) < LANES // 2
    pair = jnp.where(low, lanes(numerator), lanes(denominator))
    out_ref[...] = jnp.broadcast_to(pair, out_ref.shape)


def viscosity_kernel(cells, sums_ref, magnitude_ref, out_ref):
    total = sums_ref[...].sum(axis=0)
    low = lax.broadcasted_iota(jnp.int32, total.shape, 1) < LANES // 2
    numerator = jnp.sum(jnp.where(low, total, 0.0), axis=1, keepdims=True)
    denominator = jnp.sum(jnp.where(low, 0.0, total), axis=1, keepdims=True)
    coefficient = numerator / cells / (2.0 * (denominator / cells + epsilon))
    out_ref[...] = magnitude_ref[...] * coefficient


def body(velocity):
    _, _, depth, nx = velocity.shape
    parts = lax.axis_size("pz")
    rows = lax.axis_size("py")
    nz = depth * parts
    width = nx // parts
    f32, bf16 = jnp.float32, jnp.bfloat16
    table_x = filter_table(nx).T
    table_z = filter_table(nz)
    beside = np.zeros((2, 8, nx), bf16)
    for r in range(2):
        beside[r, :4] = table_x[[r * width - 1, (r + 1) * width] * 2]
    lanes_x = jnp.asarray(np.concatenate([table_x[:LANES], beside.reshape(16, nx)]))
    lanes_z = jnp.asarray(table_z[:BAND])
    outward, inward = [], []
    for i in range(rows - 1):
        for j in range(parts):
            pair = (i * parts + j, (i + 1) * parts + j)
            (inward if j % 2 else outward).append(pair)
            (outward if j % 2 else inward).append(pair[::-1])
    sense = (0.5 - (lax.axis_index("pz") % 2).astype(f32)).reshape(1, 1)
    around = [(i, (i + 1) % parts) for i in range(parts)]
    back = [(b, a) for a, b in around]
    velocity = velocity.reshape(3, depth, nx)
    vmem, dma = pltpu.VMEM, pltpu.SemaphoreType.DMA

    first = lax.ppermute(velocity[:, -1:], "pz", around)
    last = lax.ppermute(velocity[:, :1], "pz", back)
    send_shape = (parts, 9 * width // 2 + 8, LANES)
    send = call(
        products_kernel,
        jax.ShapeDtypeStruct(send_shape, bf16),
        2 * 9 * depth * nx * nx,
        12 * depth * nx + 2 * nx * nx,
        [vmem((9 * depth, nx), bf16), vmem(send_shape, bf16), dma((2,))],
        "products",
        (2,),
        58,
    )(lanes_x, velocity)
    send, first, last = lax.optimization_barrier((send, first, last))
    received = lax.all_to_all(send, "pz", 0, 0, tiled=True)

    one = lax.ppermute(velocity, ("py", "pz"), outward)
    two = lax.ppermute(velocity, ("py", "pz"), inward)
    strain_shape = (parts, 3 * width, LANES)
    send_strain, magnitude = call(
        strain_kernel,
        (jax.ShapeDtypeStruct(strain_shape, bf16), jax.ShapeDtypeStruct((depth, nx), f32)),
        2 * 6 * depth * nx * nx,
        36 * depth * nx + 2 * nx * nx,
        [vmem((6 * depth, nx), bf16), vmem(strain_shape, bf16), dma((2,))],
        "strain",
        (7,),
    )(lanes_x, velocity, one, two, sense, first, last)
    received_strain = lax.all_to_all(send_strain, "pz", 0, 0, tiled=True)

    smooth, edges = call(
        smooth_kernel,
        (
            jax.ShapeDtypeStruct((3, width, nz), bf16),
            jax.ShapeDtypeStruct((16, nz), f32),
        ),
        2 * 4 * width * nz * nz,
        2 * nz * nz,
        [vmem((3 * width + 16, nz), bf16)],
        "smooth",
    )(lanes_z, received)
    smooth_one = lax.ppermute(smooth, ("py", "pz"), outward)
    smooth_two = lax.ppermute(smooth, ("py", "pz"), inward)
    squares = call(
        squares_kernel,
        jax.ShapeDtypeStruct((6, width, nz), bf16),
        2 * 6 * width * nz * nz,
        24 * width * nz,
        [vmem((6 * width, nz), bf16)],
        "squares",
    )(lanes_z, received)
    model = call(
        model_kernel,
        jax.ShapeDtypeStruct((6, width, nz), f32),
        100 * width * nz,
        24 * width * nz,
        (),
        "model",
    )(smooth, smooth_one, smooth_two, sense, edges)
    sums = call(
        sums_kernel,
        jax.ShapeDtypeStruct((parts, 1, LANES), f32),
        2 * 6 * width * nz * nz,
        48 * width * nz,
        [vmem((6 * width, nz), bf16)],
        "sums",
    )(lanes_z, received_strain, smooth, squares, model)
    totals = lax.all_to_all(sums, "pz", 0, 0, tiled=True)
    cells = nx * nz
    nu_t = call(
        lambda *refs: viscosity_kernel(cells, *refs),
        jax.ShapeDtypeStruct((depth, nx), f32),
        2 * depth * nx,
        8 * depth * nx,
        (),
        "viscosity",
    )(totals, magnitude)
    filtered_velocity = jnp.transpose(smooth, (0, 2, 1))
    return (nu_t[None], filtered_velocity[:, None])


def solution(mesh):
    in_specs = (P(None, "py", "pz", None),)
    out_specs = (P("py", "pz", None), P(None, "py", None, "pz"))
    return jax.shard_map(body, mesh=mesh, in_specs=in_specs, out_specs=out_specs, check_vma=False)
```

```python
import math

import jax
import jax.numpy as jnp
import numpy as np
from jax import lax
from jax.experimental import pallas as pl
from jax.experimental.pallas import tpu as pltpu
from jax.sharding import PartitionSpec as P

index_pairs = ((0, 0), (1, 1), (2, 2), (0, 1), (0, 2), (1, 2))
pair_weights = (1.0, 1.0, 1.0, 2.0, 2.0, 2.0)
epsilon = 1e-06
LANES = 128
BAND = 8


def filter_table(length):
    offsets = np.arange(length, dtype=np.int64)
    wavenumbers = np.arange(1, length // 4, dtype=np.int64)
    phase = offsets[:, None] * wavenumbers[None, :] % length
    kernel = (1.0 + 2.0 * np.cos(phase * (2.0 * math.pi / length)).sum(axis=1)) / length
    kernel = kernel.astype(np.float32)
    lagged = (offsets[:, None] - offsets[None, :]) % length
    return kernel[lagged].astype(jnp.bfloat16)


def call(kernel, out_shape, flops, moved, scratch=(), name=None, far=(), room=24):
    outs = jax.tree.leaves(out_shape)

    def space(i):
        return pl.BlockSpec(memory_space=pltpu.HBM if i in far else pltpu.VMEM)

    def run(*args):
        out_specs = [space(len(args) + i) for i in range(len(outs))]
        return pl.pallas_call(
            kernel,
            out_shape=out_shape,
            in_specs=[space(i) for i in range(len(args))],
            out_specs=out_specs if isinstance(out_shape, tuple) else out_specs[0],
            scratch_shapes=list(scratch),
            cost_estimate=pl.CostEstimate(flops=flops, bytes_accessed=moved, transcendentals=0),
            compiler_params=pltpu.CompilerParams(vmem_limit_bytes=room * 1024 * 1024),
            name=name,
        )(*args)

    return run


def nt(a, b):
    return lax.dot_general(a, b, (((1,), (1,)), ((), ())), preferred_element_type=jnp.float32)


def turned(rows, blocks):
    at = rows.shape[1] - blocks * LANES
    return rows if blocks == 0 else jnp.concatenate([rows[:, at:], rows[:, :at]], axis=1)


def table_rows(band_ref, first, last):
    band = band_ref[:LANES, :]
    return jnp.concatenate([turned(band, a) for a in range(first, last)], axis=0)


def table_of(band):
    band = band.astype(jnp.float32)
    rows = [band] + [pltpu.roll(band, at, 1) for at in range(BAND, LANES, BAND)]
    tile = jnp.concatenate(rows, axis=0).astype(jnp.bfloat16)
    return jnp.concatenate([turned(tile, a) for a in range(band.shape[1] // LANES)], axis=0)


def send_blocks(table_ref, fields_ref, block_ref, out_ref, sem, count, depth, edges):
    receivers = block_ref.shape[0]
    width = fields_ref.shape[1] // receivers
    per = LANES // depth
    full = count // per
    if edges:
        seed = table_ref[LANES:, :]
        beside = [turned(seed, q) for q in range(receivers * width // LANES)]
        beside = jnp.concatenate(beside, axis=0)
        got = nt(beside, fields_ref[: 2 * per * depth, :])
        row = lax.broadcasted_iota(jnp.int32, (receivers * 8, LANES), 0) % 8
        got = jnp.where(row < 2, got[:, :LANES], got[:, LANES:]).reshape(receivers, 8, LANES)
        block_ref[:, count * width // per :, :] = got.astype(jnp.bfloat16)
    chunks = 2
    some = receivers // chunks
    copies = []
    for c in range(chunks):
        mine = slice(c * some, (c + 1) * some)
        blocks = some * width // LANES
        table = table_rows(table_ref, c * blocks, (c + 1) * blocks)
        for first in range(0, full, 2):
            here = min(2, full - first)
            got = nt(table, fields_ref[first * LANES : (first + here) * LANES, :])
            got = got.astype(jnp.bfloat16)
            for j in range(here):
                block = got[:, j * LANES : (j + 1) * LANES].reshape(some, width, LANES)
                block_ref[mine, (first + j) * width : (first + j + 1) * width, :] = block
        if count % per:
            last = fields_ref[full * LANES : count * depth, :]
            got = nt(table, jnp.concatenate([last, last], axis=0))
            got = got.reshape(some, width, LANES)
            half = width // 2
            lane = lax.broadcasted_iota(jnp.int32, (some, half, LANES), 2)
            block = jnp.where(lane < depth, got[:, :half, :], got[:, half:, :])
            at = full * width
            block_ref[mine, at : at + half, :] = block.astype(jnp.bfloat16)
        copies.append(pltpu.make_async_copy(block_ref.at[mine], out_ref.at[mine], sem.at[c]))
        copies[-1].start()
    for copy in copies:
        copy.wait()


def sorted_lines(recv_ref, t, start, count):
    low = lax.broadcasted_iota(jnp.int32, (count, LANES), 1) < LANES // 2
    even = recv_ref[2 * t, start : start + count, :].astype(jnp.float32)
    odd = recv_ref[2 * t + 1, start : start + count, :].astype(jnp.float32)
    one = jnp.where(low, even, pltpu.roll(odd, LANES // 2, 1))
    two = jnp.where(low, pltpu.roll(even, LANES // 2, 1), odd)
    return one, two


def place(lines_ref, at, t, rows):
    lines_ref[at : at + rows.shape[0], t * LANES : (t + 1) * LANES] = rows.astype(jnp.bfloat16)


def products_kernel(table_ref, velocity_ref, out_ref, fields_ref, block_ref, sem):
    depth = velocity_ref.shape[1]
    parts = [velocity_ref[a] for a in range(3)]
    for a in range(3):
        fields_ref[a * depth : (a + 1) * depth, :] = parts[a].astype(jnp.bfloat16)
    for p, (a, b) in enumerate(index_pairs):
        at = (3 + p) * depth
        fields_ref[at : at + depth, :] = (parts[a] * parts[b]).astype(jnp.bfloat16)
    send_blocks(table_ref, fields_ref, block_ref, out_ref, sem, 9, depth, True)


def strain(gradients):
    strain_parts = [0.5 * (gradients[b][a] + gradients[a][b]) for a, b in index_pairs]
    squares_sum = pair_weights[0] * strain_parts[0] * strain_parts[0]
    for weight, part_value in zip(pair_weights[1:], strain_parts[1:]):
        squares_sum = squares_sum + weight * part_value * part_value
    return (strain_parts, jnp.sqrt(2.0 * squares_sum))


def slopes(center, one, two, sense, first, last):
    rows, length = center.shape
    row = lax.broadcasted_iota(jnp.int32, center.shape, 0)
    along = (pltpu.roll(center, length - 1, 1) - pltpu.roll(center, 1, 1)) * 0.5
    following = jnp.where(row == rows - 1, last, pltpu.roll(center, rows - 1, 0))
    previous = jnp.where(row == 0, first, pltpu.roll(center, 1, 0))
    return (along, (two - one) * sense, (following - previous) * 0.5)


def strain_kernel(
    table_ref, velocity_ref, one_ref, two_ref, sense_ref, first_ref, last_ref, out_ref, magnitude_ref,
    fields_ref, block_ref, sem,
):
    depth = velocity_ref.shape[1]
    gradients = [
        slopes(velocity_ref[a], one_ref[a], two_ref[a], sense_ref[...], first_ref[a], last_ref[a])
        for a in range(3)
    ]
    strain_parts, magnitude = strain(gradients)
    magnitude_ref[...] = magnitude
    for p, part_value in enumerate(strain_parts):
        fields_ref[p * depth : (p + 1) * depth, :] = (magnitude * part_value).astype(jnp.bfloat16)
    send_blocks(table_ref, fields_ref, block_ref, out_ref, sem, 6, depth, False)


def smooth_kernel(table_ref, recv_ref, smooth_ref, edges_ref, band_ref, lines_ref):
    senders = recv_ref.shape[0]
    _, width, length = smooth_ref.shape
    for t in range(senders // 2):
        one, two = sorted_lines(recv_ref, t, 0, width)
        place(lines_ref, 0, t, one)
        place(lines_ref, width, t, two)
        one, two = sorted_lines(recv_ref, t, width, width)
        place(lines_ref, 2 * width, t, one)
        one, two = sorted_lines(recv_ref, t, 9 * width // 2, 8)
        place(lines_ref, 3 * width, t, jnp.concatenate([one, two], axis=0))
    got = nt(lines_ref[...], table_of(table_ref[...])).astype(jnp.bfloat16)
    for a in range(3):
        smooth_ref[a] = got[a * width : (a + 1) * width, :]
    edges_ref[...] = got[3 * width :, :].astype(jnp.float32)
    band_ref[...] = table_ref[...]


def squares_kernel(table_ref, recv_ref, squares_ref, lines_ref):
    senders = recv_ref.shape[0]
    _, width, length = squares_ref.shape
    half = width // 2
    for t in range(senders // 2):
        place(lines_ref, 0, t, sorted_lines(recv_ref, t, width, width)[1])
        for j in range(2):
            one, two = sorted_lines(recv_ref, t, (2 + j) * width, width)
            place(lines_ref, (1 + 2 * j) * width, t, one)
            place(lines_ref, (2 + 2 * j) * width, t, two)
        one, two = sorted_lines(recv_ref, t, 4 * width, half)
        place(lines_ref, 5 * width, t, one)
        place(lines_ref, 5 * width + half, t, two)
    got = nt(lines_ref[...], table_of(table_ref[...])).astype(jnp.bfloat16)
    for p in range(6):
        squares_ref[p] = got[p * width : (p + 1) * width, :]


def model_kernel(smooth_ref, one_ref, two_ref, sense_ref, edges_ref, model_ref):
    gradients = []
    for a, at in zip(range(3), (0, 8, 2)):
        center, one, two = (ref[a].astype(jnp.float32) for ref in (smooth_ref, one_ref, two_ref))
        first, last = edges_ref[at : at + 1, :], edges_ref[at + 1 : at + 2, :]
        along, across, between = slopes(center, one, two, sense_ref[...], first, last)
        gradients.append((between, across, along))
    strain_parts, magnitude = strain(gradients)
    for p, part_value in enumerate(strain_parts):
        model_ref[p] = 4.0 * magnitude * part_value


def sums_kernel(table_ref, recv_ref, smooth_ref, squares_ref, model_ref, out_ref, lines_ref):
    senders = recv_ref.shape[0]
    _, width, length = model_ref.shape
    for t in range(senders // 2):
        for j in range(3):
            one, two = sorted_lines(recv_ref, t, j * width, width)
            place(lines_ref, 2 * j * width, t, one)
            place(lines_ref, (2 * j + 1) * width, t, two)
    got = nt(lines_ref[...], table_of(table_ref[...])).astype(jnp.bfloat16)
    smooth = [smooth_ref[a].astype(jnp.float32) for a in range(3)]
    numerator = jnp.zeros((8, length), jnp.float32)
    denominator = jnp.zeros((8, length), jnp.float32)
    for p, (weight, (a, b)) in enumerate(zip(pair_weights, index_pairs)):
        leonard = squares_ref[p].astype(jnp.float32) - smooth[a] * smooth[b]
        model_term = got[p * width : (p + 1) * width, :].astype(jnp.float32) - model_ref[p]
        top = leonard * model_term
        bottom = model_term * model_term
        numerator = numerator + weight * top.reshape(width // 8, 8, length).sum(axis=0)
        denominator = denominator + weight * bottom.reshape(width // 8, 8, length).sum(axis=0)

    def lanes(x):
        total = x[:, :LANES]
        for at in range(LANES, length, LANES):
            total = total + x[:, at : at + LANES]
        total = total.sum(axis=0, keepdims=True)
        return total + pltpu.roll(total, LANES // 2, 1)

    low = lax.broadcasted_iota(jnp.int32, (1, LANES), 1) < LANES // 2
    pair = jnp.where(low, lanes(numerator), lanes(denominator))
    out_ref[...] = jnp.broadcast_to(pair, out_ref.shape)


def viscosity_kernel(cells, sums_ref, magnitude_ref, out_ref):
    total = sums_ref[...].sum(axis=0)
    low = lax.broadcasted_iota(jnp.int32, total.shape, 1) < LANES // 2
    numerator = jnp.sum(jnp.where(low, total, 0.0), axis=1, keepdims=True)
    denominator = jnp.sum(jnp.where(low, 0.0, total), axis=1, keepdims=True)
    coefficient = numerator / cells / (2.0 * (denominator / cells + epsilon))
    out_ref[...] = magnitude_ref[...] * coefficient


def body(velocity):
    _, _, depth, nx = velocity.shape
    parts = lax.axis_size("pz")
    rows = lax.axis_size("py")
    nz = depth * parts
    width = nx // parts
    f32, bf16 = jnp.float32, jnp.bfloat16
    table_x = filter_table(nx).T
    table_z = filter_table(nz)
    beside = np.zeros((2, 8, nx), bf16)
    for r in range(2):
        beside[r, :4] = table_x[[r * width - 1, (r + 1) * width] * 2]
    lanes_x = jnp.asarray(np.concatenate([table_x[:LANES], beside.reshape(16, nx)]))
    lanes_z = jnp.asarray(table_z[:BAND])
    outward, inward = [], []
    for i in range(rows - 1):
        for j in range(parts):
            pair = (i * parts + j, (i + 1) * parts + j)
            (inward if j % 2 else outward).append(pair)
            (outward if j % 2 else inward).append(pair[::-1])
    sense = (0.5 - (lax.axis_index("pz") % 2).astype(f32)).reshape(1, 1)
    around = [(i, (i + 1) % parts) for i in range(parts)]
    back = [(b, a) for a, b in around]
    velocity = velocity.reshape(3, depth, nx)
    vmem, dma = pltpu.VMEM, pltpu.SemaphoreType.DMA

    first = lax.ppermute(velocity[:, -1:], "pz", around)
    last = lax.ppermute(velocity[:, :1], "pz", back)
    send_shape = (parts, 9 * width // 2 + 8, LANES)
    send = call(
        products_kernel,
        jax.ShapeDtypeStruct(send_shape, bf16),
        2 * 9 * depth * nx * nx,
        12 * depth * nx + 2 * nx * nx,
        [vmem((9 * depth, nx), bf16), vmem(send_shape, bf16), dma((2,))],
        "products",
        (2,),
        58,
    )(lanes_x, velocity)
    send, first, last = lax.optimization_barrier((send, first, last))
    received = lax.all_to_all(send, "pz", 0, 0, tiled=True)

    one = lax.ppermute(velocity, ("py", "pz"), outward)
    two = lax.ppermute(velocity, ("py", "pz"), inward)
    strain_shape = (parts, 3 * width, LANES)
    send_strain, magnitude = call(
        strain_kernel,
        (jax.ShapeDtypeStruct(strain_shape, bf16), jax.ShapeDtypeStruct((depth, nx), f32)),
        2 * 6 * depth * nx * nx,
        36 * depth * nx + 2 * nx * nx,
        [vmem((6 * depth, nx), bf16), vmem(strain_shape, bf16), dma((2,))],
        "strain",
        (7,),
    )(lanes_x, velocity, one, two, sense, first, last)
    received_strain = lax.all_to_all(send_strain, "pz", 0, 0, tiled=True)

    smooth, edges, band = call(
        smooth_kernel,
        (
            jax.ShapeDtypeStruct((3, width, nz), bf16),
            jax.ShapeDtypeStruct((16, nz), f32),
            jax.ShapeDtypeStruct((BAND, nz), bf16),
        ),
        2 * 4 * width * nz * nz,
        2 * nz * nz,
        [vmem((3 * width + 16, nz), bf16)],
        "smooth",
    )(lanes_z, received)
    smooth_one = lax.ppermute(smooth, ("py", "pz"), outward)
    smooth_two = lax.ppermute(smooth, ("py", "pz"), inward)
    squares = call(
        squares_kernel,
        jax.ShapeDtypeStruct((6, width, nz), bf16),
        2 * 6 * width * nz * nz,
        24 * width * nz,
        [vmem((6 * width, nz), bf16)],
        "squares",
    )(lanes_z, received)
    model = call(
        model_kernel,
        jax.ShapeDtypeStruct((6, width, nz), f32),
        100 * width * nz,
        24 * width * nz,
        (),
        "model",
    )(smooth, smooth_one, smooth_two, sense, edges)
    sums = call(
        sums_kernel,
        jax.ShapeDtypeStruct((parts, 1, LANES), f32),
        2 * 6 * width * nz * nz,
        48 * width * nz,
        [vmem((6 * width, nz), bf16)],
        "sums",
    )(band, received_strain, smooth, squares, model)
    totals = lax.all_to_all(sums, "pz", 0, 0, tiled=True)
    cells = nx * nz
    nu_t = call(
        lambda *refs: viscosity_kernel(cells, *refs),
        jax.ShapeDtypeStruct((depth, nx), f32),
        2 * depth * nx,
        8 * depth * nx,
        (),
        "viscosity",
    )(totals, magnitude)
    filtered_velocity = jnp.transpose(smooth, (0, 2, 1))
    return (nu_t[None], filtered_velocity[:, None])


def solution(mesh):
    in_specs = (P(None, "py", "pz", None),)
    out_specs = (P("py", "pz", None), P(None, "py", None, "pz"))
    return jax.shard_map(body, mesh=mesh, in_specs=in_specs, out_specs=out_specs, check_vma=False)
```

```python
import math

import jax
import jax.numpy as jnp
import numpy as np
from jax import lax
from jax.experimental import pallas as pl
from jax.experimental.pallas import tpu as pltpu
from jax.sharding import PartitionSpec as P

index_pairs = ((0, 0), (1, 1), (2, 2), (0, 1), (0, 2), (1, 2))
pair_weights = (1.0, 1.0, 1.0, 2.0, 2.0, 2.0)
epsilon = 1e-06
LANES = 128
BAND = 8


def filter_table(length):
    offsets = np.arange(length, dtype=np.int64)
    wavenumbers = np.arange(1, length // 4, dtype=np.int64)
    phase = offsets[:, None] * wavenumbers[None, :] % length
    kernel = (1.0 + 2.0 * np.cos(phase * (2.0 * math.pi / length)).sum(axis=1)) / length
    kernel = kernel.astype(np.float32)
    lagged = (offsets[:, None] - offsets[None, :]) % length
    return kernel[lagged].astype(jnp.bfloat16)


def call(kernel, out_shape, flops, moved, scratch=(), name=None, far=(), room=24):
    outs = jax.tree.leaves(out_shape)

    def space(i):
        return pl.BlockSpec(memory_space=pltpu.HBM if i in far else pltpu.VMEM)

    def run(*args):
        out_specs = [space(len(args) + i) for i in range(len(outs))]
        return pl.pallas_call(
            kernel,
            out_shape=out_shape,
            in_specs=[space(i) for i in range(len(args))],
            out_specs=out_specs if isinstance(out_shape, tuple) else out_specs[0],
            scratch_shapes=list(scratch),
            cost_estimate=pl.CostEstimate(flops=flops, bytes_accessed=moved, transcendentals=0),
            compiler_params=pltpu.CompilerParams(vmem_limit_bytes=room * 1024 * 1024),
            name=name,
        )(*args)

    return run


def nt(a, b):
    return lax.dot_general(a, b, (((1,), (1,)), ((), ())), preferred_element_type=jnp.float32)


def turned(rows, blocks):
    at = rows.shape[1] - blocks * LANES
    return rows if blocks == 0 else jnp.concatenate([rows[:, at:], rows[:, :at]], axis=1)


def tile_of(band):
    band = band.astype(jnp.float32)
    rows = [band] + [pltpu.roll(band, at, 1) for at in range(BAND, LANES, BAND)]
    return jnp.concatenate(rows, axis=0).astype(jnp.bfloat16)


def table_rows(tile, first, last):
    return jnp.concatenate([turned(tile, a) for a in range(first, last)], axis=0)


def table_of(band):
    tile = tile_of(band)
    return table_rows(tile, 0, tile.shape[1] // LANES)


def send_blocks(tile, seed, fields_ref, block_ref, out_ref, sem, count, depth):
    receivers = block_ref.shape[0]
    width = fields_ref.shape[1] // receivers
    per = LANES // depth
    full = count // per
    if seed is not None:
        beside = [turned(seed, q) for q in range(receivers * width // LANES)]
        beside = jnp.concatenate(beside, axis=0)
        got = nt(beside, fields_ref[: 2 * per * depth, :])
        row = lax.broadcasted_iota(jnp.int32, (receivers * 8, LANES), 0) % 8
        got = jnp.where(row < 2, got[:, :LANES], got[:, LANES:]).reshape(receivers, 8, LANES)
        block_ref[:, count * width // per :, :] = got.astype(jnp.bfloat16)
    chunks = sem.shape[0]
    some = receivers // chunks
    copies = []
    for c in range(chunks):
        mine = slice(c * some, (c + 1) * some)
        blocks = some * width // LANES
        table = table_rows(tile, c * blocks, (c + 1) * blocks)
        for first in range(0, full, 2):
            here = min(2, full - first)
            got = nt(table, fields_ref[first * LANES : (first + here) * LANES, :])
            got = got.astype(jnp.bfloat16)
            for j in range(here):
                block = got[:, j * LANES : (j + 1) * LANES].reshape(some, width, LANES)
                block_ref[mine, (first + j) * width : (first + j + 1) * width, :] = block
        if count % per:
            last = fields_ref[full * LANES : count * depth, :]
            got = nt(table, jnp.concatenate([last, last], axis=0))
            got = got.reshape(some, width, LANES)
            half = width // 2
            lane = lax.broadcasted_iota(jnp.int32, (some, half, LANES), 2)
            block = jnp.where(lane < depth, got[:, :half, :], got[:, half:, :])
            at = full * width
            block_ref[mine, at : at + half, :] = block.astype(jnp.bfloat16)
        copies.append(pltpu.make_async_copy(block_ref.at[mine], out_ref.at[mine], sem.at[c]))
        copies[-1].start()
    for copy in copies:
        copy.wait()


def sorted_lines(recv_ref, t, start, count):
    low = lax.broadcasted_iota(jnp.int32, (count, LANES), 1) < LANES // 2
    even = recv_ref[2 * t, start : start + count, :].astype(jnp.float32)
    odd = recv_ref[2 * t + 1, start : start + count, :].astype(jnp.float32)
    one = jnp.where(low, even, pltpu.roll(odd, LANES // 2, 1))
    two = jnp.where(low, pltpu.roll(even, LANES // 2, 1), odd)
    return one, two


def place(lines_ref, at, t, rows):
    lines_ref[at : at + rows.shape[0], t * LANES : (t + 1) * LANES] = rows.astype(jnp.bfloat16)


def products_kernel(table_ref, velocity_ref, out_ref, fields_ref, block_ref, sem):
    depth = velocity_ref.shape[1]
    parts = [velocity_ref[a] for a in range(3)]
    for a in range(3):
        fields_ref[a * depth : (a + 1) * depth, :] = parts[a].astype(jnp.bfloat16)
    for p, (a, b) in enumerate(index_pairs):
        at = (3 + p) * depth
        fields_ref[at : at + depth, :] = (parts[a] * parts[b]).astype(jnp.bfloat16)
    tile, seed = table_ref[:LANES, :], table_ref[LANES:, :]
    send_blocks(tile, seed, fields_ref, block_ref, out_ref, sem, 9, depth)


def strain(gradients):
    strain_parts = [0.5 * (gradients[b][a] + gradients[a][b]) for a, b in index_pairs]
    squares_sum = pair_weights[0] * strain_parts[0] * strain_parts[0]
    for weight, part_value in zip(pair_weights[1:], strain_parts[1:]):
        squares_sum = squares_sum + weight * part_value * part_value
    return (strain_parts, jnp.sqrt(2.0 * squares_sum))


def slopes(center, one, two, sense, first, last):
    rows, length = center.shape
    row = lax.broadcasted_iota(jnp.int32, center.shape, 0)
    along = (pltpu.roll(center, length - 1, 1) - pltpu.roll(center, 1, 1)) * 0.5
    following = jnp.where(row == rows - 1, last, pltpu.roll(center, rows - 1, 0))
    previous = jnp.where(row == 0, first, pltpu.roll(center, 1, 0))
    return (along, (two - one) * sense, (following - previous) * 0.5)


def strain_kernel(
    table_ref, velocity_ref, one_ref, two_ref, sense_ref, first_ref, last_ref, out_ref, magnitude_ref,
    fields_ref, block_ref, sem,
):
    depth = velocity_ref.shape[1]
    gradients = [
        slopes(velocity_ref[a], one_ref[a], two_ref[a], sense_ref[...], first_ref[a], last_ref[a])
        for a in range(3)
    ]
    strain_parts, magnitude = strain(gradients)
    magnitude_ref[...] = magnitude
    for p, part_value in enumerate(strain_parts):
        fields_ref[p * depth : (p + 1) * depth, :] = (magnitude * part_value).astype(jnp.bfloat16)
    tile = tile_of(table_ref[...])
    send_blocks(tile, None, fields_ref, block_ref, out_ref, sem, 6, depth)


def smooth_kernel(table_ref, recv_ref, smooth_ref, edges_ref, band_ref, lines_ref):
    senders = recv_ref.shape[0]
    _, width, length = smooth_ref.shape
    for t in range(senders // 2):
        one, two = sorted_lines(recv_ref, t, 0, width)
        place(lines_ref, 0, t, one)
        place(lines_ref, width, t, two)
        one, two = sorted_lines(recv_ref, t, width, width)
        place(lines_ref, 2 * width, t, one)
        one, two = sorted_lines(recv_ref, t, 9 * width // 2, 8)
        place(lines_ref, 3 * width, t, jnp.concatenate([one, two], axis=0))
    got = nt(lines_ref[...], table_of(table_ref[...])).astype(jnp.bfloat16)
    for a in range(3):
        smooth_ref[a] = got[a * width : (a + 1) * width, :]
    edges_ref[...] = got[3 * width :, :].astype(jnp.float32)
    band_ref[...] = table_ref[...]


def squares_kernel(table_ref, recv_ref, squares_ref, lines_ref):
    senders = recv_ref.shape[0]
    _, width, length = squares_ref.shape
    half = width // 2
    for t in range(senders // 2):
        place(lines_ref, 0, t, sorted_lines(recv_ref, t, width, width)[1])
        for j in range(2):
            one, two = sorted_lines(recv_ref, t, (2 + j) * width, width)
            place(lines_ref, (1 + 2 * j) * width, t, one)
            place(lines_ref, (2 + 2 * j) * width, t, two)
        one, two = sorted_lines(recv_ref, t, 4 * width, half)
        place(lines_ref, 5 * width, t, one)
        place(lines_ref, 5 * width + half, t, two)
    got = nt(lines_ref[...], table_of(table_ref[...])).astype(jnp.bfloat16)
    for p in range(6):
        squares_ref[p] = got[p * width : (p + 1) * width, :]


def model_kernel(smooth_ref, one_ref, two_ref, sense_ref, edges_ref, model_ref):
    gradients = []
    for a, at in zip(range(3), (0, 8, 2)):
        center, one, two = (ref[a].astype(jnp.float32) for ref in (smooth_ref, one_ref, two_ref))
        first, last = edges_ref[at : at + 1, :], edges_ref[at + 1 : at + 2, :]
        along, across, between = slopes(center, one, two, sense_ref[...], first, last)
        gradients.append((between, across, along))
    strain_parts, magnitude = strain(gradients)
    for p, part_value in enumerate(strain_parts):
        model_ref[p] = 4.0 * magnitude * part_value


def sums_kernel(table_ref, recv_ref, smooth_ref, squares_ref, model_ref, out_ref, lines_ref):
    senders = recv_ref.shape[0]
    _, width, length = model_ref.shape
    for t in range(senders // 2):
        for j in range(3):
            one, two = sorted_lines(recv_ref, t, j * width, width)
            place(lines_ref, 2 * j * width, t, one)
            place(lines_ref, (2 * j + 1) * width, t, two)
    got = nt(lines_ref[...], table_of(table_ref[...])).astype(jnp.bfloat16)
    smooth = [smooth_ref[a].astype(jnp.float32) for a in range(3)]
    numerator = jnp.zeros((8, length), jnp.float32)
    denominator = jnp.zeros((8, length), jnp.float32)
    for p, (weight, (a, b)) in enumerate(zip(pair_weights, index_pairs)):
        leonard = squares_ref[p].astype(jnp.float32) - smooth[a] * smooth[b]
        model_term = got[p * width : (p + 1) * width, :].astype(jnp.float32) - model_ref[p]
        top = leonard * model_term
        bottom = model_term * model_term
        numerator = numerator + weight * top.reshape(width // 8, 8, length).sum(axis=0)
        denominator = denominator + weight * bottom.reshape(width // 8, 8, length).sum(axis=0)

    def lanes(x):
        total = x[:, :LANES]
        for at in range(LANES, length, LANES):
            total = total + x[:, at : at + LANES]
        total = total.sum(axis=0, keepdims=True)
        return total + pltpu.roll(total, LANES // 2, 1)

    low = lax.broadcasted_iota(jnp.int32, (1, LANES), 1) < LANES // 2
    pair = jnp.where(low, lanes(numerator), lanes(denominator))
    out_ref[...] = jnp.broadcast_to(pair, out_ref.shape)


def viscosity_kernel(cells, sums_ref, magnitude_ref, out_ref):
    total = sums_ref[...].sum(axis=0)
    low = lax.broadcasted_iota(jnp.int32, total.shape, 1) < LANES // 2
    numerator = jnp.sum(jnp.where(low, total, 0.0), axis=1, keepdims=True)
    denominator = jnp.sum(jnp.where(low, 0.0, total), axis=1, keepdims=True)
    coefficient = numerator / cells / (2.0 * (denominator / cells + epsilon))
    out_ref[...] = magnitude_ref[...] * coefficient


def body(velocity):
    _, _, depth, nx = velocity.shape
    parts = lax.axis_size("pz")
    rows = lax.axis_size("py")
    nz = depth * parts
    width = nx // parts
    f32, bf16 = jnp.float32, jnp.bfloat16
    table_x = filter_table(nx).T
    table_z = filter_table(nz)
    beside = np.zeros((2, 8, nx), bf16)
    for r in range(2):
        beside[r, :4] = table_x[[r * width - 1, (r + 1) * width] * 2]
    lanes_x = jnp.asarray(np.concatenate([table_x[:LANES], beside.reshape(16, nx)]))
    short_x = jnp.asarray(table_x[:BAND])
    same = np.array_equal(table_x[:BAND], table_z[:BAND])
    lanes_z = short_x if same else jnp.asarray(table_z[:BAND])
    outward, inward = [], []
    for i in range(rows - 1):
        for j in range(parts):
            pair = (i * parts + j, (i + 1) * parts + j)
            (inward if j % 2 else outward).append(pair)
            (outward if j % 2 else inward).append(pair[::-1])
    sense = (0.5 - (lax.axis_index("pz") % 2).astype(f32)).reshape(1, 1)
    around = [(i, (i + 1) % parts) for i in range(parts)]
    back = [(b, a) for a, b in around]
    velocity = velocity.reshape(3, depth, nx)
    vmem, dma = pltpu.VMEM, pltpu.SemaphoreType.DMA

    last = lax.ppermute(velocity[:, :1], "pz", back)
    first = lax.ppermute(velocity[:, -1:], "pz", around)
    send_shape = (parts, 9 * width // 2 + 8, LANES)
    send = call(
        products_kernel,
        jax.ShapeDtypeStruct(send_shape, bf16),
        2 * 9 * depth * nx * nx,
        12 * depth * nx + 2 * nx * nx,
        [vmem((9 * depth, nx), bf16), vmem(send_shape, bf16), dma((4,))],
        "products",
        (2,),
        58,
    )(lanes_x, velocity)
    send, last, first = lax.optimization_barrier((send, last, first))
    received = lax.all_to_all(send, "pz", 0, 0, tiled=True)

    one = lax.ppermute(velocity, ("py", "pz"), outward)
    two = lax.ppermute(velocity, ("py", "pz"), inward)
    strain_shape = (parts, 3 * width, LANES)
    send_strain, magnitude = call(
        strain_kernel,
        (jax.ShapeDtypeStruct(strain_shape, bf16), jax.ShapeDtypeStruct((depth, nx), f32)),
        2 * 6 * depth * nx * nx,
        36 * depth * nx + 2 * nx * nx,
        [vmem((6 * depth, nx), bf16), vmem(strain_shape, bf16), dma((2,))],
        "strain",
        (7,),
    )(short_x, velocity, one, two, sense, first, last)
    received_strain = lax.all_to_all(send_strain, "pz", 0, 0, tiled=True)

    smooth, edges, band = call(
        smooth_kernel,
        (
            jax.ShapeDtypeStruct((3, width, nz), bf16),
            jax.ShapeDtypeStruct((16, nz), f32),
            jax.ShapeDtypeStruct((BAND, nz), bf16),
        ),
        2 * 4 * width * nz * nz,
        2 * nz * nz,
        [vmem((3 * width + 16, nz), bf16)],
        "smooth",
    )(lanes_z, received)
    smooth_one = lax.ppermute(smooth, ("py", "pz"), outward)
    smooth_two = lax.ppermute(smooth, ("py", "pz"), inward)
    squares = call(
        squares_kernel,
        jax.ShapeDtypeStruct((6, width, nz), bf16),
        2 * 6 * width * nz * nz,
        24 * width * nz,
        [vmem((6 * width, nz), bf16)],
        "squares",
    )(lanes_z, received)
    model = call(
        model_kernel,
        jax.ShapeDtypeStruct((6, width, nz), f32),
        100 * width * nz,
        24 * width * nz,
        (),
        "model",
    )(smooth, smooth_one, smooth_two, sense, edges)
    sums = call(
        sums_kernel,
        jax.ShapeDtypeStruct((parts, 1, LANES), f32),
        2 * 6 * width * nz * nz,
        48 * width * nz,
        [vmem((6 * width, nz), bf16)],
        "sums",
    )(band, received_strain, smooth, squares, model)
    totals = lax.all_to_all(sums, "pz", 0, 0, tiled=True)
    cells = nx * nz
    nu_t = call(
        lambda *refs: viscosity_kernel(cells, *refs),
        jax.ShapeDtypeStruct((depth, nx), f32),
        2 * depth * nx,
        8 * depth * nx,
        (),
        "viscosity",
    )(totals, magnitude)
    filtered_velocity = jnp.transpose(smooth, (0, 2, 1))
    return (nu_t[None], filtered_velocity[:, None])


def solution(mesh):
    in_specs = (P(None, "py", "pz", None),)
    out_specs = (P("py", "pz", None), P(None, "py", None, "pz"))
    return jax.shard_map(body, mesh=mesh, in_specs=in_specs, out_specs=out_specs, check_vma=False)
```

```python
import math

import jax
import jax.numpy as jnp
import numpy as np
from jax import lax
from jax.experimental import pallas as pl
from jax.experimental.pallas import tpu as pltpu
from jax.sharding import PartitionSpec as P

index_pairs = ((0, 0), (1, 1), (2, 2), (0, 1), (0, 2), (1, 2))
pair_weights = (1.0, 1.0, 1.0, 2.0, 2.0, 2.0)
epsilon = 1e-06
LANES = 128
BAND = 8


def filter_table(length):
    offsets = np.arange(length, dtype=np.int64)
    wavenumbers = np.arange(1, length // 4, dtype=np.int64)
    phase = offsets[:, None] * wavenumbers[None, :] % length
    kernel = (1.0 + 2.0 * np.cos(phase * (2.0 * math.pi / length)).sum(axis=1)) / length
    kernel = kernel.astype(np.float32)
    lagged = (offsets[:, None] - offsets[None, :]) % length
    return kernel[lagged].astype(jnp.bfloat16)


def call(kernel, out_shape, flops, moved, scratch=(), name=None, far=(), room=24):
    outs = jax.tree.leaves(out_shape)

    def space(i):
        return pl.BlockSpec(memory_space=pltpu.HBM if i in far else pltpu.VMEM)

    def run(*args):
        out_specs = [space(len(args) + i) for i in range(len(outs))]
        return pl.pallas_call(
            kernel,
            out_shape=out_shape,
            in_specs=[space(i) for i in range(len(args))],
            out_specs=out_specs if isinstance(out_shape, tuple) else out_specs[0],
            scratch_shapes=list(scratch),
            cost_estimate=pl.CostEstimate(flops=flops, bytes_accessed=moved, transcendentals=0),
            compiler_params=pltpu.CompilerParams(vmem_limit_bytes=room * 1024 * 1024),
            name=name,
        )(*args)

    return run


def nt(a, b):
    return lax.dot_general(a, b, (((1,), (1,)), ((), ())), preferred_element_type=jnp.float32)


def turned(rows, blocks):
    at = rows.shape[1] - blocks * LANES
    return rows if blocks == 0 else jnp.concatenate([rows[:, at:], rows[:, :at]], axis=1)


def tile_of(band):
    band = band.astype(jnp.float32)
    rows = [band] + [pltpu.roll(band, at, 1) for at in range(BAND, LANES, BAND)]
    return jnp.concatenate(rows, axis=0).astype(jnp.bfloat16)


def table_rows(tile, first, last):
    return jnp.concatenate([turned(tile, a) for a in range(first, last)], axis=0)


def table_of(band):
    tile = tile_of(band)
    return table_rows(tile, 0, tile.shape[1] // LANES)


def send_blocks(tile, seed, fields_ref, block_ref, out_ref, sem, count, depth):
    receivers = block_ref.shape[0]
    width = fields_ref.shape[1] // receivers
    per = LANES // depth
    full = count // per
    if seed is not None:
        beside = [turned(seed, q) for q in range(receivers * width // LANES)]
        beside = jnp.concatenate(beside, axis=0)
        got = nt(beside, fields_ref[: 2 * per * depth, :])
        row = lax.broadcasted_iota(jnp.int32, (receivers * 8, LANES), 0) % 8
        got = jnp.where(row < 2, got[:, :LANES], got[:, LANES:]).reshape(receivers, 8, LANES)
        block_ref[:, count * width // per :, :] = got.astype(jnp.bfloat16)
    chunks = sem.shape[0]
    some = receivers // chunks
    copies = []
    for c in range(chunks):
        mine = slice(c * some, (c + 1) * some)
        blocks = some * width // LANES
        table = table_rows(tile, c * blocks, (c + 1) * blocks)
        for first in range(0, full, 2):
            here = min(2, full - first)
            got = nt(table, fields_ref[first * LANES : (first + here) * LANES, :])
            got = got.astype(jnp.bfloat16)
            for j in range(here):
                block = got[:, j * LANES : (j + 1) * LANES].reshape(some, width, LANES)
                block_ref[mine, (first + j) * width : (first + j + 1) * width, :] = block
        if count % per:
            last = fields_ref[full * LANES : count * depth, :]
            got = nt(table, jnp.concatenate([last, last], axis=0))
            got = got.reshape(some, width, LANES)
            half = width // 2
            lane = lax.broadcasted_iota(jnp.int32, (some, half, LANES), 2)
            block = jnp.where(lane < depth, got[:, :half, :], got[:, half:, :])
            at = full * width
            block_ref[mine, at : at + half, :] = block.astype(jnp.bfloat16)
        copies.append(pltpu.make_async_copy(block_ref.at[mine], out_ref.at[mine], sem.at[c]))
        copies[-1].start()
    for copy in copies:
        copy.wait()


def sorted_lines(recv_ref, t, start, count):
    low = lax.broadcasted_iota(jnp.int32, (count, LANES), 1) < LANES // 2
    even = recv_ref[2 * t, start : start + count, :].astype(jnp.float32)
    odd = recv_ref[2 * t + 1, start : start + count, :].astype(jnp.float32)
    one = jnp.where(low, even, pltpu.roll(odd, LANES // 2, 1))
    two = jnp.where(low, pltpu.roll(even, LANES // 2, 1), odd)
    return one, two


def place(lines_ref, at, t, rows):
    lines_ref[at : at + rows.shape[0], t * LANES : (t + 1) * LANES] = rows.astype(jnp.bfloat16)


def products_kernel(table_ref, velocity_ref, out_ref, fields_ref, block_ref, sem):
    depth = velocity_ref.shape[1]
    parts = [velocity_ref[a] for a in range(3)]
    for a in range(3):
        fields_ref[a * depth : (a + 1) * depth, :] = parts[a].astype(jnp.bfloat16)
    for p, (a, b) in enumerate(index_pairs):
        at = (3 + p) * depth
        fields_ref[at : at + depth, :] = (parts[a] * parts[b]).astype(jnp.bfloat16)
    tile, seed = table_ref[:LANES, :], table_ref[LANES:, :]
    send_blocks(tile, seed, fields_ref, block_ref, out_ref, sem, 9, depth)


def strain(gradients):
    strain_parts = [0.5 * (gradients[b][a] + gradients[a][b]) for a, b in index_pairs]
    squares_sum = pair_weights[0] * strain_parts[0] * strain_parts[0]
    for weight, part_value in zip(pair_weights[1:], strain_parts[1:]):
        squares_sum = squares_sum + weight * part_value * part_value
    return (strain_parts, jnp.sqrt(2.0 * squares_sum))


def slopes(center, one, two, sense, first, last):
    rows, length = center.shape
    row = lax.broadcasted_iota(jnp.int32, center.shape, 0)
    along = (pltpu.roll(center, length - 1, 1) - pltpu.roll(center, 1, 1)) * 0.5
    following = jnp.where(row == rows - 1, last, pltpu.roll(center, rows - 1, 0))
    previous = jnp.where(row == 0, first, pltpu.roll(center, 1, 0))
    return (along, (two - one) * sense, (following - previous) * 0.5)


def strain_kernel(
    table_ref, velocity_ref, one_ref, two_ref, sense_ref, first_ref, last_ref, out_ref, magnitude_ref,
    fields_ref, block_ref, sem,
):
    depth = velocity_ref.shape[1]
    gradients = [
        slopes(velocity_ref[a], one_ref[a], two_ref[a], sense_ref[...], first_ref[a], last_ref[a])
        for a in range(3)
    ]
    strain_parts, magnitude = strain(gradients)
    magnitude_ref[...] = magnitude
    for p, part_value in enumerate(strain_parts):
        fields_ref[p * depth : (p + 1) * depth, :] = (magnitude * part_value).astype(jnp.bfloat16)
    tile = tile_of(table_ref[...])
    send_blocks(tile, None, fields_ref, block_ref, out_ref, sem, 6, depth)


def smooth_kernel(table_ref, recv_ref, smooth_ref, edges_ref, band_ref, lines_ref):
    senders = recv_ref.shape[0]
    _, width, length = smooth_ref.shape
    for t in range(senders // 2):
        one, two = sorted_lines(recv_ref, t, 0, width)
        place(lines_ref, 0, t, one)
        place(lines_ref, width, t, two)
        one, two = sorted_lines(recv_ref, t, width, width)
        place(lines_ref, 2 * width, t, one)
        one, two = sorted_lines(recv_ref, t, 9 * width // 2, 8)
        place(lines_ref, 3 * width, t, jnp.concatenate([one, two], axis=0))
    got = nt(lines_ref[...], table_of(table_ref[...])).astype(jnp.bfloat16)
    for a in range(3):
        smooth_ref[a] = got[a * width : (a + 1) * width, :]
    edges_ref[...] = got[3 * width :, :].astype(jnp.float32)
    band_ref[...] = table_ref[...]


def squares_kernel(table_ref, recv_ref, squares_ref, lines_ref):
    senders = recv_ref.shape[0]
    _, width, length = squares_ref.shape
    half = width // 2
    for t in range(senders // 2):
        place(lines_ref, 0, t, sorted_lines(recv_ref, t, width, width)[1])
        for j in range(2):
            one, two = sorted_lines(recv_ref, t, (2 + j) * width, width)
            place(lines_ref, (1 + 2 * j) * width, t, one)
            place(lines_ref, (2 + 2 * j) * width, t, two)
        one, two = sorted_lines(recv_ref, t, 4 * width, half)
        place(lines_ref, 5 * width, t, one)
        place(lines_ref, 5 * width + half, t, two)
    got = nt(lines_ref[...], table_of(table_ref[...])).astype(jnp.bfloat16)
    for p in range(6):
        squares_ref[p] = got[p * width : (p + 1) * width, :]


def model_kernel(smooth_ref, one_ref, two_ref, sense_ref, edges_ref, model_ref):
    gradients = []
    for a, at in zip(range(3), (0, 8, 2)):
        center, one, two = (ref[a].astype(jnp.float32) for ref in (smooth_ref, one_ref, two_ref))
        first, last = edges_ref[at : at + 1, :], edges_ref[at + 1 : at + 2, :]
        along, across, between = slopes(center, one, two, sense_ref[...], first, last)
        gradients.append((between, across, along))
    strain_parts, magnitude = strain(gradients)
    for p, part_value in enumerate(strain_parts):
        model_ref[p] = 4.0 * magnitude * part_value


def sums_kernel(table_ref, recv_ref, smooth_ref, squares_ref, model_ref, out_ref, lines_ref):
    senders = recv_ref.shape[0]
    _, width, length = model_ref.shape
    for t in range(senders // 2):
        for j in range(3):
            one, two = sorted_lines(recv_ref, t, j * width, width)
            place(lines_ref, 2 * j * width, t, one)
            place(lines_ref, (2 * j + 1) * width, t, two)
    got = nt(lines_ref[...], table_of(table_ref[...])).astype(jnp.bfloat16)
    smooth = [smooth_ref[a].astype(jnp.float32) for a in range(3)]
    numerator = jnp.zeros((8, length), jnp.float32)
    denominator = jnp.zeros((8, length), jnp.float32)
    for p, (weight, (a, b)) in enumerate(zip(pair_weights, index_pairs)):
        leonard = squares_ref[p].astype(jnp.float32) - smooth[a] * smooth[b]
        model_term = got[p * width : (p + 1) * width, :].astype(jnp.float32) - model_ref[p]
        top = leonard * model_term
        bottom = model_term * model_term
        numerator = numerator + weight * top.reshape(width // 8, 8, length).sum(axis=0)
        denominator = denominator + weight * bottom.reshape(width // 8, 8, length).sum(axis=0)

    def lanes(x):
        total = x[:, :LANES]
        for at in range(LANES, length, LANES):
            total = total + x[:, at : at + LANES]
        total = total.sum(axis=0, keepdims=True)
        return total + pltpu.roll(total, LANES // 2, 1)

    low = lax.broadcasted_iota(jnp.int32, (1, LANES), 1) < LANES // 2
    pair = jnp.where(low, lanes(numerator), lanes(denominator))
    out_ref[...] = jnp.broadcast_to(pair, out_ref.shape)


def viscosity_kernel(cells, sums_ref, magnitude_ref, out_ref):
    total = sums_ref[...].sum(axis=0)
    low = lax.broadcasted_iota(jnp.int32, total.shape, 1) < LANES // 2
    numerator = jnp.sum(jnp.where(low, total, 0.0), axis=1, keepdims=True)
    denominator = jnp.sum(jnp.where(low, 0.0, total), axis=1, keepdims=True)
    coefficient = numerator / cells / (2.0 * (denominator / cells + epsilon))
    out_ref[...] = magnitude_ref[...] * coefficient


def body(velocity):
    _, _, depth, nx = velocity.shape
    parts = lax.axis_size("pz")
    rows = lax.axis_size("py")
    nz = depth * parts
    width = nx // parts
    f32, bf16 = jnp.float32, jnp.bfloat16
    table_x = filter_table(nx).T
    table_z = filter_table(nz)
    beside = np.zeros((2, 8, nx), bf16)
    for r in range(2):
        beside[r, :4] = table_x[[r * width - 1, (r + 1) * width] * 2]
    lanes_x = jnp.asarray(np.concatenate([table_x[:LANES], beside.reshape(16, nx)]))
    short_x = jnp.asarray(table_x[:BAND])
    same = np.array_equal(table_x[:BAND], table_z[:BAND])
    lanes_z = short_x if same else jnp.asarray(table_z[:BAND])
    outward, inward = [], []
    for i in range(rows - 1):
        for j in range(parts):
            pair = (i * parts + j, (i + 1) * parts + j)
            (inward if j % 2 else outward).append(pair)
            (outward if j % 2 else inward).append(pair[::-1])
    sense = (0.5 - (lax.axis_index("pz") % 2).astype(f32)).reshape(1, 1)
    around = [(i, (i + 1) % parts) for i in range(parts)]
    back = [(b, a) for a, b in around]
    velocity = velocity.reshape(3, depth, nx)
    vmem, dma = pltpu.VMEM, pltpu.SemaphoreType.DMA

    last = lax.ppermute(velocity[:, :1], "pz", back)
    first = lax.ppermute(velocity[:, -1:], "pz", around)
    send_shape = (parts, 9 * width // 2 + 8, LANES)
    send = call(
        products_kernel,
        jax.ShapeDtypeStruct(send_shape, bf16),
        2 * 9 * depth * nx * nx,
        12 * depth * nx + 2 * nx * nx,
        [vmem((9 * depth, nx), bf16), vmem(send_shape, bf16), dma((4,))],
        "products",
        (2,),
        58,
    )(lanes_x, velocity)
    send, last, first = lax.optimization_barrier((send, last, first))
    received = lax.all_to_all(send, "pz", 0, 0, tiled=True)

    one = lax.ppermute(velocity, ("py", "pz"), outward)
    two = lax.ppermute(velocity, ("py", "pz"), inward)
    strain_shape = (parts, 3 * width, LANES)
    send_strain, magnitude = call(
        strain_kernel,
        (jax.ShapeDtypeStruct(strain_shape, bf16), jax.ShapeDtypeStruct((depth, nx), f32)),
        2 * 6 * depth * nx * nx,
        36 * depth * nx + 2 * nx * nx,
        [vmem((6 * depth, nx), bf16), vmem(strain_shape, bf16), dma((2,))],
        "strain",
        (7,),
        54,
    )(short_x, velocity, one, two, sense, first, last)
    received_strain = lax.all_to_all(send_strain, "pz", 0, 0, tiled=True)

    smooth, edges, band = call(
        smooth_kernel,
        (
            jax.ShapeDtypeStruct((3, width, nz), bf16),
            jax.ShapeDtypeStruct((16, nz), f32),
            jax.ShapeDtypeStruct((BAND, nz), bf16),
        ),
        2 * 4 * width * nz * nz,
        2 * nz * nz,
        [vmem((3 * width + 16, nz), bf16)],
        "smooth",
    )(lanes_z, received)
    smooth_one = lax.ppermute(smooth, ("py", "pz"), outward)
    smooth_two = lax.ppermute(smooth, ("py", "pz"), inward)
    squares = call(
        squares_kernel,
        jax.ShapeDtypeStruct((6, width, nz), bf16),
        2 * 6 * width * nz * nz,
        24 * width * nz,
        [vmem((6 * width, nz), bf16)],
        "squares",
    )(lanes_z, received)
    model = call(
        model_kernel,
        jax.ShapeDtypeStruct((6, width, nz), f32),
        100 * width * nz,
        24 * width * nz,
        (),
        "model",
    )(smooth, smooth_one, smooth_two, sense, edges)
    sums = call(
        sums_kernel,
        jax.ShapeDtypeStruct((parts, 1, LANES), f32),
        2 * 6 * width * nz * nz,
        48 * width * nz,
        [vmem((6 * width, nz), bf16)],
        "sums",
    )(band, received_strain, smooth, squares, model)
    totals = lax.all_to_all(sums, "pz", 0, 0, tiled=True)
    cells = nx * nz
    nu_t = call(
        lambda *refs: viscosity_kernel(cells, *refs),
        jax.ShapeDtypeStruct((depth, nx), f32),
        2 * depth * nx,
        8 * depth * nx,
        (),
        "viscosity",
    )(totals, magnitude)
    filtered_velocity = jnp.transpose(smooth, (0, 2, 1))
    return (nu_t[None], filtered_velocity[:, None])


def solution(mesh):
    in_specs = (P(None, "py", "pz", None),)
    out_specs = (P("py", "pz", None), P(None, "py", None, "pz"))
    return jax.shard_map(body, mesh=mesh, in_specs=in_specs, out_specs=out_specs, check_vma=False)
```

```python
import math

import jax
import jax.numpy as jnp
import numpy as np
from jax import lax
from jax.experimental import pallas as pl
from jax.experimental.pallas import tpu as pltpu
from jax.sharding import PartitionSpec as P

index_pairs = ((0, 0), (1, 1), (2, 2), (0, 1), (0, 2), (1, 2))
pair_weights = (1.0, 1.0, 1.0, 2.0, 2.0, 2.0)
epsilon = 1e-06
LANES = 128
BAND = 8


def filter_table(length):
    offsets = np.arange(length, dtype=np.int64)
    wavenumbers = np.arange(1, length // 4, dtype=np.int64)
    phase = offsets[:, None] * wavenumbers[None, :] % length
    kernel = (1.0 + 2.0 * np.cos(phase * (2.0 * math.pi / length)).sum(axis=1)) / length
    kernel = kernel.astype(np.float32)
    lagged = (offsets[:, None] - offsets[None, :]) % length
    return kernel[lagged].astype(jnp.bfloat16)


def call(kernel, out_shape, flops, moved, scratch=(), name=None, far=(), room=24):
    outs = jax.tree.leaves(out_shape)

    def space(i):
        return pl.BlockSpec(memory_space=pltpu.HBM if i in far else pltpu.VMEM)

    def run(*args):
        out_specs = [space(len(args) + i) for i in range(len(outs))]
        return pl.pallas_call(
            kernel,
            out_shape=out_shape,
            in_specs=[space(i) for i in range(len(args))],
            out_specs=out_specs if isinstance(out_shape, tuple) else out_specs[0],
            scratch_shapes=list(scratch),
            cost_estimate=pl.CostEstimate(flops=flops, bytes_accessed=moved, transcendentals=0),
            compiler_params=pltpu.CompilerParams(vmem_limit_bytes=room * 1024 * 1024),
            name=name,
        )(*args)

    return run


def nt(a, b):
    return lax.dot_general(a, b, (((1,), (1,)), ((), ())), preferred_element_type=jnp.float32)


def turned(rows, blocks):
    at = rows.shape[1] - blocks * LANES
    return rows if blocks == 0 else jnp.concatenate([rows[:, at:], rows[:, :at]], axis=1)


def table_rows(band_ref, first, last):
    band = band_ref[:LANES, :]
    return jnp.concatenate([turned(band, a) for a in range(first, last)], axis=0)


def table_of(band):
    band = band.astype(jnp.float32)
    rows = [band] + [pltpu.roll(band, at, 1) for at in range(BAND, LANES, BAND)]
    tile = jnp.concatenate(rows, axis=0).astype(jnp.bfloat16)
    return jnp.concatenate([turned(tile, a) for a in range(band.shape[1] // LANES)], axis=0)


def send_blocks(table_ref, fields_ref, block_ref, out_ref, sem, count, depth, edges):
    receivers = block_ref.shape[0]
    width = fields_ref.shape[1] // receivers
    per = LANES // depth
    full = count // per
    if edges:
        seed = table_ref[LANES:, :]
        beside = [turned(seed, q) for q in range(receivers * width // LANES)]
        beside = jnp.concatenate(beside, axis=0)
        got = nt(beside, fields_ref[: 2 * per * depth, :])
        row = lax.broadcasted_iota(jnp.int32, (receivers * 8, LANES), 0) % 8
        got = jnp.where(row < 2, got[:, :LANES], got[:, LANES:]).reshape(receivers, 8, LANES)
        block_ref[:, count * width // per :, :] = got.astype(jnp.bfloat16)
    chunks = sem.shape[0]
    some = receivers // chunks
    copies = []
    for c in range(chunks):
        mine = slice(c * some, (c + 1) * some)
        blocks = some * width // LANES
        table = table_rows(table_ref, c * blocks, (c + 1) * blocks)
        for first in range(0, full, 2):
            here = min(2, full - first)
            got = nt(table, fields_ref[first * LANES : (first + here) * LANES, :])
            got = got.astype(jnp.bfloat16)
            for j in range(here):
                block = got[:, j * LANES : (j + 1) * LANES].reshape(some, width, LANES)
                block_ref[mine, (first + j) * width : (first + j + 1) * width, :] = block
        if count % per:
            last = fields_ref[full * LANES : count * depth, :]
            got = nt(table, jnp.concatenate([last, last], axis=0))
            got = got.reshape(some, width, LANES)
            half = width // 2
            lane = lax.broadcasted_iota(jnp.int32, (some, half, LANES), 2)
            block = jnp.where(lane < depth, got[:, :half, :], got[:, half:, :])
            at = full * width
            block_ref[mine, at : at + half, :] = block.astype(jnp.bfloat16)
        copies.append(pltpu.make_async_copy(block_ref.at[mine], out_ref.at[mine], sem.at[c]))
        copies[-1].start()
    for copy in copies:
        copy.wait()


def sorted_lines(recv_ref, t, start, count):
    low = lax.broadcasted_iota(jnp.int32, (count, LANES), 1) < LANES // 2
    even = recv_ref[2 * t, start : start + count, :].astype(jnp.float32)
    odd = recv_ref[2 * t + 1, start : start + count, :].astype(jnp.float32)
    one = jnp.where(low, even, pltpu.roll(odd, LANES // 2, 1))
    two = jnp.where(low, pltpu.roll(even, LANES // 2, 1), odd)
    return one, two


def place(lines_ref, at, t, rows):
    lines_ref[at : at + rows.shape[0], t * LANES : (t + 1) * LANES] = rows.astype(jnp.bfloat16)


def products_kernel(table_ref, velocity_ref, out_ref, fields_ref, block_ref, sem):
    depth = velocity_ref.shape[1]
    parts = [velocity_ref[a] for a in range(3)]
    for a in range(3):
        fields_ref[a * depth : (a + 1) * depth, :] = parts[a].astype(jnp.bfloat16)
    for p, (a, b) in enumerate(index_pairs):
        at = (3 + p) * depth
        fields_ref[at : at + depth, :] = (parts[a] * parts[b]).astype(jnp.bfloat16)
    send_blocks(table_ref, fields_ref, block_ref, out_ref, sem, 9, depth, True)


def strain(gradients):
    strain_parts = [0.5 * (gradients[b][a] + gradients[a][b]) for a, b in index_pairs]
    squares_sum = pair_weights[0] * strain_parts[0] * strain_parts[0]
    for weight, part_value in zip(pair_weights[1:], strain_parts[1:]):
        squares_sum = squares_sum + weight * part_value * part_value
    return (strain_parts, jnp.sqrt(2.0 * squares_sum))


def slopes(center, one, two, sense, first, last):
    rows, length = center.shape
    row = lax.broadcasted_iota(jnp.int32, center.shape, 0)
    along = (pltpu.roll(center, length - 1, 1) - pltpu.roll(center, 1, 1)) * 0.5
    following = jnp.where(row == rows - 1, last, pltpu.roll(center, rows - 1, 0))
    previous = jnp.where(row == 0, first, pltpu.roll(center, 1, 0))
    return (along, (two - one) * sense, (following - previous) * 0.5)


def strain_kernel(
    table_ref, velocity_ref, one_ref, two_ref, sense_ref, first_ref, last_ref, out_ref, magnitude_ref,
    fields_ref, block_ref, sem,
):
    depth = velocity_ref.shape[1]
    gradients = [
        slopes(velocity_ref[a], one_ref[a], two_ref[a], sense_ref[...], first_ref[a], last_ref[a])
        for a in range(3)
    ]
    strain_parts, magnitude = strain(gradients)
    magnitude_ref[...] = magnitude
    for p, part_value in enumerate(strain_parts):
        fields_ref[p * depth : (p + 1) * depth, :] = (magnitude * part_value).astype(jnp.bfloat16)
    send_blocks(table_ref, fields_ref, block_ref, out_ref, sem, 6, depth, False)


def smooth_kernel(table_ref, recv_ref, smooth_ref, edges_ref, band_ref, lines_ref):
    senders = recv_ref.shape[0]
    _, width, length = smooth_ref.shape
    for t in range(senders // 2):
        one, two = sorted_lines(recv_ref, t, 0, width)
        place(lines_ref, 0, t, one)
        place(lines_ref, width, t, two)
        one, two = sorted_lines(recv_ref, t, width, width)
        place(lines_ref, 2 * width, t, one)
        one, two = sorted_lines(recv_ref, t, 9 * width // 2, 8)
        place(lines_ref, 3 * width, t, jnp.concatenate([one, two], axis=0))
    got = nt(lines_ref[...], table_rows(table_ref, 0, length // LANES)).astype(jnp.bfloat16)
    for a in range(3):
        smooth_ref[a] = got[a * width : (a + 1) * width, :]
    edges_ref[...] = got[3 * width :, :].astype(jnp.float32)
    band_ref[...] = table_ref[:BAND, :]


def squares_kernel(table_ref, recv_ref, squares_ref, lines_ref):
    senders = recv_ref.shape[0]
    _, width, length = squares_ref.shape
    half = width // 2
    for t in range(senders // 2):
        place(lines_ref, 0, t, sorted_lines(recv_ref, t, width, width)[1])
        for j in range(2):
            one, two = sorted_lines(recv_ref, t, (2 + j) * width, width)
            place(lines_ref, (1 + 2 * j) * width, t, one)
            place(lines_ref, (2 + 2 * j) * width, t, two)
        one, two = sorted_lines(recv_ref, t, 4 * width, half)
        place(lines_ref, 5 * width, t, one)
        place(lines_ref, 5 * width + half, t, two)
    got = nt(lines_ref[...], table_rows(table_ref, 0, length // LANES)).astype(jnp.bfloat16)
    for p in range(6):
        squares_ref[p] = got[p * width : (p + 1) * width, :]


def model_kernel(smooth_ref, one_ref, two_ref, sense_ref, edges_ref, model_ref):
    gradients = []
    for a, at in zip(range(3), (0, 8, 2)):
        center, one, two = (ref[a].astype(jnp.float32) for ref in (smooth_ref, one_ref, two_ref))
        first, last = edges_ref[at : at + 1, :], edges_ref[at + 1 : at + 2, :]
        along, across, between = slopes(center, one, two, sense_ref[...], first, last)
        gradients.append((between, across, along))
    strain_parts, magnitude = strain(gradients)
    for p, part_value in enumerate(strain_parts):
        model_ref[p] = 4.0 * magnitude * part_value


def sums_kernel(table_ref, recv_ref, smooth_ref, squares_ref, model_ref, out_ref, lines_ref):
    senders = recv_ref.shape[0]
    _, width, length = model_ref.shape
    for t in range(senders // 2):
        for j in range(3):
            one, two = sorted_lines(recv_ref, t, j * width, width)
            place(lines_ref, 2 * j * width, t, one)
            place(lines_ref, (2 * j + 1) * width, t, two)
    got = nt(lines_ref[...], table_of(table_ref[...])).astype(jnp.bfloat16)
    smooth = [smooth_ref[a].astype(jnp.float32) for a in range(3)]
    numerator = jnp.zeros((8, length), jnp.float32)
    denominator = jnp.zeros((8, length), jnp.float32)
    for p, (weight, (a, b)) in enumerate(zip(pair_weights, index_pairs)):
        leonard = squares_ref[p].astype(jnp.float32) - smooth[a] * smooth[b]
        model_term = got[p * width : (p + 1) * width, :].astype(jnp.float32) - model_ref[p]
        top = leonard * model_term
        bottom = model_term * model_term
        numerator = numerator + weight * top.reshape(width // 8, 8, length).sum(axis=0)
        denominator = denominator + weight * bottom.reshape(width // 8, 8, length).sum(axis=0)

    def lanes(x):
        total = x[:, :LANES]
        for at in range(LANES, length, LANES):
            total = total + x[:, at : at + LANES]
        total = total.sum(axis=0, keepdims=True)
        return total + pltpu.roll(total, LANES // 2, 1)

    low = lax.broadcasted_iota(jnp.int32, (1, LANES), 1) < LANES // 2
    pair = jnp.where(low, lanes(numerator), lanes(denominator))
    out_ref[...] = jnp.broadcast_to(pair, out_ref.shape)


def viscosity_kernel(cells, sums_ref, magnitude_ref, out_ref):
    total = sums_ref[...].sum(axis=0)
    low = lax.broadcasted_iota(jnp.int32, total.shape, 1) < LANES // 2
    numerator = jnp.sum(jnp.where(low, total, 0.0), axis=1, keepdims=True)
    denominator = jnp.sum(jnp.where(low, 0.0, total), axis=1, keepdims=True)
    coefficient = numerator / cells / (2.0 * (denominator / cells + epsilon))
    out_ref[...] = magnitude_ref[...] * coefficient


def body(velocity):
    _, _, depth, nx = velocity.shape
    parts = lax.axis_size("pz")
    rows = lax.axis_size("py")
    nz = depth * parts
    width = nx // parts
    f32, bf16 = jnp.float32, jnp.bfloat16
    table_x = filter_table(nx).T
    table_z = filter_table(nz)
    beside = np.zeros((2, 8, nx), bf16)
    for r in range(2):
        beside[r, :4] = table_x[[r * width - 1, (r + 1) * width] * 2]
    lanes_x = jnp.asarray(np.concatenate([table_x[:LANES], beside.reshape(16, nx)]))
    same = np.array_equal(table_x[:LANES], table_z[:LANES])
    lanes_z = lanes_x if same else jnp.asarray(table_z[:LANES])
    outward, inward = [], []
    for i in range(rows - 1):
        for j in range(parts):
            pair = (i * parts + j, (i + 1) * parts + j)
            (inward if j % 2 else outward).append(pair)
            (outward if j % 2 else inward).append(pair[::-1])
    sense = (0.5 - (lax.axis_index("pz") % 2).astype(f32)).reshape(1, 1)
    around = [(i, (i + 1) % parts) for i in range(parts)]
    back = [(b, a) for a, b in around]
    velocity = velocity.reshape(3, depth, nx)
    vmem, dma = pltpu.VMEM, pltpu.SemaphoreType.DMA

    first = lax.ppermute(velocity[:, -1:], "pz", around)
    last = lax.ppermute(velocity[:, :1], "pz", back)
    send_shape = (parts, 9 * width // 2 + 8, LANES)
    send = call(
        products_kernel,
        jax.ShapeDtypeStruct(send_shape, bf16),
        2 * 9 * depth * nx * nx,
        12 * depth * nx + 2 * nx * nx,
        [vmem((9 * depth, nx), bf16), vmem(send_shape, bf16), dma((4,))],
        "products",
        (2,),
        58,
    )(lanes_x, velocity)
    send, first, last = lax.optimization_barrier((send, first, last))
    received = lax.all_to_all(send, "pz", 0, 0, tiled=True)

    one = lax.ppermute(velocity, ("py", "pz"), outward)
    two = lax.ppermute(velocity, ("py", "pz"), inward)
    strain_shape = (parts, 3 * width, LANES)
    send_strain, magnitude = call(
        strain_kernel,
        (jax.ShapeDtypeStruct(strain_shape, bf16), jax.ShapeDtypeStruct((depth, nx), f32)),
        2 * 6 * depth * nx * nx,
        36 * depth * nx + 2 * nx * nx,
        [vmem((6 * depth, nx), bf16), vmem(strain_shape, bf16), dma((2,))],
        "strain",
        (7,),
    )(lanes_x, velocity, one, two, sense, first, last)
    received_strain = lax.all_to_all(send_strain, "pz", 0, 0, tiled=True)

    smooth, edges, band = call(
        smooth_kernel,
        (
            jax.ShapeDtypeStruct((3, width, nz), bf16),
            jax.ShapeDtypeStruct((16, nz), f32),
            jax.ShapeDtypeStruct((BAND, nz), bf16),
        ),
        2 * 4 * width * nz * nz,
        2 * nz * nz,
        [vmem((3 * width + 16, nz), bf16)],
        "smooth",
    )(lanes_z, received)
    smooth_one = lax.ppermute(smooth, ("py", "pz"), outward)
    smooth_two = lax.ppermute(smooth, ("py", "pz"), inward)
    squares = call(
        squares_kernel,
        jax.ShapeDtypeStruct((6, width, nz), bf16),
        2 * 6 * width * nz * nz,
        24 * width * nz,
        [vmem((6 * width, nz), bf16)],
        "squares",
    )(lanes_z, received)
    model = call(
        model_kernel,
        jax.ShapeDtypeStruct((6, width, nz), f32),
        100 * width * nz,
        24 * width * nz,
        (),
        "model",
    )(smooth, smooth_one, smooth_two, sense, edges)
    sums = call(
        sums_kernel,
        jax.ShapeDtypeStruct((parts, 1, LANES), f32),
        2 * 6 * width * nz * nz,
        48 * width * nz,
        [vmem((6 * width, nz), bf16)],
        "sums",
    )(band, received_strain, smooth, squares, model)
    totals = lax.all_to_all(sums, "pz", 0, 0, tiled=True)
    cells = nx * nz
    nu_t = call(
        lambda *refs: viscosity_kernel(cells, *refs),
        jax.ShapeDtypeStruct((depth, nx), f32),
        2 * depth * nx,
        8 * depth * nx,
        (),
        "viscosity",
    )(totals, magnitude)
    filtered_velocity = jnp.transpose(smooth, (0, 2, 1))
    return (nu_t[None], filtered_velocity[:, None])


def solution(mesh):
    in_specs = (P(None, "py", "pz", None),)
    out_specs = (P("py", "pz", None), P(None, "py", None, "pz"))
    return jax.shard_map(body, mesh=mesh, in_specs=in_specs, out_specs=out_specs, check_vma=False)
```

```python
import math

import jax
import jax.numpy as jnp
import numpy as np
from jax import lax
from jax.experimental import pallas as pl
from jax.experimental.pallas import tpu as pltpu
from jax.sharding import PartitionSpec as P

index_pairs = ((0, 0), (1, 1), (2, 2), (0, 1), (0, 2), (1, 2))
pair_weights = (1.0, 1.0, 1.0, 2.0, 2.0, 2.0)
epsilon = 1e-06
LANES = 128
BAND = 8


def filter_table(length):
    offsets = np.arange(length, dtype=np.int64)
    wavenumbers = np.arange(1, length // 4, dtype=np.int64)
    phase = offsets[:, None] * wavenumbers[None, :] % length
    kernel = (1.0 + 2.0 * np.cos(phase * (2.0 * math.pi / length)).sum(axis=1)) / length
    kernel = kernel.astype(np.float32)
    lagged = (offsets[:, None] - offsets[None, :]) % length
    return kernel[lagged].astype(jnp.bfloat16)


def call(kernel, out_shape, flops, moved, scratch=(), name=None, far=(), room=24):
    outs = jax.tree.leaves(out_shape)

    def space(i):
        return pl.BlockSpec(memory_space=pltpu.HBM if i in far else pltpu.VMEM)

    def run(*args):
        out_specs = [space(len(args) + i) for i in range(len(outs))]
        return pl.pallas_call(
            kernel,
            out_shape=out_shape,
            in_specs=[space(i) for i in range(len(args))],
            out_specs=out_specs if isinstance(out_shape, tuple) else out_specs[0],
            scratch_shapes=list(scratch),
            cost_estimate=pl.CostEstimate(flops=flops, bytes_accessed=moved, transcendentals=0),
            compiler_params=pltpu.CompilerParams(vmem_limit_bytes=room * 1024 * 1024),
            name=name,
        )(*args)

    return run


def nt(a, b):
    return lax.dot_general(a, b, (((1,), (1,)), ((), ())), preferred_element_type=jnp.float32)


def turned(rows, blocks):
    at = rows.shape[1] - blocks * LANES
    return rows if blocks == 0 else jnp.concatenate([rows[:, at:], rows[:, :at]], axis=1)


def table_rows(band_ref, first, last):
    band = band_ref[:LANES, :]
    return jnp.concatenate([turned(band, a) for a in range(first, last)], axis=0)


def table_of(band):
    band = band.astype(jnp.float32)
    rows = [band] + [pltpu.roll(band, at, 1) for at in range(BAND, LANES, BAND)]
    tile = jnp.concatenate(rows, axis=0).astype(jnp.bfloat16)
    return jnp.concatenate([turned(tile, a) for a in range(band.shape[1] // LANES)], axis=0)


def send_blocks(table_ref, fields_ref, block_ref, out_ref, sem, count, depth, edges, shares):
    receivers = block_ref.shape[0]
    width = fields_ref.shape[1] // receivers
    per = LANES // depth
    full = count // per
    if edges:
        seed = table_ref[LANES:, :]
        beside = [turned(seed, q) for q in range(receivers * width // LANES)]
        beside = jnp.concatenate(beside, axis=0)
        got = nt(beside, fields_ref[: 2 * per * depth, :])
        row = lax.broadcasted_iota(jnp.int32, (receivers * 8, LANES), 0) % 8
        got = jnp.where(row < 2, got[:, :LANES], got[:, LANES:]).reshape(receivers, 8, LANES)
        block_ref[:, count * width // per :, :] = got.astype(jnp.bfloat16)
    copies, done = [], 0
    for c, some in enumerate(shares):
        mine = slice(done, done + some)
        first_block, last_block = done * width // LANES, (done + some) * width // LANES
        done += some
        table = table_rows(table_ref, first_block, last_block)
        for first in range(0, full, 2):
            here = min(2, full - first)
            got = nt(table, fields_ref[first * LANES : (first + here) * LANES, :])
            got = got.astype(jnp.bfloat16)
            for j in range(here):
                block = got[:, j * LANES : (j + 1) * LANES].reshape(some, width, LANES)
                block_ref[mine, (first + j) * width : (first + j + 1) * width, :] = block
        if count % per:
            last = fields_ref[full * LANES : count * depth, :]
            got = nt(table, jnp.concatenate([last, last], axis=0))
            got = got.reshape(some, width, LANES)
            half = width // 2
            lane = lax.broadcasted_iota(jnp.int32, (some, half, LANES), 2)
            block = jnp.where(lane < depth, got[:, :half, :], got[:, half:, :])
            at = full * width
            block_ref[mine, at : at + half, :] = block.astype(jnp.bfloat16)
        copies.append(pltpu.make_async_copy(block_ref.at[mine], out_ref.at[mine], sem.at[c]))
        copies[-1].start()
    for copy in copies:
        copy.wait()


def sorted_lines(recv_ref, t, start, count):
    low = lax.broadcasted_iota(jnp.int32, (count, LANES), 1) < LANES // 2
    even = recv_ref[2 * t, start : start + count, :].astype(jnp.float32)
    odd = recv_ref[2 * t + 1, start : start + count, :].astype(jnp.float32)
    one = jnp.where(low, even, pltpu.roll(odd, LANES // 2, 1))
    two = jnp.where(low, pltpu.roll(even, LANES // 2, 1), odd)
    return one, two


def place(lines_ref, at, t, rows):
    lines_ref[at : at + rows.shape[0], t * LANES : (t + 1) * LANES] = rows.astype(jnp.bfloat16)


def products_kernel(table_ref, velocity_ref, out_ref, fields_ref, block_ref, sem):
    depth = velocity_ref.shape[1]
    parts = [velocity_ref[a] for a in range(3)]
    for a in range(3):
        fields_ref[a * depth : (a + 1) * depth, :] = parts[a].astype(jnp.bfloat16)
    for p, (a, b) in enumerate(index_pairs):
        at = (3 + p) * depth
        fields_ref[at : at + depth, :] = (parts[a] * parts[b]).astype(jnp.bfloat16)
    send_blocks(table_ref, fields_ref, block_ref, out_ref, sem, 9, depth, True, (8, 4, 4))


def strain(gradients):
    strain_parts = [0.5 * (gradients[b][a] + gradients[a][b]) for a, b in index_pairs]
    squares_sum = pair_weights[0] * strain_parts[0] * strain_parts[0]
    for weight, part_value in zip(pair_weights[1:], strain_parts[1:]):
        squares_sum = squares_sum + weight * part_value * part_value
    return (strain_parts, jnp.sqrt(2.0 * squares_sum))


def slopes(center, one, two, sense, first, last):
    rows, length = center.shape
    row = lax.broadcasted_iota(jnp.int32, center.shape, 0)
    along = (pltpu.roll(center, length - 1, 1) - pltpu.roll(center, 1, 1)) * 0.5
    following = jnp.where(row == rows - 1, last, pltpu.roll(center, rows - 1, 0))
    previous = jnp.where(row == 0, first, pltpu.roll(center, 1, 0))
    return (along, (two - one) * sense, (following - previous) * 0.5)


def strain_kernel(
    table_ref, velocity_ref, one_ref, two_ref, sense_ref, first_ref, last_ref, out_ref, magnitude_ref,
    fields_ref, block_ref, sem,
):
    depth = velocity_ref.shape[1]
    gradients = [
        slopes(velocity_ref[a], one_ref[a], two_ref[a], sense_ref[...], first_ref[a], last_ref[a])
        for a in range(3)
    ]
    strain_parts, magnitude = strain(gradients)
    magnitude_ref[...] = magnitude
    for p, part_value in enumerate(strain_parts):
        fields_ref[p * depth : (p + 1) * depth, :] = (magnitude * part_value).astype(jnp.bfloat16)
    send_blocks(table_ref, fields_ref, block_ref, out_ref, sem, 6, depth, False, (8, 8))


def smooth_kernel(table_ref, recv_ref, smooth_ref, edges_ref, band_ref, lines_ref):
    senders = recv_ref.shape[0]
    _, width, length = smooth_ref.shape
    for t in range(senders // 2):
        one, two = sorted_lines(recv_ref, t, 0, width)
        place(lines_ref, 0, t, one)
        place(lines_ref, width, t, two)
        one, two = sorted_lines(recv_ref, t, width, width)
        place(lines_ref, 2 * width, t, one)
        one, two = sorted_lines(recv_ref, t, 9 * width // 2, 8)
        place(lines_ref, 3 * width, t, jnp.concatenate([one, two], axis=0))
    got = nt(lines_ref[...], table_rows(table_ref, 0, length // LANES)).astype(jnp.bfloat16)
    for a in range(3):
        smooth_ref[a] = got[a * width : (a + 1) * width, :]
    edges_ref[...] = got[3 * width :, :].astype(jnp.float32)
    band_ref[...] = table_ref[:BAND, :]


def squares_kernel(table_ref, recv_ref, squares_ref, lines_ref):
    senders = recv_ref.shape[0]
    _, width, length = squares_ref.shape
    half = width // 2
    for t in range(senders // 2):
        place(lines_ref, 0, t, sorted_lines(recv_ref, t, width, width)[1])
        for j in range(2):
            one, two = sorted_lines(recv_ref, t, (2 + j) * width, width)
            place(lines_ref, (1 + 2 * j) * width, t, one)
            place(lines_ref, (2 + 2 * j) * width, t, two)
        one, two = sorted_lines(recv_ref, t, 4 * width, half)
        place(lines_ref, 5 * width, t, one)
        place(lines_ref, 5 * width + half, t, two)
    got = nt(lines_ref[...], table_rows(table_ref, 0, length // LANES)).astype(jnp.bfloat16)
    for p in range(6):
        squares_ref[p] = got[p * width : (p + 1) * width, :]


def model_kernel(smooth_ref, one_ref, two_ref, sense_ref, edges_ref, model_ref):
    gradients = []
    for a, at in zip(range(3), (0, 8, 2)):
        center, one, two = (ref[a].astype(jnp.float32) for ref in (smooth_ref, one_ref, two_ref))
        first, last = edges_ref[at : at + 1, :], edges_ref[at + 1 : at + 2, :]
        along, across, between = slopes(center, one, two, sense_ref[...], first, last)
        gradients.append((between, across, along))
    strain_parts, magnitude = strain(gradients)
    for p, part_value in enumerate(strain_parts):
        model_ref[p] = 4.0 * magnitude * part_value


def sums_kernel(table_ref, recv_ref, smooth_ref, squares_ref, model_ref, out_ref, lines_ref):
    senders = recv_ref.shape[0]
    _, width, length = model_ref.shape
    for t in range(senders // 2):
        for j in range(3):
            one, two = sorted_lines(recv_ref, t, j * width, width)
            place(lines_ref, 2 * j * width, t, one)
            place(lines_ref, (2 * j + 1) * width, t, two)
    got = nt(lines_ref[...], table_of(table_ref[...])).astype(jnp.bfloat16)
    smooth = [smooth_ref[a].astype(jnp.float32) for a in range(3)]
    numerator = jnp.zeros((8, length), jnp.float32)
    denominator = jnp.zeros((8, length), jnp.float32)
    for p, (weight, (a, b)) in enumerate(zip(pair_weights, index_pairs)):
        leonard = squares_ref[p].astype(jnp.float32) - smooth[a] * smooth[b]
        model_term = got[p * width : (p + 1) * width, :].astype(jnp.float32) - model_ref[p]
        top = leonard * model_term
        bottom = model_term * model_term
        numerator = numerator + weight * top.reshape(width // 8, 8, length).sum(axis=0)
        denominator = denominator + weight * bottom.reshape(width // 8, 8, length).sum(axis=0)

    def lanes(x):
        total = x[:, :LANES]
        for at in range(LANES, length, LANES):
            total = total + x[:, at : at + LANES]
        total = total.sum(axis=0, keepdims=True)
        return total + pltpu.roll(total, LANES // 2, 1)

    low = lax.broadcasted_iota(jnp.int32, (1, LANES), 1) < LANES // 2
    pair = jnp.where(low, lanes(numerator), lanes(denominator))
    out_ref[...] = jnp.broadcast_to(pair, out_ref.shape)


def viscosity_kernel(cells, sums_ref, magnitude_ref, out_ref):
    total = sums_ref[...].sum(axis=0)
    low = lax.broadcasted_iota(jnp.int32, total.shape, 1) < LANES // 2
    numerator = jnp.sum(jnp.where(low, total, 0.0), axis=1, keepdims=True)
    denominator = jnp.sum(jnp.where(low, 0.0, total), axis=1, keepdims=True)
    coefficient = numerator / cells / (2.0 * (denominator / cells + epsilon))
    out_ref[...] = magnitude_ref[...] * coefficient


def body(velocity):
    _, _, depth, nx = velocity.shape
    parts = lax.axis_size("pz")
    rows = lax.axis_size("py")
    nz = depth * parts
    width = nx // parts
    f32, bf16 = jnp.float32, jnp.bfloat16
    table_x = filter_table(nx).T
    table_z = filter_table(nz)
    beside = np.zeros((2, 8, nx), bf16)
    for r in range(2):
        beside[r, :4] = table_x[[r * width - 1, (r + 1) * width] * 2]
    lanes_x = jnp.asarray(np.concatenate([table_x[:LANES], beside.reshape(16, nx)]))
    same = np.array_equal(table_x[:LANES], table_z[:LANES])
    lanes_z = lanes_x if same else jnp.asarray(table_z[:LANES])
    outward, inward = [], []
    for i in range(rows - 1):
        for j in range(parts):
            pair = (i * parts + j, (i + 1) * parts + j)
            (inward if j % 2 else outward).append(pair)
            (outward if j % 2 else inward).append(pair[::-1])
    sense = (0.5 - (lax.axis_index("pz") % 2).astype(f32)).reshape(1, 1)
    around = [(i, (i + 1) % parts) for i in range(parts)]
    back = [(b, a) for a, b in around]
    velocity = velocity.reshape(3, depth, nx)
    vmem, dma = pltpu.VMEM, pltpu.SemaphoreType.DMA

    first = lax.ppermute(velocity[:, -1:], "pz", around)
    last = lax.ppermute(velocity[:, :1], "pz", back)
    send_shape = (parts, 9 * width // 2 + 8, LANES)
    send = call(
        products_kernel,
        jax.ShapeDtypeStruct(send_shape, bf16),
        2 * 9 * depth * nx * nx,
        12 * depth * nx + 2 * nx * nx,
        [vmem((9 * depth, nx), bf16), vmem(send_shape, bf16), dma((3,))],
        "products",
        (2,),
        58,
    )(lanes_x, velocity)
    send, first, last = lax.optimization_barrier((send, first, last))
    received = lax.all_to_all(send, "pz", 0, 0, tiled=True)

    one = lax.ppermute(velocity, ("py", "pz"), outward)
    two = lax.ppermute(velocity, ("py", "pz"), inward)
    strain_shape = (parts, 3 * width, LANES)
    send_strain, magnitude = call(
        strain_kernel,
        (jax.ShapeDtypeStruct(strain_shape, bf16), jax.ShapeDtypeStruct((depth, nx), f32)),
        2 * 6 * depth * nx * nx,
        36 * depth * nx + 2 * nx * nx,
        [vmem((6 * depth, nx), bf16), vmem(strain_shape, bf16), dma((2,))],
        "strain",
        (7,),
    )(lanes_x, velocity, one, two, sense, first, last)
    received_strain = lax.all_to_all(send_strain, "pz", 0, 0, tiled=True)

    smooth, edges, band = call(
        smooth_kernel,
        (
            jax.ShapeDtypeStruct((3, width, nz), bf16),
            jax.ShapeDtypeStruct((16, nz), f32),
            jax.ShapeDtypeStruct((BAND, nz), bf16),
        ),
        2 * 4 * width * nz * nz,
        2 * nz * nz,
        [vmem((3 * width + 16, nz), bf16)],
        "smooth",
    )(lanes_z, received)
    smooth_one = lax.ppermute(smooth, ("py", "pz"), outward)
    smooth_two = lax.ppermute(smooth, ("py", "pz"), inward)
    squares = call(
        squares_kernel,
        jax.ShapeDtypeStruct((6, width, nz), bf16),
        2 * 6 * width * nz * nz,
        24 * width * nz,
        [vmem((6 * width, nz), bf16)],
        "squares",
    )(lanes_z, received)
    model = call(
        model_kernel,
        jax.ShapeDtypeStruct((6, width, nz), f32),
        100 * width * nz,
        24 * width * nz,
        (),
        "model",
    )(smooth, smooth_one, smooth_two, sense, edges)
    sums = call(
        sums_kernel,
        jax.ShapeDtypeStruct((parts, 1, LANES), f32),
        2 * 6 * width * nz * nz,
        48 * width * nz,
        [vmem((6 * width, nz), bf16)],
        "sums",
    )(band, received_strain, smooth, squares, model)
    totals = lax.all_to_all(sums, "pz", 0, 0, tiled=True)
    cells = nx * nz
    nu_t = call(
        lambda *refs: viscosity_kernel(cells, *refs),
        jax.ShapeDtypeStruct((depth, nx), f32),
        2 * depth * nx,
        8 * depth * nx,
        (),
        "viscosity",
    )(totals, magnitude)
    filtered_velocity = jnp.transpose(smooth, (0, 2, 1))
    return (nu_t[None], filtered_velocity[:, None])


def solution(mesh):
    in_specs = (P(None, "py", "pz", None),)
    out_specs = (P("py", "pz", None), P(None, "py", None, "pz"))
    return jax.shard_map(body, mesh=mesh, in_specs=in_specs, out_specs=out_specs, check_vma=False)
```

```python
import math

import jax
import jax.numpy as jnp
import numpy as np
from jax import lax
from jax.experimental import pallas as pl
from jax.experimental.pallas import tpu as pltpu
from jax.sharding import PartitionSpec as P

index_pairs = ((0, 0), (1, 1), (2, 2), (0, 1), (0, 2), (1, 2))
pair_weights = (1.0, 1.0, 1.0, 2.0, 2.0, 2.0)
epsilon = 1e-06
LANES = 128
BAND = 8


def filter_table(length):
    offsets = np.arange(length, dtype=np.int64)
    wavenumbers = np.arange(1, length // 4, dtype=np.int64)
    phase = offsets[:, None] * wavenumbers[None, :] % length
    kernel = (1.0 + 2.0 * np.cos(phase * (2.0 * math.pi / length)).sum(axis=1)) / length
    kernel = kernel.astype(np.float32)
    lagged = (offsets[:, None] - offsets[None, :]) % length
    return kernel[lagged].astype(jnp.bfloat16)


def call(kernel, out_shape, flops, moved, scratch=(), name=None, far=(), room=24):
    outs = jax.tree.leaves(out_shape)

    def space(i):
        return pl.BlockSpec(memory_space=pltpu.HBM if i in far else pltpu.VMEM)

    def run(*args):
        out_specs = [space(len(args) + i) for i in range(len(outs))]
        return pl.pallas_call(
            kernel,
            out_shape=out_shape,
            in_specs=[space(i) for i in range(len(args))],
            out_specs=out_specs if isinstance(out_shape, tuple) else out_specs[0],
            scratch_shapes=list(scratch),
            cost_estimate=pl.CostEstimate(flops=flops, bytes_accessed=moved, transcendentals=0),
            compiler_params=pltpu.CompilerParams(vmem_limit_bytes=room * 1024 * 1024),
            name=name,
        )(*args)

    return run


def nt(a, b):
    return lax.dot_general(a, b, (((1,), (1,)), ((), ())), preferred_element_type=jnp.float32)


def turned(rows, blocks):
    at = rows.shape[1] - blocks * LANES
    return rows if blocks == 0 else jnp.concatenate([rows[:, at:], rows[:, :at]], axis=1)


def table_rows(band_ref, first, last):
    band = band_ref[:LANES, :]
    return jnp.concatenate([turned(band, a) for a in range(first, last)], axis=0)


def table_of(band):
    band = band.astype(jnp.float32)
    rows = [band] + [pltpu.roll(band, at, 1) for at in range(BAND, LANES, BAND)]
    tile = jnp.concatenate(rows, axis=0).astype(jnp.bfloat16)
    return jnp.concatenate([turned(tile, a) for a in range(band.shape[1] // LANES)], axis=0)


def send_blocks(table_ref, fields_ref, block_ref, out_ref, sem, count, depth, edges):
    receivers = block_ref.shape[0]
    width = fields_ref.shape[1] // receivers
    per = LANES // depth
    full = count // per
    if edges:
        seed = table_ref[LANES:, :]
        beside = [turned(seed, q) for q in range(receivers * width // LANES)]
        beside = jnp.concatenate(beside, axis=0)
        got = nt(beside, fields_ref[: 2 * per * depth, :])
        row = lax.broadcasted_iota(jnp.int32, (receivers * 8, LANES), 0) % 8
        got = jnp.where(row < 2, got[:, :LANES], got[:, LANES:]).reshape(receivers, 8, LANES)
        block_ref[:, count * width // per :, :] = got.astype(jnp.bfloat16)
    chunks = sem.shape[0]
    some = receivers // chunks
    copies = []
    for c in range(chunks):
        mine = slice(c * some, (c + 1) * some)
        blocks = some * width // LANES
        table = table_rows(table_ref, c * blocks, (c + 1) * blocks)
        for first in range(0, full, 2):
            here = min(2, full - first)
            got = nt(table, fields_ref[first * LANES : (first + here) * LANES, :])
            got = got.astype(jnp.bfloat16)
            for j in range(here):
                block = got[:, j * LANES : (j + 1) * LANES].reshape(some, width, LANES)
                block_ref[mine, (first + j) * width : (first + j + 1) * width, :] = block
        if count % per:
            last = fields_ref[full * LANES : count * depth, :]
            got = nt(table, jnp.concatenate([last, last], axis=0))
            got = got.reshape(some, width, LANES)
            half = width // 2
            lane = lax.broadcasted_iota(jnp.int32, (some, half, LANES), 2)
            block = jnp.where(lane < depth, got[:, :half, :], got[:, half:, :])
            at = full * width
            block_ref[mine, at : at + half, :] = block.astype(jnp.bfloat16)
        copies.append(pltpu.make_async_copy(block_ref.at[mine], out_ref.at[mine], sem.at[c]))
        copies[-1].start()
    for copy in copies:
        copy.wait()


def sorted_lines(recv_ref, t, start, count):
    low = lax.broadcasted_iota(jnp.int32, (count, LANES), 1) < LANES // 2
    even = recv_ref[2 * t, start : start + count, :].astype(jnp.float32)
    odd = recv_ref[2 * t + 1, start : start + count, :].astype(jnp.float32)
    one = jnp.where(low, even, pltpu.roll(odd, LANES // 2, 1))
    two = jnp.where(low, pltpu.roll(even, LANES // 2, 1), odd)
    return one, two


def place(lines_ref, at, t, rows):
    lines_ref[at : at + rows.shape[0], t * LANES : (t + 1) * LANES] = rows.astype(jnp.bfloat16)


def products_kernel(table_ref, velocity_ref, out_ref, fields_ref, block_ref, sem):
    depth = velocity_ref.shape[1]
    parts = [velocity_ref[a] for a in range(3)]
    for a in range(3):
        fields_ref[a * depth : (a + 1) * depth, :] = parts[a].astype(jnp.bfloat16)
    for p, (a, b) in enumerate(index_pairs):
        at = (3 + p) * depth
        fields_ref[at : at + depth, :] = (parts[a] * parts[b]).astype(jnp.bfloat16)
    send_blocks(table_ref, fields_ref, block_ref, out_ref, sem, 9, depth, True)


def strain(gradients):
    strain_parts = [0.5 * (gradients[b][a] + gradients[a][b]) for a, b in index_pairs]
    squares_sum = pair_weights[0] * strain_parts[0] * strain_parts[0]
    for weight, part_value in zip(pair_weights[1:], strain_parts[1:]):
        squares_sum = squares_sum + weight * part_value * part_value
    return (strain_parts, jnp.sqrt(2.0 * squares_sum))


def slopes(center, one, two, sense, first, last):
    rows, length = center.shape
    row = lax.broadcasted_iota(jnp.int32, center.shape, 0)
    along = (pltpu.roll(center, length - 1, 1) - pltpu.roll(center, 1, 1)) * 0.5
    following = jnp.where(row == rows - 1, last, pltpu.roll(center, rows - 1, 0))
    previous = jnp.where(row == 0, first, pltpu.roll(center, 1, 0))
    return (along, (two - one) * sense, (following - previous) * 0.5)


def strain_kernel(
    table_ref, velocity_ref, one_ref, two_ref, sense_ref, first_ref, last_ref, out_ref, magnitude_ref,
    fields_ref, block_ref, sem,
):
    depth = velocity_ref.shape[1]
    gradients = [
        slopes(velocity_ref[a], one_ref[a], two_ref[a], sense_ref[...], first_ref[a], last_ref[a])
        for a in range(3)
    ]
    strain_parts, magnitude = strain(gradients)
    magnitude_ref[...] = magnitude
    for p, part_value in enumerate(strain_parts):
        fields_ref[p * depth : (p + 1) * depth, :] = (magnitude * part_value).astype(jnp.bfloat16)
    send_blocks(table_ref, fields_ref, block_ref, out_ref, sem, 6, depth, False)


def smooth_kernel(table_ref, recv_ref, smooth_ref, edges_ref, band_ref, lines_ref):
    senders = recv_ref.shape[0]
    _, width, length = smooth_ref.shape
    for t in range(senders // 2):
        one, two = sorted_lines(recv_ref, t, 0, width)
        place(lines_ref, 0, t, one)
        place(lines_ref, width, t, two)
        one, two = sorted_lines(recv_ref, t, width, width)
        place(lines_ref, 2 * width, t, one)
        one, two = sorted_lines(recv_ref, t, 9 * width // 2, 8)
        place(lines_ref, 3 * width, t, jnp.concatenate([one, two], axis=0))
    got = nt(lines_ref[...], table_rows(table_ref, 0, length // LANES)).astype(jnp.bfloat16)
    for a in range(3):
        smooth_ref[a] = got[a * width : (a + 1) * width, :]
    edges_ref[...] = got[3 * width :, :].astype(jnp.float32)
    band_ref[...] = table_ref[:BAND, :]


def squares_kernel(table_ref, recv_ref, squares_ref, lines_ref):
    senders = recv_ref.shape[0]
    _, width, length = squares_ref.shape
    half = width // 2
    for t in range(senders // 2):
        place(lines_ref, 0, t, sorted_lines(recv_ref, t, width, width)[1])
        for j in range(2):
            one, two = sorted_lines(recv_ref, t, (2 + j) * width, width)
            place(lines_ref, (1 + 2 * j) * width, t, one)
            place(lines_ref, (2 + 2 * j) * width, t, two)
        one, two = sorted_lines(recv_ref, t, 4 * width, half)
        place(lines_ref, 5 * width, t, one)
        place(lines_ref, 5 * width + half, t, two)
    got = nt(lines_ref[...], table_rows(table_ref, 0, length // LANES)).astype(jnp.bfloat16)
    for p in range(6):
        squares_ref[p] = got[p * width : (p + 1) * width, :]


def model_kernel(smooth_ref, one_ref, two_ref, sense_ref, edges_ref, model_ref):
    gradients = []
    for a, at in zip(range(3), (0, 8, 2)):
        center, one, two = (ref[a].astype(jnp.float32) for ref in (smooth_ref, one_ref, two_ref))
        first, last = edges_ref[at : at + 1, :], edges_ref[at + 1 : at + 2, :]
        along, across, between = slopes(center, one, two, sense_ref[...], first, last)
        gradients.append((between, across, along))
    strain_parts, magnitude = strain(gradients)
    for p, part_value in enumerate(strain_parts):
        model_ref[p] = 4.0 * magnitude * part_value


def sums_kernel(table_ref, recv_ref, smooth_ref, squares_ref, model_ref, out_ref, lines_ref):
    senders = recv_ref.shape[0]
    _, width, length = model_ref.shape
    for t in range(senders // 2):
        for j in range(3):
            one, two = sorted_lines(recv_ref, t, j * width, width)
            place(lines_ref, 2 * j * width, t, one)
            place(lines_ref, (2 * j + 1) * width, t, two)
    got = nt(lines_ref[...], table_of(table_ref[...])).astype(jnp.bfloat16)
    smooth = [smooth_ref[a].astype(jnp.float32) for a in range(3)]
    numerator = jnp.zeros((8, length), jnp.float32)
    denominator = jnp.zeros((8, length), jnp.float32)
    for p, (weight, (a, b)) in enumerate(zip(pair_weights, index_pairs)):
        leonard = squares_ref[p].astype(jnp.float32) - smooth[a] * smooth[b]
        model_term = got[p * width : (p + 1) * width, :].astype(jnp.float32) - model_ref[p]
        top = leonard * model_term
        bottom = model_term * model_term
        numerator = numerator + weight * top.reshape(width // 8, 8, length).sum(axis=0)
        denominator = denominator + weight * bottom.reshape(width // 8, 8, length).sum(axis=0)

    def lanes(x):
        total = x[:, :LANES]
        for at in range(LANES, length, LANES):
            total = total + x[:, at : at + LANES]
        total = total.sum(axis=0, keepdims=True)
        return total + pltpu.roll(total, LANES // 2, 1)

    low = lax.broadcasted_iota(jnp.int32, (1, LANES), 1) < LANES // 2
    pair = jnp.where(low, lanes(numerator), lanes(denominator))
    out_ref[...] = jnp.broadcast_to(pair, out_ref.shape)


def viscosity_kernel(cells, sums_ref, magnitude_ref, out_ref):
    total = sums_ref[...].sum(axis=0)
    low = lax.broadcasted_iota(jnp.int32, total.shape, 1) < LANES // 2
    numerator = jnp.sum(jnp.where(low, total, 0.0), axis=1, keepdims=True)
    denominator = jnp.sum(jnp.where(low, 0.0, total), axis=1, keepdims=True)
    coefficient = numerator / cells / (2.0 * (denominator / cells + epsilon))
    out_ref[...] = magnitude_ref[...] * coefficient


def body(velocity):
    _, _, depth, nx = velocity.shape
    parts = lax.axis_size("pz")
    rows = lax.axis_size("py")
    nz = depth * parts
    width = nx // parts
    f32, bf16 = jnp.float32, jnp.bfloat16
    table_x = filter_table(nx).T
    table_z = filter_table(nz)
    beside = np.zeros((2, 8, nx), bf16)
    for r in range(2):
        beside[r, :4] = table_x[[r * width - 1, (r + 1) * width] * 2]
    lanes_x = jnp.asarray(np.concatenate([table_x[:LANES], beside.reshape(16, nx)]))
    same = np.array_equal(table_x[:LANES], table_z[:LANES])
    lanes_z = lanes_x if same else jnp.asarray(table_z[:LANES])
    outward, inward = [], []
    for i in range(rows - 1):
        for j in range(parts):
            pair = (i * parts + j, (i + 1) * parts + j)
            (inward if j % 2 else outward).append(pair)
            (outward if j % 2 else inward).append(pair[::-1])
    sense = (0.5 - (lax.axis_index("pz") % 2).astype(f32)).reshape(1, 1)
    around = [(i, (i + 1) % parts) for i in range(parts)]
    back = [(b, a) for a, b in around]
    velocity = velocity.reshape(3, depth, nx)
    vmem, dma = pltpu.VMEM, pltpu.SemaphoreType.DMA

    first = lax.ppermute(velocity[:, -1:], "pz", around)
    last = lax.ppermute(velocity[:, :1], "pz", back)
    send_shape = (parts, 9 * width // 2 + 8, LANES)
    send = call(
        products_kernel,
        jax.ShapeDtypeStruct(send_shape, bf16),
        2 * 9 * depth * nx * nx,
        12 * depth * nx + 2 * nx * nx,
        [vmem((9 * depth, nx), bf16), vmem(send_shape, bf16), dma((4,))],
        "products",
        (2,),
        58,
    )(lanes_x, velocity)
    send, first, last = lax.optimization_barrier((send, first, last))
    received = lax.all_to_all(send, "pz", 0, 0, tiled=True)

    one = lax.ppermute(velocity, ("py", "pz"), outward)
    two = lax.ppermute(velocity, ("py", "pz"), inward)
    strain_shape = (parts, 3 * width, LANES)
    send_strain, magnitude = call(
        strain_kernel,
        (jax.ShapeDtypeStruct(strain_shape, bf16), jax.ShapeDtypeStruct((depth, nx), f32)),
        2 * 6 * depth * nx * nx,
        36 * depth * nx + 2 * nx * nx,
        [vmem((6 * depth, nx), bf16), vmem(strain_shape, bf16), dma((1,))],
        "strain",
        (7,),
    )(lanes_x, velocity, one, two, sense, first, last)
    received_strain = lax.all_to_all(send_strain, "pz", 0, 0, tiled=True)

    smooth, edges, band = call(
        smooth_kernel,
        (
            jax.ShapeDtypeStruct((3, width, nz), bf16),
            jax.ShapeDtypeStruct((16, nz), f32),
            jax.ShapeDtypeStruct((BAND, nz), bf16),
        ),
        2 * 4 * width * nz * nz,
        2 * nz * nz,
        [vmem((3 * width + 16, nz), bf16)],
        "smooth",
    )(lanes_z, received)
    smooth_one = lax.ppermute(smooth, ("py", "pz"), outward)
    smooth_two = lax.ppermute(smooth, ("py", "pz"), inward)
    squares = call(
        squares_kernel,
        jax.ShapeDtypeStruct((6, width, nz), bf16),
        2 * 6 * width * nz * nz,
        24 * width * nz,
        [vmem((6 * width, nz), bf16)],
        "squares",
    )(lanes_z, received)
    model = call(
        model_kernel,
        jax.ShapeDtypeStruct((6, width, nz), f32),
        100 * width * nz,
        24 * width * nz,
        (),
        "model",
    )(smooth, smooth_one, smooth_two, sense, edges)
    sums = call(
        sums_kernel,
        jax.ShapeDtypeStruct((parts, 1, LANES), f32),
        2 * 6 * width * nz * nz,
        48 * width * nz,
        [vmem((6 * width, nz), bf16)],
        "sums",
    )(band, received_strain, smooth, squares, model)
    totals = lax.all_to_all(sums, "pz", 0, 0, tiled=True)
    cells = nx * nz
    nu_t = call(
        lambda *refs: viscosity_kernel(cells, *refs),
        jax.ShapeDtypeStruct((depth, nx), f32),
        2 * depth * nx,
        8 * depth * nx,
        (),
        "viscosity",
    )(totals, magnitude)
    filtered_velocity = jnp.transpose(smooth, (0, 2, 1))
    return (nu_t[None], filtered_velocity[:, None])


def solution(mesh):
    in_specs = (P(None, "py", "pz", None),)
    out_specs = (P("py", "pz", None), P(None, "py", None, "pz"))
    return jax.shard_map(body, mesh=mesh, in_specs=in_specs, out_specs=out_specs, check_vma=False)
```
